512 devices in a mesh: tm: 128 (over y, x, z_hi, core), coord: 4 (over z_lo).
Axes of the slice: x: 4, y: 8, z: 8 (z_hi: 2, z_lo: 4; z = z_hi * 4 + z_lo), core: 2. Of those that a mesh axis runs over, the one named last changes fastest.
Arguments:
- state: float32 [256, 16384], P('tm', 'coord'), may hold values from -6 to 6
- multiplier: float32 [256, 2048], P('tm', 'coord'), may hold values from -6 to 6
- force: float32 [256, 16384], P('tm', 'coord'), may hold values from -6 to 6
- initial: float32 [16384], P('coord'), may hold values from -6 to 6
- mass: float32 [16384], P('coord'), may hold values from 0.25 to 4
- stiff_diag: float32 [16384], P('coord'), may hold values from 0.9 to 1.8
- stab: float32 [2048], P('coord'), may hold values from 2.5 to 10
- bank: float32 [16, 128, 128], replicated, may hold values from -0.20412415 to 0.20412415
- k_offsets: int32 [128, 3], P('coord'), may hold values from 0 to 4, as said below
- k_tiles: int32 [128, 3], P('coord'), may hold values from 0 to 15
- g_cols: int32 [16, 4], P('coord'), may hold values from 0 to 31, as said below
- g_tiles: int32 [16, 4], P('coord'), may hold values from 0 to 15
Outputs:
- new_state: float32 [256, 16384], P('tm', 'coord')
- new_multiplier: float32 [256, 2048], P('tm', 'coord')
The draws below stay inside these ranges and needn't reach their ends.
Inputs may be any that keep to these rules, and one draw needn't show every extreme that they name: `k_offsets`: each row holds 3 different values. `g_cols`: each row holds 4 different values.
All inputs are finite; a program needn't handle non-finite values.
Results may differ from the reference program's by a relative error of at most 0.0055.
Values sent between devices are 32-bit elements; how exact they have to be, the bound alone decides.
No kernel may reach another device: no remote copies, remote signals or barrier semaphores. Data moves between devices by JAX's collectives and lax.ppermute only.
A program may use at most 64 MiB of HBM per device.

```python
import math
import jax
import jax.numpy as jnp
from jax import lax

CO_DEV = 4096
CN_DEV = 512
BLK = 128
KNB = 3
GNB = 4
REACH = 2
NTILE = 16
SWEEPS = 8
TSTEPS = 256
NCO = 16384
NCN = 2048
NBG = 128
NCB = 16


def pick_distinct(key, row_count, options, choose, forced):
    scores = jax.random.randint(key, (row_count, options), 0, 1 << 20)
    scores = scores * options + jnp.arange(options, dtype=jnp.int32)[None, :]
    column_ids = jnp.arange(options, dtype=jnp.int32)[None, :]
    scores = jnp.where(column_ids == forced[:, None], -1, scores)
    order = jnp.argsort(scores, axis=1)
    return order[:, :choose].astype(jnp.int32)


def draw_k_offsets(key, part):
    row_count = NCO // BLK
    forced = jnp.arange(row_count, dtype=jnp.int32) % 2 * (2 * REACH)
    return pick_distinct(jax.random.fold_in(key, 11), row_count, 2 * REACH + 1, KNB, forced)


def draw_g_cols(key, part):
    row_count = NCN // BLK
    per_device = CN_DEV // BLK
    nblocks = CO_DEV // BLK
    row_ids = jnp.arange(row_count, dtype=jnp.int32)
    forced = jnp.where(row_ids % per_device == per_device - 1, nblocks - 1, jnp.where(row_ids % per_device == 0, 0, -5))
    return pick_distinct(jax.random.fold_in(key, 23), row_count, nblocks, GNB, forced)


def draw_bank(key, part):
    spread = 0.8 * (KNB * BLK) ** (-0.5)
    bank_key = jax.random.fold_in(key, 37)
    values = jnp.clip(jax.random.normal(bank_key, (NTILE, BLK, BLK), jnp.float32), -5.0, 5.0)
    return values * spread


def touch_ends(drawn, rng, smallest, top_value):
    index_at = [jax.random.randint(jax.random.fold_in(rng, axis), (), 0, length) for axis, length in enumerate(drawn.shape)]
    main_axis = drawn.shape.index(max(drawn.shape))
    next_to = index_at[:main_axis] + [(index_at[main_axis] + 1) % drawn.shape[main_axis]] + index_at[main_axis + 1:]
    return drawn.at[tuple(index_at)].set(smallest).at[tuple(next_to)].set(top_value)


def steps_of(stream_key, shape, pieces, low, top_value):
    factor_of = 1.0
    for dim, parts in pieces:
        draws = jax.random.uniform(jax.random.fold_in(jax.random.fold_in(stream_key, 6), dim), (parts,), jnp.float32, low / len(pieces), top_value / len(pieces))
        factor_of = factor_of * jnp.repeat(jnp.exp(draws), shape[dim] // parts).reshape((-1,) + (1,) * (len(shape) - 1 - dim))
    return factor_of


def bell_draw(rng, shape, deviation, most, pieces=(), kind=jnp.bfloat16):
    drawn = jax.random.normal(rng, shape, jnp.float32) * deviation
    if len(pieces) > 0:
        drawn = steps_of(rng, shape, pieces, -0.22, 0.18) * drawn
    return jnp.clip(drawn, min=-most, max=most).astype(kind)


def setup_inputs(seed: int = 0) -> dict:
    key_of = jax.random.split(jax.random.key(seed), 13)
    return {
        "state": bell_draw(key_of[0], (TSTEPS, NCO), 1.0, 6.0, ((0, 128), (1, 4)), jnp.float32),
        "multiplier": bell_draw(key_of[1], (TSTEPS, NCN), 1.0, 6.0, ((0, 128), (1, 4)), jnp.float32),
        "force": bell_draw(key_of[2], (TSTEPS, NCO), 1.0, 6.0, ((0, 128), (1, 4)), jnp.float32),
        "initial": bell_draw(key_of[3], (NCO,), 1.0, 6.0, ((0, 4),), jnp.float32),
        "mass": jnp.clip(jnp.exp(math.log(4.0) - 2.7725887 * jax.random.uniform(key_of[4], (NCO,), jnp.float32) ** steps_of(key_of[4], (NCO,), ((0, 4),), -0.2, 0.2)), 0.25, 4.0),
        "stiff_diag": jnp.clip(jnp.exp(math.log(1.8) - 0.6931472 * jax.random.uniform(key_of[5], (NCO,), jnp.float32) ** steps_of(key_of[5], (NCO,), ((0, 4),), -0.2, 0.2)), 0.9, 1.8),
        "stab": jnp.clip(jnp.exp(math.log(10.0) - 1.3862944 * jax.random.uniform(key_of[6], (NCN,), jnp.float32) ** steps_of(key_of[6], (NCN,), ((0, 4),), -0.2, 0.2)), 2.5, 10.0),
        "bank": draw_bank(jax.random.fold_in(key_of[12], 71), 0),
        "k_offsets": draw_k_offsets(jax.random.fold_in(key_of[12], 71), 0),
        "k_tiles": touch_ends(jax.random.randint(key_of[9], (NBG, KNB), 0, NTILE), jax.random.fold_in(key_of[9], 1), 0, NTILE - 1).astype(jnp.int32),
        "g_cols": draw_g_cols(jax.random.fold_in(key_of[12], 71), 0),
        "g_tiles": touch_ends(jax.random.randint(key_of[11], (NCB, GNB), 0, NTILE), jax.random.fold_in(key_of[11], 1), 0, NTILE - 1).astype(jnp.int32),
    }


ALPHA = 1e-3
HIGHEST = lax.Precision.HIGHEST


def slot_factors(slot_ids, all_steps):
    decay_root = math.exp(math.log(ALPHA) / all_steps)
    pair_ids = slot_ids // 2
    is_odd = (slot_ids % 2) == 1
    angles = (2.0 * math.pi / all_steps) * pair_ids.astype(jnp.float32)
    cosine = jnp.cos(angles)
    sine_val = jnp.sin(angles)
    is_zero = pair_ids == 0
    real_self = jnp.where(is_odd, 1.0 + decay_root, 1.0 - decay_root)
    real_other = jnp.where(is_odd, 1.0 - decay_root, 1.0 + decay_root)
    shared = 1.0 - decay_root * cosine
    diag_self = jnp.where(is_zero, real_self, shared)
    diag_other = jnp.where(is_zero, real_other, shared)
    cross_self = jnp.where(is_zero, 0.0, jnp.where(is_odd, decay_root * sine_val, -decay_root * sine_val))
    return diag_self, diag_other, cross_self, -cross_self


def fourier_table(slot_ids, time_ids, all_steps):
    frequency = jnp.where(slot_ids == 1, all_steps // 2, slot_ids // 2)
    phase_idx = (frequency[:, None] * time_ids[None, :]) % all_steps
    angles = (2.0 * math.pi / all_steps) * phase_idx.astype(jnp.float32)
    is_sine = ((slot_ids % 2) == 1) & (slot_ids > 1)
    return jnp.where(is_sine[:, None], -jnp.sin(angles), jnp.cos(angles))


def inverse_table(all_steps):
    all_ids = jnp.arange(all_steps, dtype=jnp.int32)
    matrix_table = fourier_table(all_ids, all_ids, all_steps)
    weights = jnp.where(all_ids < 2, 1.0, 2.0) / all_steps
    return (matrix_table * weights[:, None]).T


def swap_pairs(values):
    slot_count = values.shape[0]
    return values.reshape(slot_count // 2, 2, -1)[:, ::-1].reshape(slot_count, -1)


def inner_solve(rhs_coord, rhs_cons, slot_ids, all_steps, mass, stiff_diag, stab, coupled, constrain, transpose):
    diag_self, diag_other, cross_self, cross_other = slot_factors(slot_ids, all_steps)
    d_self = diag_self[:, None] * mass + stiff_diag
    d_other = diag_other[:, None] * mass + stiff_diag
    cross_mass = cross_self[:, None] * mass
    determinant = d_self * d_other - (cross_self * cross_other)[:, None] * (mass * mass)

    def precondition(residual):
        return (d_other * residual - cross_mass * swap_pairs(residual)) / determinant

    iterate = precondition(rhs_coord)
    lagrange = (constrain(iterate) - rhs_cons) / stab
    for sweep_idx in range(SWEEPS - 1):
        applied = diag_self[:, None] * mass * iterate + cross_mass * swap_pairs(iterate) + stiff_diag * iterate + coupled(iterate)
        residual = rhs_coord - applied - transpose(lagrange)
        iterate = iterate + precondition(residual)
        lagrange = (constrain(iterate) - rhs_cons) / stab
    return iterate, lagrange


def reference(state, multiplier, force, initial, mass, stiff_diag, stab, bank, k_offsets, k_tiles, g_cols, g_tiles):
    all_steps = state.shape[0]
    nblocks = state.shape[1] // BLK
    ncblocks = multiplier.shape[1] // BLK
    padded_rows = jnp.arange(nblocks, dtype=jnp.int32)[:, None] + k_offsets
    k_mats = bank[k_tiles]
    owner_block = (jnp.arange(ncblocks, dtype=jnp.int32) // (CN_DEV // BLK)) * (CO_DEV // BLK)
    g_global = g_cols + owner_block[:, None]
    g_mats = bank[g_tiles]

    def coupled(values):
        row_count = values.shape[0]
        padded = jnp.pad(values, ((0, 0), (REACH * BLK, REACH * BLK)))
        blocks = padded.reshape(row_count, nblocks + 2 * REACH, BLK)
        picked = blocks[:, padded_rows]
        return jnp.einsum('rbki,bkij->rbj', picked, k_mats, precision=HIGHEST).reshape(row_count, -1)

    def constrain(values):
        row_count = values.shape[0]
        blocks = values.reshape(row_count, nblocks, BLK)
        picked = blocks[:, g_global]
        return jnp.einsum('rcgi,cgij->rcj', picked, g_mats, precision=HIGHEST).reshape(row_count, -1)

    def transpose(lagrange):
        row_count = lagrange.shape[0]
        lblocks = lagrange.reshape(row_count, ncblocks, BLK)
        terms = jnp.einsum('rcj,cgij->rcgi', lblocks, g_mats, precision=HIGHEST)
        summed = jnp.zeros((row_count, nblocks, BLK), jnp.float32).at[:, g_global].add(terms)
        return summed.reshape(row_count, -1)

    previous = jnp.concatenate([initial[None, :], state[:-1]], axis=0)
    resid_coord = force - (mass * (state - previous) + stiff_diag * state + coupled(state) + transpose(multiplier))
    resid_cons = stab * multiplier - constrain(state)
    time_ids = jnp.arange(all_steps, dtype=jnp.int32)
    exponent = (math.log(ALPHA) / all_steps) * time_ids.astype(jnp.float32)
    weights_up = jnp.exp(exponent)[:, None]
    weights_down = jnp.exp(-exponent)[:, None]
    forward = fourier_table(time_ids, time_ids, all_steps)
    spec_coord = jnp.dot(forward, weights_up * resid_coord, precision=HIGHEST)
    spec_cons = jnp.dot(forward, weights_up * resid_cons, precision=HIGHEST)
    sol_coord, sol_cons = inner_solve(spec_coord, spec_cons, time_ids, all_steps, mass, stiff_diag, stab, coupled, constrain, transpose)
    backward = inverse_table(all_steps)
    new_state = state + weights_down * jnp.dot(backward, sol_coord, precision=HIGHEST)
    new_multiplier = multiplier + weights_down * jnp.dot(backward, sol_cons, precision=HIGHEST)
    return new_state, new_multiplier
```

```python
import math

import jax
import jax.numpy as jnp
import numpy as np
from jax import lax
from jax.experimental import pallas as pl
from jax.experimental.pallas import tpu as pltpu
from jax.sharding import Mesh, PartitionSpec as P

BLK = 128
REACH = 2
SWEEPS = 8
ALPHA = 0.001
HIGHEST = lax.Precision.HIGHEST
F32 = jnp.float32
BF16 = jnp.bfloat16


def tables(steps, low):
    ids = np.arange(steps)
    frequency = np.where(ids == 1, steps // 2, ids // 2)
    angles = 2.0 * np.pi / steps * ((frequency[:, None] * ids[None, :]) % steps)
    is_sine = (ids % 2 == 1) & (ids > 1)
    wave = np.where(is_sine[:, None], -np.sin(angles), np.cos(angles))
    scale = np.exp(math.log(ALPHA) * ids / steps)
    forward = wave * scale[None, :]
    weights = np.where(ids < 2, 1.0, 2.0) / steps
    inverse = (wave * weights[:, None]).T / scale[:, None]
    inverse = inverse.reshape(steps // (2 * low), low, 2, steps // 2, 2)
    inverse = inverse.transpose(1, 2, 0, 4, 3).reshape(low, steps // low, steps)
    beta = math.exp(math.log(ALPHA) / steps)
    pair = np.arange(steps // 2)
    theta = 2.0 * np.pi * pair / steps
    zero = pair == 0
    a_even = np.where(zero, 1.0 - beta, 1.0 - beta * np.cos(theta))
    a_odd = np.where(zero, 1.0 + beta, 1.0 - beta * np.cos(theta))
    b_even = np.where(zero, 0.0, -beta * np.sin(theta))
    factors = np.stack([a_even, a_odd, b_even, zero.astype(np.float64)], axis=1)
    return forward.astype(np.float32), inverse.astype(np.float32), factors.astype(np.float32)


def split3(value):
    high = value.astype(BF16)
    rest = value - high.astype(F32)
    mid = rest.astype(BF16)
    return high, mid, (rest - mid.astype(F32)).astype(BF16)


def bank_kernel(bank_ref, w1, w2, w3, v1, v2, v3):
    for tile in range(bank_ref.shape[0]):
        pair, side = tile // 2, slice(tile % 2 * BLK, tile % 2 * BLK + BLK)
        value = bank_ref[tile]
        for mat, (o1, o2, o3) in ((value, (w1, w2, w3)), (value.T, (v1, v2, v3))):
            high, mid, low = split3(mat)
            o1[pair, :BLK, side] = high
            o1[pair, BLK:, side] = high
            o2[pair, :BLK, side] = mid
            o2[pair, BLK:, side] = mid
            o3[pair, :BLK, side] = low
            o3[pair, BLK:, side] = high


def swapped(value):
    rows = value.shape[0]
    even = lax.broadcasted_iota(jnp.int32, value.shape, 0) % 2 == 0
    return jnp.where(even, pltpu.roll(value, rows - 1, 0), pltpu.roll(value, 1, 0))


def doubled(value, odd):
    rows = value.shape[0]
    even = lax.broadcasted_iota(jnp.int32, value.shape, 0) % 2 == 0
    if odd:
        return jnp.where(even, pltpu.roll(value, rows - 1, 0), value)
    return jnp.where(even, value, pltpu.roll(value, 1, 0))


def make_solve(nb, ncb, co, tiles, knb, gnb, lay):
    nrow = 2 * nb * co
    crow = 2 * ncb * co
    prow = tiles * nrow

    def kernel(
        fac_ref, own_ref, r_ref, w1, w2, w3, v1, v2, v3, out_ref,
        p_ref, q_ref, acc, xs, rhs, e_ref, c_ref, gy, sc, istab, idxv, idxs, sem,
    ):
        a_even, a_odd, b_even, is_zero = fac_ref[0], fac_ref[1], fac_ref[2], fac_ref[3]

        def part(name, rows):
            return r_ref[lay[name] * 2 * co : lay[name] * 2 * co + rows]

        idxv[...] = part("idx", 2 * co).astype(jnp.int32)
        copy = pltpu.make_async_copy(idxv, idxs, sem)
        copy.start()
        p_ref[prow : prow + 8] = jnp.zeros((8, BLK), F32)

        def products(value, mats, dst):
            rows = value.shape[0]
            high, mid, low = split3(value)
            two = jnp.concatenate([high, mid], axis=1)
            ends = jnp.concatenate([high, low], axis=1)
            m1, m2, m3 = mats
            for pair in range(tiles // 2):
                res = jnp.dot(two, m1[pair], preferred_element_type=F32)
                res += jnp.dot(two, m2[pair], preferred_element_type=F32)
                res += jnp.dot(ends, m3[pair], preferred_element_type=F32)
                for side in range(2):
                    start = (2 * pair + side) * rows
                    dst[start : start + rows] = res[:, side * BLK : side * BLK + BLK]

        def couple():
            for b in range(nb):
                for o in range(co):
                    row = (b * co + o) * 2
                    total = p_ref[pl.ds(idxs[2 * o, b * knb], 2), :]
                    for k in range(1, knb):
                        total = total + p_ref[pl.ds(idxs[2 * o, b * knb + k], 2), :]
                    acc[row : row + 2] = total

        def constrain():
            for c in range(ncb):
                for o in range(co):
                    row = (c * co + o) * 2
                    at = nb * knb + c * gnb
                    total = p_ref[pl.ds(idxs[2 * o, at], 2), :]
                    for j in range(1, gnb):
                        total = total + p_ref[pl.ds(idxs[2 * o, at + j], 2), :]
                    gy[row : row + 2] = total

        def scatter():
            for c in range(ncb):
                for o in range(co):
                    row = (c * co + o) * 2
                    for j in range(gnb):
                        at = idxs[2 * o, nb * knb + c * gnb + j]
                        tile = at // nrow
                        dst = pl.ds(at - tile * nrow, 2)
                        acc[dst, :] += q_ref[pl.ds(tile * crow + row, 2), :]

        even = lax.broadcasted_iota(jnp.int32, (nrow, BLK), 0) % 2 == 0
        state = part("state", nrow)
        mult = part("mult", crow)
        products(state, (w1, w2, w3), p_ref)
        products(mult, (v1, v2, v3), q_ref)
        cm = part("wrap", nrow)
        mass = doubled(cm, True)
        half = part("stiff", nrow // 2)
        stiff = jnp.concatenate([doubled(half, False), doubled(half, True)], axis=0)
        shalf = part("stab", crow // 2)
        stab = jnp.concatenate([doubled(shalf, False), doubled(shalf, True)], axis=0)
        wrap = jnp.where(even, cm, is_zero * pltpu.roll(cm, 1, 0))
        a_self = jnp.where(even, a_even, a_odd)
        a_other = jnp.where(even, a_odd, a_even)
        b_self = jnp.where(even, b_even, -b_even)
        d_self = a_self * mass + stiff
        d_other = a_other * mass + stiff
        cross = b_self * mass
        inv = 1.0 / (d_self * d_other + cross * cross)
        e_ref[...] = d_other * inv
        c_ref[...] = cross * inv
        istab[...] = 1.0 / stab
        copy.wait()
        couple()
        constrain()
        scatter()
        spec = part("force", nrow) + wrap - (d_self * state + cross * swapped(state)) - acc[...]
        rhs[...] = spec
        sc[...] = stab * mult - gy[...]
        xs[...] = e_ref[...] * spec - c_ref[...] * swapped(spec)

        def sweep(_, carry):
            products(xs[...], (w1, w2, w3), p_ref)
            constrain()
            products((gy[...] - sc[...]) * istab[...], (v1, v2, v3), q_ref)
            couple()
            scatter()
            res = rhs[...] - acc[...]
            xs[...] = e_ref[...] * res - c_ref[...] * swapped(res)
            return carry

        lax.fori_loop(0, SWEEPS - 1, sweep, 0)
        products(xs[...], (w1, w2, w3), p_ref)
        constrain()
        gy[...] = (gy[...] - sc[...]) * istab[...]
        own = own_ref[0]
        parts = out_ref.shape[0] // (4 * lay["chunks"])
        for b in range(nb + ncb):
            src, blk = (xs, b) if b < nb else (gy, b - nb)
            value = src[pl.ds((blk * co + own) * 2, 2), :]
            for z in range(parts):
                row = ((b // 2) * parts + z) * 4 + b % 2 * 2
                out_ref[row : row + 2] = value
        used = -(-(nb + ncb) // 2) * parts * 4
        out_ref[used:] = jnp.zeros((out_ref.shape[0] - used, BLK), F32)

    return kernel, [
        pltpu.VMEM((prow + 8, BLK), F32),
        pltpu.VMEM((tiles * crow, BLK), F32),
        pltpu.VMEM((nrow, BLK), F32),
        pltpu.VMEM((nrow, BLK), F32),
        pltpu.VMEM((nrow, BLK), F32),
        pltpu.VMEM((nrow, BLK), F32),
        pltpu.VMEM((nrow, BLK), F32),
        pltpu.VMEM((crow, BLK), F32),
        pltpu.VMEM((crow, BLK), F32),
        pltpu.VMEM((crow, BLK), F32),
        pltpu.VMEM((2 * co, BLK), jnp.int32),
        pltpu.SMEM((2 * co, BLK), jnp.int32),
        pltpu.SemaphoreType.DMA(()),
    ]


def inverse_kernel(table_ref, x_ref, out_ref):
    slots = table_ref.shape[1]
    rows = table_ref.shape[0]
    for h in range(2):
        value = jnp.concatenate(
            [x_ref[pl.ds(2 * h + s, slots // 2, stride=4), :] for s in range(2)], axis=0
        )
        res = jnp.dot(table_ref[...], value, precision=HIGHEST, preferred_element_type=F32)
        for l in range(2):
            half = rows // 2
            out_ref[pl.ds(2 * h + l, half, stride=4), :] = res[l * half : (l + 1) * half]


VM = pl.BlockSpec(memory_space=pltpu.VMEM)
SM = pl.BlockSpec(memory_space=pltpu.SMEM)


def layout(nb, ncb):
    state, force, mult = 0, nb, 2 * nb
    wrap = mult + ncb
    stiff = wrap + nb
    stab = stiff + nb // 2
    idx = stab + ncb // 2
    return {"state": state, "force": force, "mult": mult, "wrap": wrap, "stiff": stiff, "stab": stab, "idx": idx}


def solve_call(fac, own, recv, mats, nb, ncb, co, tiles, knb, gnb, lay, parts):
    kernel, scratch = make_solve(nb, ncb, co, tiles, knb, gnb, lay)
    return pl.pallas_call(
        kernel,
        out_shape=jax.ShapeDtypeStruct((lay["chunks"] * parts * 4, BLK), F32),
        in_specs=[SM, SM] + [VM] * 7,
        out_specs=VM,
        scratch_shapes=scratch,
        name="solve",
    )(fac, own, recv, *mats)


def bank_call(bank):
    shape = jax.ShapeDtypeStruct((bank.shape[0] // 2, 2 * BLK, 2 * BLK), BF16)
    return pl.pallas_call(
        bank_kernel, out_shape=[shape] * 6, in_specs=[VM], out_specs=[VM] * 6, name="bank"
    )(bank)


def inverse_call(table, value, high):
    return pl.pallas_call(
        inverse_kernel,
        out_shape=jax.ShapeDtypeStruct((high * 4, BLK), F32),
        in_specs=[VM, VM],
        out_specs=VM,
        name="inverse",
    )(table, value)


def index_row(k_offsets, k_tiles, g_cols, g_tiles, o, nb, co, tiles):
    block = o * nb + jnp.arange(nb, dtype=jnp.int32)[:, None] + k_offsets - REACH
    inside = (block >= 0) & (block < nb * co)
    stored = ((block % nb) * co + block // nb) * 2
    rows = nb * co * 2
    k_rows = jnp.where(inside, k_tiles * rows + stored, tiles * rows)
    g_rows = g_tiles * rows + (g_cols * co + o) * 2
    both = jnp.concatenate([k_rows.reshape(-1), g_rows.reshape(-1)])
    return jnp.pad(both, (0, 2 * BLK - both.shape[0])).astype(F32).reshape(1, 2, BLK)


def make_local(forward, inverse, factors, low):
    steps = forward.shape[0]
    group = ("high", "low")

    def blocks(value):
        return value.reshape(value.shape[0], -1, BLK).transpose(1, 0, 2)

    def local(
        state, multiplier, force, initial, mass, stiff_diag, stab,
        bank, k_offsets, k_tiles, g_cols, g_tiles,
    ):
        nb = state.shape[1] // BLK
        ncb = multiplier.shape[1] // BLK
        tiles = bank.shape[0]
        tm = lax.axis_size(group)
        co = lax.axis_size("coord")
        high = tm // low
        t = lax.axis_index(group)
        o = lax.axis_index("coord")
        lay = layout(nb, ncb)
        lay["chunks"] = high
        first = jnp.where(t == 0, mass * initial, 0.0)
        force = force + jnp.stack([first, jnp.zeros_like(first)])
        st = blocks(state)
        sent = jnp.concatenate([st, blocks(force), blocks(multiplier), st], axis=0)
        sent = jnp.pad(sent, ((0, tm - sent.shape[0]), (0, 0), (0, 0)))
        columns = lax.all_to_all(sent, group, split_axis=0, concat_axis=0, tiled=True)
        columns = columns.reshape(steps, BLK)

        mb = mass.reshape(nb, BLK)
        extra = jnp.concatenate(
            [
                jnp.stack([jnp.zeros_like(mb), mb], axis=1),
                stiff_diag.reshape(2, nb // 2, BLK).transpose(1, 0, 2),
                stab.reshape(2, ncb // 2, BLK).transpose(1, 0, 2),
                index_row(k_offsets, k_tiles, g_cols, g_tiles, o, nb, co, tiles),
            ],
            axis=0,
        )
        at = t - lay["wrap"]
        extra = lax.dynamic_index_in_dim(
            extra, jnp.clip(at, 0, extra.shape[0] - 1), 0, keepdims=False
        )
        last = columns[-1] * extra[1] * -ALPHA
        is_wrap = (at >= 0) & (at < nb)
        extra = extra + jnp.stack([jnp.where(is_wrap, last, 0.0), jnp.zeros_like(last)])
        spectrum = jnp.dot(forward, columns, precision=HIGHEST).reshape(tm, 2, BLK)
        spectrum = jnp.where(at < 0, spectrum, extra[None])
        spread = jnp.broadcast_to(spectrum[:, None], (tm, co, 2, BLK)).reshape(tm * co, 2, BLK)
        recv = lax.all_to_all(
            spread, group + ("coord",), split_axis=0, concat_axis=0, tiled=True
        ).reshape(tm * co * 2, BLK)

        mats = bank_call(bank)
        fac = lax.dynamic_index_in_dim(jnp.asarray(factors), t, 0, keepdims=False)
        solved = solve_call(
            fac, o.reshape(1).astype(jnp.int32), recv, mats,
            nb, ncb, co, tiles, k_tiles.shape[1], g_tiles.shape[1], lay, low,
        )
        slots = lax.all_to_all(
            solved.reshape(tm, 4, BLK), group, split_axis=0, concat_axis=0, tiled=True
        ).reshape(tm * 4, BLK)
        table = lax.dynamic_index_in_dim(
            jnp.asarray(inverse), lax.axis_index("low"), 0, keepdims=False
        )
        rows = inverse_call(table, slots, high).reshape(high, 4, BLK)
        rows = lax.all_to_all(rows, "high", split_axis=0, concat_axis=0, tiled=True)
        rows = rows.reshape(high * 2, 2, BLK)
        update = rows[: nb + ncb].transpose(1, 0, 2).reshape(2, (nb + ncb) * BLK)
        return state + update[:, : nb * BLK], multiplier + update[:, nb * BLK :]

    return local


def solution(mesh):
    tm, co = mesh.shape["tm"], mesh.shape["coord"]
    low = 4
    split = Mesh(mesh.devices.reshape(tm // low, low, co), ("high", "low", "coord"))
    forward, inverse, factors = tables(2 * tm, low)
    time = ("high", "low")
    return jax.shard_map(
        make_local(forward, inverse, factors, low),
        mesh=split,
        in_specs=(
            P(time, "coord"),
            P(time, "coord"),
            P(time, "coord"),
            P("coord"),
            P("coord"),
            P("coord"),
            P("coord"),
            P(),
            P("coord", None),
            P("coord", None),
            P("coord", None),
            P("coord", None),
        ),
        out_specs=(P(time, "coord"), P(time, "coord")),
        check_vma=False,
    )
```

```python
import math

import jax
import jax.numpy as jnp
import numpy as np
from jax import lax
from jax.experimental import pallas as pl
from jax.experimental.pallas import tpu as pltpu
from jax.sharding import Mesh, PartitionSpec as P

BLK = 128
REACH = 2
SWEEPS = 8
ALPHA = 0.001
HIGHEST = lax.Precision.HIGHEST
F32 = jnp.float32
BF16 = jnp.bfloat16


def tables(steps, low):
    ids = np.arange(steps)
    frequency = np.where(ids == 1, steps // 2, ids // 2)
    angles = 2.0 * np.pi / steps * ((frequency[:, None] * ids[None, :]) % steps)
    is_sine = (ids % 2 == 1) & (ids > 1)
    wave = np.where(is_sine[:, None], -np.sin(angles), np.cos(angles))
    scale = np.exp(math.log(ALPHA) * ids / steps)
    forward = wave * scale[None, :]
    weights = np.where(ids < 2, 1.0, 2.0) / steps
    inverse = (wave * weights[:, None]).T / scale[:, None]
    inverse = inverse.reshape(steps // (2 * low), low, 1, 2, steps // 2, 1, 2).swapaxes(0, 1)
    inverse = inverse * np.eye(2).reshape(1, 1, 2, 1, 1, 2, 1)
    inverse = inverse.reshape(2 * steps, 2 * steps)
    beta = math.exp(math.log(ALPHA) / steps)
    pair = np.arange(steps // 2)
    theta = 2.0 * np.pi * pair / steps
    zero = pair == 0
    a_even = np.where(zero, 1.0 - beta, 1.0 - beta * np.cos(theta))
    a_odd = np.where(zero, 1.0 + beta, 1.0 - beta * np.cos(theta))
    b_even = np.where(zero, 0.0, -beta * np.sin(theta))
    factors = np.stack([a_even, a_odd, b_even, zero.astype(np.float64)], axis=1)
    return forward.astype(np.float32), inverse.astype(np.float32), factors.astype(np.float32)


def split3(value):
    high = value.astype(BF16)
    rest = value - high.astype(F32)
    mid = rest.astype(BF16)
    return high, mid, (rest - mid.astype(F32)).astype(BF16)


def bank_kernel(bank_ref, w1, w2, w3, v1, v2, v3):
    for tile in range(bank_ref.shape[0]):
        pair, side = tile // 2, slice(tile % 2 * BLK, tile % 2 * BLK + BLK)
        value = bank_ref[tile]
        for mat, outs in ((value, (w1, w2, w3)), (value.T, (v1, v2, v3))):
            for out, piece in zip(outs, split3(mat)):
                out[pair, :, side] = piece


def swapped(value):
    rows = value.shape[0]
    even = lax.broadcasted_iota(jnp.int32, value.shape, 0) % 2 == 0
    return jnp.where(even, pltpu.roll(value, rows - 1, 0), pltpu.roll(value, 1, 0))


def doubled(value, odd):
    rows = value.shape[0]
    even = lax.broadcasted_iota(jnp.int32, value.shape, 0) % 2 == 0
    if odd:
        return jnp.where(even, pltpu.roll(value, rows - 1, 0), value)
    return jnp.where(even, value, pltpu.roll(value, 1, 0))


def make_solve(nb, ncb, co, tiles, knb, gnb, lay):
    nrow = 2 * nb * co
    crow = 2 * ncb * co
    prow = tiles * nrow

    def kernel(
        fac_ref, own_ref, r_ref, w1, w2, w3, v1, v2, v3, out_ref,
        p_ref, q_ref, acc, gts, xs, rhs, e_ref, c_ref, gy, sc, istab, idxv, idxs, sem,
    ):
        a_even, a_odd, b_even, is_zero = fac_ref[0], fac_ref[1], fac_ref[2], fac_ref[3]

        def part(name, rows):
            return r_ref[lay[name] * 2 * co : lay[name] * 2 * co + rows]

        raw = part("idx", 2 * co).astype(jnp.int32)
        lane = lax.broadcasted_iota(jnp.int32, raw.shape, 1)
        line = lax.broadcasted_iota(jnp.int32, raw.shape, 0)
        coord = line // 2
        column = jnp.where(line % 2 == 0, raw, pltpu.roll(raw, 1, 0))
        tile = jnp.where(line % 2 == 0, pltpu.roll(raw, 2 * co - 1, 0), raw)
        block = coord * nb + lane // knb + column - REACH
        inside = (block >= 0) & (block < nb * co)
        k_row = ((block % nb) * co + block // nb) * 2
        k_row = jnp.where(inside, tile * nrow + k_row, prow)
        g_row = (column * co + coord) * 2
        is_k = lane < nb * knb
        q_row = tile * crow + (((lane - nb * knb) // gnb) * co + coord) * 2
        idxv[: 2 * co] = jnp.where(is_k, k_row, tile * nrow + g_row)
        idxv[2 * co : 4 * co] = q_row
        idxv[4 * co :] = g_row
        copy = pltpu.make_async_copy(idxv, idxs, sem)
        copy.start()
        p_ref[prow : prow + 8] = jnp.zeros((8, BLK), F32)
        gts[...] = jnp.zeros(gts.shape, F32)

        def products(value, mats, dst):
            rows = value.shape[0]
            high, mid, low = split3(value)
            two = jnp.concatenate([high, mid], axis=1)
            ends = jnp.concatenate([high, low], axis=1)
            m1, m2, m3 = mats
            for pair in range(tiles // 2):
                b1, b2, b3 = m1[pair], m2[pair], m3[pair]
                res = jnp.dot(two, jnp.concatenate([b1, b1]), preferred_element_type=F32)
                res += jnp.dot(two, jnp.concatenate([b2, b2]), preferred_element_type=F32)
                res += jnp.dot(ends, jnp.concatenate([b3, b1]), preferred_element_type=F32)
                for side in range(2):
                    start = (2 * pair + side) * rows
                    dst[start : start + rows] = res[:, side * BLK : side * BLK + BLK]

        def couple():
            for b in range(nb):
                for o in range(co):
                    row = (b * co + o) * 2
                    total = p_ref[pl.ds(idxs[2 * o, b * knb], 2), :]
                    for k in range(1, knb):
                        total = total + p_ref[pl.ds(idxs[2 * o, b * knb + k], 2), :]
                    acc[row : row + 2] = total

        def constrain():
            for c in range(ncb):
                for o in range(co):
                    row = (c * co + o) * 2
                    at = nb * knb + c * gnb
                    total = p_ref[pl.ds(idxs[2 * o, at], 2), :]
                    for j in range(1, gnb):
                        total = total + p_ref[pl.ds(idxs[2 * o, at + j], 2), :]
                    gy[row : row + 2] = total

        def scatter():
            for c in range(ncb):
                for o in range(co):
                    for j in range(gnb):
                        src = idxs[2 * (co + o), nb * knb + c * gnb + j]
                        dst = idxs[2 * (2 * co + o), nb * knb + c * gnb + j]
                        gts[c, pl.ds(dst, 2), :] = q_ref[pl.ds(src, 2), :]

        def coupled():
            total = acc[...]
            for c in range(ncb):
                total = total + gts[c]
            return total

        even = lax.broadcasted_iota(jnp.int32, (nrow, BLK), 0) % 2 == 0
        state = part("state", nrow)
        mult = part("mult", crow)
        products(state, (w1, w2, w3), p_ref)
        products(mult, (v1, v2, v3), q_ref)
        cm = part("wrap", nrow)
        mass = doubled(cm, True)
        half = part("stiff", nrow // 2)
        stiff = jnp.concatenate([doubled(half, False), doubled(half, True)], axis=0)
        shalf = part("stab", crow // 2)
        stab = jnp.concatenate([doubled(shalf, False), doubled(shalf, True)], axis=0)
        wrap = jnp.where(even, cm, is_zero * pltpu.roll(cm, 1, 0))
        a_self = jnp.where(even, a_even, a_odd)
        a_other = jnp.where(even, a_odd, a_even)
        b_self = jnp.where(even, b_even, -b_even)
        d_self = a_self * mass + stiff
        d_other = a_other * mass + stiff
        cross = b_self * mass
        inv = 1.0 / (d_self * d_other + cross * cross)
        e_ref[...] = d_other * inv
        c_ref[...] = cross * inv
        istab[...] = 1.0 / stab
        copy.wait()
        couple()
        constrain()
        scatter()
        spec = part("force", nrow) + wrap - (d_self * state + cross * swapped(state)) - coupled()
        rhs[...] = spec
        sc[...] = stab * mult - gy[...]
        xs[...] = e_ref[...] * spec - c_ref[...] * swapped(spec)

        def sweep(_, carry):
            products(xs[...], (w1, w2, w3), p_ref)
            constrain()
            products((gy[...] - sc[...]) * istab[...], (v1, v2, v3), q_ref)
            couple()
            scatter()
            res = rhs[...] - coupled()
            xs[...] = e_ref[...] * res - c_ref[...] * swapped(res)
            return carry

        lax.fori_loop(0, SWEEPS - 1, sweep, 0)
        products(xs[...], (w1, w2, w3), p_ref)
        constrain()
        gy[...] = (gy[...] - sc[...]) * istab[...]
        own = own_ref[0]
        parts = out_ref.shape[0] // (4 * lay["chunks"])
        for b in range(nb + ncb):
            src, blk = (xs, b) if b < nb else (gy, b - nb)
            value = src[pl.ds((blk * co + own) * 2, 2), :]
            for z in range(parts):
                row = ((b // 2) * parts + z) * 4 + b % 2 * 2
                out_ref[row : row + 2] = value
        used = -(-(nb + ncb) // 2) * parts * 4
        out_ref[used:] = jnp.zeros((out_ref.shape[0] - used, BLK), F32)

    return kernel, [
        pltpu.VMEM((prow + 8, BLK), F32),
        pltpu.VMEM((tiles * crow, BLK), F32),
        pltpu.VMEM((nrow, BLK), F32),
        pltpu.VMEM((ncb, nrow, BLK), F32),
        pltpu.VMEM((nrow, BLK), F32),
        pltpu.VMEM((nrow, BLK), F32),
        pltpu.VMEM((nrow, BLK), F32),
        pltpu.VMEM((nrow, BLK), F32),
        pltpu.VMEM((crow, BLK), F32),
        pltpu.VMEM((crow, BLK), F32),
        pltpu.VMEM((crow, BLK), F32),
        pltpu.VMEM((6 * co, BLK), jnp.int32),
        pltpu.SMEM((6 * co, BLK), jnp.int32),
        pltpu.SemaphoreType.DMA(()),
    ]


VM = pl.BlockSpec(memory_space=pltpu.VMEM)
SM = pl.BlockSpec(memory_space=pltpu.SMEM)


def layout(nb, ncb):
    state, force, mult = 0, nb, 2 * nb
    wrap = mult + ncb
    stiff = wrap + nb
    stab = stiff + nb // 2
    idx = stab + ncb // 2
    return {"state": state, "force": force, "mult": mult, "wrap": wrap, "stiff": stiff, "stab": stab, "idx": idx}


def solve_call(fac, own, recv, mats, nb, ncb, co, tiles, knb, gnb, lay, parts):
    kernel, scratch = make_solve(nb, ncb, co, tiles, knb, gnb, lay)
    return pl.pallas_call(
        kernel,
        out_shape=jax.ShapeDtypeStruct((lay["chunks"] * parts * 4, BLK), F32),
        in_specs=[SM, SM] + [VM] * 7,
        out_specs=VM,
        scratch_shapes=scratch,
        name="solve",
    )(fac, own, recv, *mats)


def bank_call(bank):
    shape = jax.ShapeDtypeStruct((bank.shape[0] // 2, BLK, 2 * BLK), BF16)
    return pl.pallas_call(
        bank_kernel, out_shape=[shape] * 6, in_specs=[VM], out_specs=[VM] * 6, name="bank"
    )(bank)


def index_rows(k_offsets, k_tiles, g_cols, g_tiles):
    first = jnp.concatenate([k_offsets.reshape(-1), g_cols.reshape(-1)])
    second = jnp.concatenate([k_tiles.reshape(-1), g_tiles.reshape(-1)])
    both = jnp.pad(jnp.stack([first, second]), ((0, 0), (0, BLK - first.shape[0])))
    return both.astype(F32)[None]


def make_local(forward, inverse, factors, low):
    steps = forward.shape[0]
    group = ("high", "low")

    def blocks(value):
        return value.reshape(value.shape[0], -1, BLK).transpose(1, 0, 2)

    def local(
        state, multiplier, force, initial, mass, stiff_diag, stab,
        bank, k_offsets, k_tiles, g_cols, g_tiles,
    ):
        nb = state.shape[1] // BLK
        ncb = multiplier.shape[1] // BLK
        tiles = bank.shape[0]
        tm = lax.axis_size(group)
        co = lax.axis_size("coord")
        high = tm // low
        t = lax.axis_index(group)
        o = lax.axis_index("coord")
        lay = layout(nb, ncb)
        lay["chunks"] = high
        st = blocks(state)
        sent = jnp.concatenate([st, blocks(force), blocks(multiplier), st], axis=0)
        sent = jnp.pad(sent, ((0, tm - sent.shape[0]), (0, 0), (0, 0)))
        columns = lax.all_to_all(sent, group, split_axis=0, concat_axis=0, tiled=True)
        columns = columns.reshape(steps, BLK)

        mb = mass.reshape(nb, BLK)
        extra = jnp.concatenate(
            [
                jnp.stack([initial.reshape(nb, BLK), mb], axis=1),
                stiff_diag.reshape(2, nb // 2, BLK).transpose(1, 0, 2),
                stab.reshape(2, ncb // 2, BLK).transpose(1, 0, 2),
                index_rows(k_offsets, k_tiles, g_cols, g_tiles),
            ],
            axis=0,
        )
        at = t - lay["wrap"]
        extra = lax.dynamic_index_in_dim(
            extra, jnp.clip(at, 0, extra.shape[0] - 1), 0, keepdims=False
        )
        is_wrap = (at >= 0) & (at < nb)
        wrap = jnp.where(is_wrap, extra[1] * (extra[0] - ALPHA * columns[-1]), extra[0])
        extra = jnp.stack([wrap, extra[1]])
        spectrum = jnp.dot(forward, columns, precision=HIGHEST).reshape(tm, 2, BLK)
        spectrum = jnp.where(at < 0, spectrum, extra[None])
        spread = jnp.broadcast_to(spectrum[:, None], (tm, co, 2, BLK)).reshape(tm * co, 2, BLK)
        recv = lax.all_to_all(
            spread, group + ("coord",), split_axis=0, concat_axis=0, tiled=True
        ).reshape(tm * co * 2, BLK)

        mats = bank_call(bank)
        recv = pltpu.with_memory_space_constraint(recv, pltpu.VMEM)
        fac = lax.dynamic_index_in_dim(jnp.asarray(factors), t, 0, keepdims=False)
        solved = solve_call(
            fac, o.reshape(1).astype(jnp.int32), recv, mats,
            nb, ncb, co, tiles, k_tiles.shape[1], g_tiles.shape[1], lay, low,
        )
        slots = lax.all_to_all(
            solved.reshape(tm, 4, BLK), group, split_axis=0, concat_axis=0, tiled=True
        ).reshape(tm * 4, BLK)
        table = lax.dynamic_slice_in_dim(
            jnp.asarray(inverse), lax.axis_index("low") * (4 * high), 4 * high, axis=0
        )
        table = lax.optimization_barrier(table)
        rows = lax.optimization_barrier(jnp.dot(table, slots, precision=HIGHEST))
        rows = rows.reshape(high, 4, BLK)
        rows = lax.all_to_all(rows, "high", split_axis=0, concat_axis=0, tiled=True)
        rows = rows.reshape(high * 2, 2, BLK)
        update = rows[: nb + ncb].transpose(1, 0, 2).reshape(2, (nb + ncb) * BLK)
        return state + update[:, : nb * BLK], multiplier + update[:, nb * BLK :]

    return local


def solution(mesh):
    tm, co = mesh.shape["tm"], mesh.shape["coord"]
    low = 4
    split = Mesh(mesh.devices.reshape(tm // low, low, co), ("high", "low", "coord"))
    forward, inverse, factors = tables(2 * tm, low)
    time = ("high", "low")
    return jax.shard_map(
        make_local(forward, inverse, factors, low),
        mesh=split,
        in_specs=(
            P(time, "coord"),
            P(time, "coord"),
            P(time, "coord"),
            P("coord"),
            P("coord"),
            P("coord"),
            P("coord"),
            P(),
            P("coord", None),
            P("coord", None),
            P("coord", None),
            P("coord", None),
        ),
        out_specs=(P(time, "coord"), P(time, "coord")),
        check_vma=False,
    )
```

```python
import math

import jax
import jax.numpy as jnp
import numpy as np
from jax import lax
from jax.experimental import pallas as pl
from jax.experimental.pallas import tpu as pltpu
from jax.sharding import Mesh, PartitionSpec as P

BLK = 128
REACH = 2
SWEEPS = 8
ALPHA = 0.001
HIGHEST = lax.Precision.HIGHEST
F32 = jnp.float32
BF16 = jnp.bfloat16


def tables(steps, low):
    ids = np.arange(steps)
    frequency = np.where(ids == 1, steps // 2, ids // 2)
    angles = 2.0 * np.pi / steps * ((frequency[:, None] * ids[None, :]) % steps)
    is_sine = (ids % 2 == 1) & (ids > 1)
    wave = np.where(is_sine[:, None], -np.sin(angles), np.cos(angles))
    scale = np.exp(math.log(ALPHA) * ids / steps)
    forward = wave * scale[None, :]
    weights = np.where(ids < 2, 1.0, 2.0) / steps
    inverse = (wave * weights[:, None]).T / scale[:, None]
    inverse = inverse.reshape(steps // (2 * low), low, 2, steps).swapaxes(0, 1).reshape(steps, steps)
    beta = math.exp(math.log(ALPHA) / steps)
    pair = np.arange(steps // 2)
    theta = 2.0 * np.pi * pair / steps
    zero = pair == 0
    a_even = np.where(zero, 1.0 - beta, 1.0 - beta * np.cos(theta))
    a_odd = np.where(zero, 1.0 + beta, 1.0 - beta * np.cos(theta))
    b_even = np.where(zero, 0.0, -beta * np.sin(theta))
    factors = np.stack([a_even, a_odd, b_even, zero.astype(np.float64)], axis=1)
    return forward.astype(np.float32), inverse.astype(np.float32), factors.astype(np.float32)


def split3(value):
    high = value.astype(BF16)
    rest = value - high.astype(F32)
    mid = rest.astype(BF16)
    return high, mid, (rest - mid.astype(F32)).astype(BF16)


def bank_kernel(bank_ref, w1, w2, v1, v2):
    for tile in range(bank_ref.shape[0]):
        value = bank_ref[tile]
        for mat, outs in ((value, (w1, w2)), (value.T, (v1, v2))):
            for out, piece in zip(outs, split3(mat)):
                out[tile] = piece


def gather_kernel(state, force, mult, out, sems):
    copies = []
    start = 0
    while start < out.shape[0]:
        for src in (state, force, mult) if start == 0 else (state, force):
            count = min(src.shape[0], out.shape[0] - start)
            if count > 0:
                copies.append((src.at[pl.ds(0, count)], out.at[pl.ds(start, count)]))
                start += count
    copies = [pltpu.make_async_copy(a, b, sems.at[i]) for i, (a, b) in enumerate(copies)]
    for copy in copies:
        copy.start()
    for copy in copies:
        copy.wait()


def finish_kernel(cols_ref, tiles_ref, state, mult, stab, update, w1, w2, new_state, new_mult):
    ncb, gnb = cols_ref.shape
    new_state[...] = state[...] + update[...]
    owner = lax.broadcasted_iota(jnp.int32, mult.shape, 0) // 2
    total = jnp.zeros(mult.shape, F32)
    for j in range(gnb):
        value = jnp.concatenate(
            [new_state[pl.ds(cols_ref[c, j] * 2, 2), :] for c in range(ncb)], axis=0
        )
        high, mid, _ = split3(value)
        two = jnp.concatenate([high, mid], axis=1)
        for c in range(ncb):
            b1, b2 = w1[tiles_ref[c, j]], w2[tiles_ref[c, j]]
            res = jnp.dot(two, jnp.concatenate([b1, b1]), preferred_element_type=F32)
            res += jnp.dot(two, jnp.concatenate([b2, b2]), preferred_element_type=F32)
            total += jnp.where(owner == c, res, 0.0)
    new_mult[...] = mult[...] + (total - stab[...] * mult[...]) / stab[...]


def swapped(value):
    rows = value.shape[0]
    even = lax.broadcasted_iota(jnp.int32, value.shape, 0) % 2 == 0
    return jnp.where(even, pltpu.roll(value, rows - 1, 0), pltpu.roll(value, 1, 0))


def doubled(value, odd):
    rows = value.shape[0]
    even = lax.broadcasted_iota(jnp.int32, value.shape, 0) % 2 == 0
    if odd:
        return jnp.where(even, pltpu.roll(value, rows - 1, 0), value)
    return jnp.where(even, value, pltpu.roll(value, 1, 0))


def make_solve(nb, ncb, co, tiles, knb, gnb, lay):
    nrow = 2 * nb * co
    crow = 2 * ncb * co
    prow = tiles * nrow

    def kernel(
        fac_ref, own_ref, r_ref, w1, w2, v1, v2, out_ref,
        p_ref, q_ref, acc, gts, xs, rhs, e_ref, c_ref, gy, sc, istab, idxv, idxs, sem,
    ):
        a_even, a_odd, b_even, is_zero = fac_ref[0], fac_ref[1], fac_ref[2], fac_ref[3]

        def part(name, rows, start=0):
            start += lay[name] * 2 * co
            return r_ref[start : start + rows]

        raw = part("idx", 2 * co).astype(jnp.int32)
        lane = lax.broadcasted_iota(jnp.int32, raw.shape, 1)
        line = lax.broadcasted_iota(jnp.int32, raw.shape, 0)
        coord = line // 2
        column = jnp.where(line % 2 == 0, raw, pltpu.roll(raw, 1, 0))
        tile = jnp.where(line % 2 == 0, pltpu.roll(raw, 2 * co - 1, 0), raw)
        block = coord * nb + lane // knb + column - REACH
        inside = (block >= 0) & (block < nb * co)
        k_row = ((block % nb) * co + block // nb) * 2
        k_row = jnp.where(inside, tile * nrow + k_row, prow)
        g_row = (column * co + coord) * 2
        is_k = lane < nb * knb
        q_row = tile * crow + (((lane - nb * knb) // gnb) * co + coord) * 2
        idxv[: 2 * co] = jnp.where(is_k, k_row, tile * nrow + g_row)
        idxv[2 * co : 4 * co] = q_row
        idxv[4 * co :] = g_row
        copy = pltpu.make_async_copy(idxv, idxs, sem)
        copy.start()
        p_ref[prow : prow + 8] = jnp.zeros((8, BLK), F32)
        gts[...] = jnp.zeros(gts.shape, F32)

        def products(value, mats, dst, beside):
            rows = value.shape[0]
            high, mid, low = split3(value)
            two = jnp.concatenate([high, mid], axis=1)
            m1, m2 = mats
            for pair in range(tiles // 2):
                b1 = jnp.concatenate([m1[2 * pair], m1[2 * pair + 1]], axis=1)
                b2 = jnp.concatenate([m2[2 * pair], m2[2 * pair + 1]], axis=1)
                res = jnp.dot(two, jnp.concatenate([b1, b1]), preferred_element_type=F32)
                res += jnp.dot(two, jnp.concatenate([b2, b2]), preferred_element_type=F32)
                res += jnp.dot(low, b1, preferred_element_type=F32)
                for side in range(2):
                    start = (2 * pair + side) * rows
                    dst[start : start + rows] = res[:, side * BLK : side * BLK + BLK]
                beside(pair)

        def couple(i):
            count = nb // (tiles // 2)
            for b in range(i * count, (i + 1) * count):
                for o in range(co):
                    row = (b * co + o) * 2
                    total = p_ref[pl.ds(idxs[2 * o, b * knb], 2), :]
                    for k in range(1, knb):
                        total = total + p_ref[pl.ds(idxs[2 * o, b * knb + k], 2), :]
                    acc[row : row + 2] = total

        def constrain():
            for c in range(ncb):
                for o in range(co):
                    row = (c * co + o) * 2
                    at = nb * knb + c * gnb
                    total = p_ref[pl.ds(idxs[2 * o, at], 2), :]
                    for j in range(1, gnb):
                        total = total + p_ref[pl.ds(idxs[2 * o, at + j], 2), :]
                    gy[row : row + 2] = total

        def scatter():
            for c in range(ncb):
                for o in range(co):
                    for j in range(gnb):
                        src = idxs[2 * (co + o), nb * knb + c * gnb + j]
                        dst = idxs[2 * (2 * co + o), nb * knb + c * gnb + j]
                        gts[c, pl.ds(dst, 2), :] = q_ref[pl.ds(src, 2), :]

        def coupled():
            total = acc[...]
            for c in range(ncb):
                total = total + gts[c]
            return total

        chunk = nrow // (tiles // 2)
        even = lax.broadcasted_iota(jnp.int32, (chunk, BLK), 0) % 2 == 0

        def prepare(i):
            start = i * chunk
            rows = slice(start, start + chunk)
            state = part("state", chunk, start)
            cm = part("wrap", chunk, start)
            mass = doubled(cm, True)
            stiff = doubled(part("stiff", chunk, start % (nrow // 2)), start >= nrow // 2)
            wrap = jnp.where(even, cm, is_zero * pltpu.roll(cm, 1, 0))
            d_self = jnp.where(even, a_even, a_odd) * mass + stiff
            d_other = jnp.where(even, a_odd, a_even) * mass + stiff
            cross = jnp.where(even, b_even, -b_even) * mass
            inv = 1.0 / (d_self * d_other + cross * cross)
            e_ref[rows] = d_other * inv
            c_ref[rows] = cross * inv
            rhs[rows] = part("force", chunk, start) + wrap - (d_self * state + cross * swapped(state))

        def precondition(res):
            xs[...] = e_ref[...] * res - c_ref[...] * swapped(res)

        mult = part("mult", crow)
        shalf = part("stab", crow // 2)
        stab = jnp.concatenate([doubled(shalf, False), doubled(shalf, True)], axis=0)
        istab[...] = 1.0 / stab
        products(part("state", nrow), (w1, w2), p_ref, prepare)
        copy.wait()
        products(mult, (v1, v2), q_ref, couple)
        constrain()
        scatter()
        spec = rhs[...] - coupled()
        rhs[...] = spec
        sc[...] = stab * mult - gy[...]
        precondition(spec)

        def sweep(_, carry):
            products(xs[...], (w1, w2), p_ref, lambda i: None)
            constrain()
            products((gy[...] - sc[...]) * istab[...], (v1, v2), q_ref, couple)
            scatter()
            precondition(rhs[...] - coupled())
            return carry

        lax.fori_loop(0, SWEEPS - 1, sweep, 0)
        own = own_ref[0]
        parts = out_ref.shape[0] // (2 * nb)
        for b in range(nb):
            value = xs[pl.ds((b * co + own) * 2, 2), :]
            for z in range(parts):
                row = (b * parts + z) * 2
                out_ref[row : row + 2] = value

    return kernel, [
        pltpu.VMEM((prow + 8, BLK), F32),
        pltpu.VMEM((tiles * crow, BLK), F32),
        pltpu.VMEM((nrow, BLK), F32),
        pltpu.VMEM((ncb, nrow, BLK), F32),
        pltpu.VMEM((nrow, BLK), F32),
        pltpu.VMEM((nrow, BLK), F32),
        pltpu.VMEM((nrow, BLK), F32),
        pltpu.VMEM((nrow, BLK), F32),
        pltpu.VMEM((crow, BLK), F32),
        pltpu.VMEM((crow, BLK), F32),
        pltpu.VMEM((crow, BLK), F32),
        pltpu.VMEM((6 * co, BLK), jnp.int32),
        pltpu.SMEM((6 * co, BLK), jnp.int32),
        pltpu.SemaphoreType.DMA(()),
    ]


VM = pl.BlockSpec(memory_space=pltpu.VMEM)
SM = pl.BlockSpec(memory_space=pltpu.SMEM)


def layout(nb, ncb):
    state, force, mult = 0, nb, 2 * nb
    wrap = mult + ncb
    stiff = wrap + nb
    stab = stiff + nb // 2
    idx = stab + ncb // 2
    return {"state": state, "force": force, "mult": mult, "wrap": wrap, "stiff": stiff, "stab": stab, "idx": idx}


def solve_call(fac, own, recv, mats, nb, ncb, co, tiles, knb, gnb, lay, parts):
    kernel, scratch = make_solve(nb, ncb, co, tiles, knb, gnb, lay)
    return pl.pallas_call(
        kernel,
        out_shape=jax.ShapeDtypeStruct((2 * nb * parts, BLK), F32),
        in_specs=[SM, SM] + [VM] * 5,
        out_specs=VM,
        scratch_shapes=scratch,
        name="solve",
    )(fac, own, recv, *mats)


def bank_call(bank):
    shape = jax.ShapeDtypeStruct(bank.shape, BF16)
    return pl.pallas_call(
        bank_kernel, out_shape=[shape] * 4, in_specs=[VM], out_specs=[VM] * 4, name="bank"
    )(bank)


def gather_call(state, force, mult, count):
    return pl.pallas_call(
        gather_kernel,
        out_shape=jax.ShapeDtypeStruct((count, 2, BLK), F32),
        in_specs=[pl.BlockSpec(memory_space=pl.ANY)] * 3,
        out_specs=pl.BlockSpec(memory_space=pl.ANY),
        scratch_shapes=[pltpu.SemaphoreType.DMA((8,))],
        name="gather",
    )(state, force, mult)


def finish_call(cols, tiles, state, mult, stab, update, w1, w2):
    return pl.pallas_call(
        finish_kernel,
        out_shape=[
            jax.ShapeDtypeStruct(state.shape, F32),
            jax.ShapeDtypeStruct(mult.shape, F32),
        ],
        in_specs=[SM, SM] + [VM] * 6,
        out_specs=[VM, VM],
        name="finish",
    )(cols, tiles, state, mult, stab, update, w1, w2)


def index_rows(k_offsets, k_tiles, g_cols, g_tiles):
    first = jnp.concatenate([k_offsets.reshape(-1), g_cols.reshape(-1)])
    second = jnp.concatenate([k_tiles.reshape(-1), g_tiles.reshape(-1)])
    both = jnp.pad(jnp.stack([first, second]), ((0, 0), (0, BLK - first.shape[0])))
    return both.astype(F32)[None]


def make_local(forward, inverse, factors, low):
    steps = forward.shape[0]
    group = ("high", "low")

    def blocks(value):
        return value.reshape(value.shape[0], -1, BLK).transpose(1, 0, 2)

    def local(
        state, multiplier, force, initial, mass, stiff_diag, stab,
        bank, k_offsets, k_tiles, g_cols, g_tiles,
    ):
        nb = state.shape[1] // BLK
        ncb = multiplier.shape[1] // BLK
        tiles = bank.shape[0]
        tm = lax.axis_size(group)
        co = lax.axis_size("coord")
        high = tm // low
        t = lax.axis_index(group)
        o = lax.axis_index("coord")
        lay = layout(nb, ncb)
        sent = gather_call(blocks(state), blocks(force), blocks(multiplier), tm)
        columns = lax.all_to_all(sent, group, split_axis=0, concat_axis=0, tiled=True)
        columns = columns.reshape(steps, BLK)

        mb = mass.reshape(nb, BLK)
        extra = jnp.concatenate(
            [
                jnp.stack([initial.reshape(nb, BLK), mb], axis=1),
                stiff_diag.reshape(2, nb // 2, BLK).transpose(1, 0, 2),
                stab.reshape(2, ncb // 2, BLK).transpose(1, 0, 2),
                index_rows(k_offsets, k_tiles, g_cols, g_tiles),
            ],
            axis=0,
        )
        at = t - lay["wrap"]
        extra = lax.dynamic_index_in_dim(
            extra, jnp.clip(at, 0, extra.shape[0] - 1), 0, keepdims=False
        )
        is_wrap = (at >= 0) & (at < nb)
        wrap = jnp.where(is_wrap, extra[1] * (extra[0] - ALPHA * columns[-1]), extra[0])
        extra = jnp.stack([wrap, extra[1]])
        spectrum = jnp.dot(forward, columns, precision=HIGHEST).reshape(tm, 2, BLK)
        spectrum = jnp.where(at < 0, spectrum, extra[None])
        spread = jnp.broadcast_to(spectrum[:, None], (tm, co, 2, BLK)).reshape(tm * co, 2, BLK)
        recv = lax.all_to_all(
            spread, group + ("coord",), split_axis=0, concat_axis=0, tiled=True
        ).reshape(tm * co * 2, BLK)

        mats = bank_call(bank)
        recv = pltpu.with_memory_space_constraint(recv, pltpu.VMEM)
        fac = lax.dynamic_index_in_dim(jnp.asarray(factors), t, 0, keepdims=False)
        solved = solve_call(
            fac, o.reshape(1).astype(jnp.int32), recv, mats,
            nb, ncb, co, tiles, k_tiles.shape[1], g_tiles.shape[1], lay, low,
        )
        slots = lax.all_to_all(
            solved.reshape(tm, 2, BLK), group, split_axis=0, concat_axis=0, tiled=True
        ).reshape(steps, BLK)
        table = lax.dynamic_slice_in_dim(
            jnp.asarray(inverse), lax.axis_index("low") * (2 * high), 2 * high, axis=0
        )
        table = lax.optimization_barrier(table)
        rows = lax.optimization_barrier(jnp.dot(table, slots, precision=HIGHEST))
        rows = lax.all_to_all(
            rows.reshape(high, 2, BLK), "high", split_axis=0, concat_axis=0, tiled=True
        ).reshape(2 * nb, BLK)
        new_state, new_mult = finish_call(
            g_cols,
            g_tiles,
            blocks(state).reshape(2 * nb, BLK),
            blocks(multiplier).reshape(2 * ncb, BLK),
            jnp.repeat(stab.reshape(ncb, BLK), 2, axis=0),
            pltpu.with_memory_space_constraint(rows, pltpu.VMEM),
            *[pltpu.with_memory_space_constraint(m, pltpu.VMEM) for m in mats[:2]],
        )

        def lines(value):
            return value.reshape(-1, 2, BLK).transpose(1, 0, 2).reshape(2, -1)

        return lines(new_state), lines(new_mult)

    return local


def solution(mesh):
    tm, co = mesh.shape["tm"], mesh.shape["coord"]
    low = 4
    split = Mesh(mesh.devices.reshape(tm // low, low, co), ("high", "low", "coord"))
    forward, inverse, factors = tables(2 * tm, low)
    time = ("high", "low")
    return jax.shard_map(
        make_local(forward, inverse, factors, low),
        mesh=split,
        in_specs=(
            P(time, "coord"),
            P(time, "coord"),
            P(time, "coord"),
            P("coord"),
            P("coord"),
            P("coord"),
            P("coord"),
            P(),
            P("coord", None),
            P("coord", None),
            P("coord", None),
            P("coord", None),
        ),
        out_specs=(P(time, "coord"), P(time, "coord")),
        check_vma=False,
    )
```

```python
import functools
import math

import jax
import jax.numpy as jnp
import ml_dtypes
import numpy as np
from jax import lax
from jax.experimental import pallas as pl
from jax.experimental.pallas import tpu as pltpu
from jax.sharding import Mesh, PartitionSpec as P

BLK = 128
REACH = 2
SWEEPS = 8
ALPHA = 0.001
HIGHEST = lax.Precision.HIGHEST
F32 = jnp.float32
BF16 = jnp.bfloat16


def tables(steps, low):
    ids = np.arange(steps)
    frequency = np.where(ids == 1, steps // 2, ids // 2)
    angles = 2.0 * np.pi / steps * ((frequency[:, None] * ids[None, :]) % steps)
    is_sine = (ids % 2 == 1) & (ids > 1)
    wave = np.where(is_sine[:, None], -np.sin(angles), np.cos(angles))
    scale = np.exp(math.log(ALPHA) * ids / steps)
    forward = wave * scale[None, :]
    weights = np.where(ids < 2, 1.0, 2.0) / steps
    inverse = (wave * weights[:, None]).T / scale[:, None]
    inverse = inverse.reshape(steps // (2 * low), low, 2, steps).swapaxes(0, 1).reshape(steps, steps)
    beta = math.exp(math.log(ALPHA) / steps)
    pair = np.arange(steps // 2)
    theta = 2.0 * np.pi * pair / steps
    zero = pair == 0
    a_even = np.where(zero, 1.0 - beta, 1.0 - beta * np.cos(theta))
    a_odd = np.where(zero, 1.0 + beta, 1.0 - beta * np.cos(theta))
    b_even = np.where(zero, 0.0, -beta * np.sin(theta))
    factors = np.stack([a_even, a_odd, b_even, zero.astype(np.float64)], axis=1)
    return pieces_of(forward), inverse.astype(np.float32), factors.astype(np.float32)


def pieces_of(table):
    rest, pieces = table.astype(np.float32), []
    for _ in range(3):
        pieces.append(rest.astype(ml_dtypes.bfloat16))
        rest = rest - pieces[-1].astype(np.float32)
    return pieces


def split3(value):
    high = value.astype(BF16)
    rest = value - high.astype(F32)
    mid = rest.astype(BF16)
    return high, mid, (rest - mid.astype(F32)).astype(BF16)


def bank_kernel(bank_ref, w1, w2, v1, v2):
    for tile in range(bank_ref.shape[0]):
        value = bank_ref[tile]
        for mat, outs in ((value, (w1, w2)), (value.T, (v1, v2))):
            for out, piece in zip(outs, split3(mat)):
                out[tile] = piece


def gather_kernel(state, force, mult, out, sbuf, fbuf, mbuf, sin, sout):
    ns, nm = sbuf.shape[0], mbuf.shape[0]
    pairs = [(state, sbuf), (force, fbuf), (mult, mbuf)]
    loads = [pltpu.make_async_copy(a, b, sin.at[i]) for i, (a, b) in enumerate(pairs)]
    for load in loads:
        load.start()
    targets = [(sbuf, 0, ns), (fbuf, ns, ns), (mbuf, 2 * ns, nm), (sbuf, 2 * ns + nm, ns)]
    end = 3 * ns + nm
    while end < out.shape[0]:
        count = min(ns, out.shape[0] - end)
        targets.append((fbuf, end, count))
        end += count
    stores = []
    for load, (_, buf) in zip(loads, pairs):
        load.wait()
        for src, start, count in targets:
            if src is buf:
                stores.append(
                    pltpu.make_async_copy(
                        buf.at[pl.ds(0, count)], out.at[pl.ds(start, count)], sout.at[len(stores)]
                    )
                )
                stores[-1].start()
    for store in stores:
        store.wait()


def extra_kernel(at_ref, initial, mass, stiff, stab, offs, ktiles, cols, gtiles, out, buf):
    nb, ncb = mass.shape[0], stab.shape[0]
    buf[...] = jnp.zeros(buf.shape, F32)
    start = 0
    for first, second in (
        (initial[...], mass[...]),
        (stiff[: nb // 2], stiff[nb // 2 :]),
        (stab[: ncb // 2], stab[ncb // 2 :]),
        (offs[...].astype(F32), ktiles[...].astype(F32)),
        (cols[...].astype(F32), gtiles[...].astype(F32)),
    ):
        count, width = first.shape
        buf[pl.ds(start, count, stride=2), :width] = first
        buf[pl.ds(start + 1, count, stride=2), :width] = second
        start += 2 * count
    out[...] = buf[pl.ds(at_ref[0], 2), :]


def spread_kernel(at_ref, x_ref, extra, t1, t2, t3, out, *, wraps):
    rows = x_ref.shape[0]
    co = out.shape[0] // rows
    at = at_ref[0]

    @pl.when(at < 0)
    def _():
        high, mid, low = split3(x_ref[...])
        two = jnp.concatenate([high, mid], axis=1)
        res = jnp.dot(t2[...], two, preferred_element_type=F32)
        low_part = jnp.dot(t3[...], high, preferred_element_type=F32)
        low_part += jnp.dot(t1[...], low, preferred_element_type=F32)
        res += jnp.dot(t1[...], two, preferred_element_type=F32)
        res = res[:, :BLK] + (res[:, BLK:] + low_part)
        for p in range(rows // 2):
            for o in range(co):
                row = (p * co + o) * 2
                out[row : row + 2] = res[2 * p : 2 * p + 2]

    @pl.when(at >= 0)
    def _():
        first, second = extra[0:1], extra[1:2]
        wrap = second * (first - ALPHA * x_ref[rows - 1 : rows])
        first = jnp.where(at < wraps, wrap, first)
        even = lax.broadcasted_iota(jnp.int32, (8, BLK), 0) % 2 == 0
        value = jnp.where(even, first, second)
        for row in range(0, out.shape[0], 8):
            out[row : row + 8] = value


def finish_kernel(cols_ref, tiles_ref, state, mult, stab, update, w1, w2, new_state, new_mult):
    ncb, gnb = cols_ref.shape
    new_state[...] = state[...] + update[...]
    owner = lax.broadcasted_iota(jnp.int32, mult.shape, 0) // 2
    total = jnp.zeros(mult.shape, F32)
    for j in range(gnb):
        value = jnp.concatenate(
            [new_state[pl.ds(cols_ref[c, j] * 2, 2), :] for c in range(ncb)], axis=0
        )
        high, mid, _ = split3(value)
        two = jnp.concatenate([high, mid], axis=1)
        for c in range(ncb):
            b1, b2 = w1[tiles_ref[c, j]], w2[tiles_ref[c, j]]
            res = jnp.dot(two, jnp.concatenate([b1, b1]), preferred_element_type=F32)
            res += jnp.dot(two, jnp.concatenate([b2, b2]), preferred_element_type=F32)
            total += jnp.where(owner == c, res, 0.0)
    weight = jnp.zeros(mult.shape, F32)
    for c in range(ncb):
        weight = jnp.where(owner == c, stab[c : c + 1], weight)
    new_mult[...] = mult[...] + (total - weight * mult[...]) / weight


def swapped(value):
    rows = value.shape[0]
    even = lax.broadcasted_iota(jnp.int32, value.shape, 0) % 2 == 0
    return jnp.where(even, pltpu.roll(value, rows - 1, 0), pltpu.roll(value, 1, 0))


def doubled(value, odd):
    rows = value.shape[0]
    even = lax.broadcasted_iota(jnp.int32, value.shape, 0) % 2 == 0
    if odd:
        return jnp.where(even, pltpu.roll(value, rows - 1, 0), value)
    return jnp.where(even, value, pltpu.roll(value, 1, 0))


def make_solve(nb, ncb, co, tiles, knb, gnb, lay):
    nrow = 2 * nb * co
    crow = 2 * ncb * co
    prow = tiles * nrow
    nidx = 2 * co * (knb + ncb)

    def kernel(
        fac_ref, own_ref, r_ref, w1, w2, v1, v2, out_ref,
        p_ref, q_ref, acc, gts, xs, rhs, e_ref, c_ref, gy, sc, istab, idxv, idxs, sem,
    ):
        a_even, a_odd, b_even, is_zero = fac_ref[0], fac_ref[1], fac_ref[2], fac_ref[3]

        def part(name, rows, start=0):
            start += lay[name] * 2 * co
            return r_ref[start : start + rows]

        raw = part("idx", nidx).astype(jnp.int32)
        lane = lax.broadcasted_iota(jnp.int32, raw.shape, 1)
        line = lax.broadcasted_iota(jnp.int32, raw.shape, 0)
        coord = line // 2 % co
        column, tile = raw, pltpu.roll(raw, nidx - 1, 0)
        block = coord * nb + lane + column - REACH
        inside = (block >= 0) & (block < nb * co)
        k_row = ((block % nb) * co + block // nb) * 2
        k_row = jnp.where(inside, tile * nrow + k_row, prow)
        g_row = (column * co + coord) * 2
        q_row = tile * crow + line - 2 * knb * co
        idxv[:nidx] = jnp.where(line < 2 * knb * co, k_row, tile * nrow + g_row)
        idxv[nidx : 2 * nidx] = q_row
        idxv[2 * nidx :] = g_row
        copy = pltpu.make_async_copy(idxv, idxs, sem)
        copy.start()
        p_ref[prow : prow + 8] = jnp.zeros((8, BLK), F32)
        gts[...] = jnp.zeros(gts.shape, F32)

        def products(value, mats, dst, beside):
            rows = value.shape[0]
            high, mid, low = split3(value)
            two = jnp.concatenate([high, mid], axis=1)
            m1, m2 = mats
            for pair in range(tiles // 2):
                b1 = jnp.concatenate([m1[2 * pair], m1[2 * pair + 1]], axis=1)
                b2 = jnp.concatenate([m2[2 * pair], m2[2 * pair + 1]], axis=1)
                res = jnp.dot(two, jnp.concatenate([b1, b1]), preferred_element_type=F32)
                res += jnp.dot(two, jnp.concatenate([b2, b2]), preferred_element_type=F32)
                res += jnp.dot(low, b1, preferred_element_type=F32)
                for side in range(2):
                    start = (2 * pair + side) * rows
                    dst[start : start + rows] = res[:, side * BLK : side * BLK + BLK]
                beside(pair)

        def couple(i):
            count = nb // (tiles // 2)
            for b in range(i * count, (i + 1) * count):
                for o in range(co):
                    row = (b * co + o) * 2
                    total = p_ref[pl.ds(idxs[2 * o, b], 2), :]
                    for k in range(1, knb):
                        total = total + p_ref[pl.ds(idxs[2 * (k * co + o), b], 2), :]
                    acc[row : row + 2] = total

        def constrain():
            for c in range(ncb):
                for o in range(co):
                    row = (c * co + o) * 2
                    at = 2 * ((knb + c) * co + o)
                    total = p_ref[pl.ds(idxs[at, 0], 2), :]
                    for j in range(1, gnb):
                        total = total + p_ref[pl.ds(idxs[at, j], 2), :]
                    gy[row : row + 2] = total

        def scatter():
            for c in range(ncb):
                for o in range(co):
                    at = 2 * ((knb + c) * co + o)
                    for j in range(gnb):
                        src, dst = idxs[nidx + at, j], idxs[2 * nidx + at, j]
                        gts[c, pl.ds(dst, 2), :] = q_ref[pl.ds(src, 2), :]

        def coupled():
            total = acc[...]
            for c in range(ncb):
                total = total + gts[c]
            return total

        chunk = nrow // (tiles // 2)
        even = lax.broadcasted_iota(jnp.int32, (chunk, BLK), 0) % 2 == 0

        def prepare(i):
            start = i * chunk
            rows = slice(start, start + chunk)
            state = part("state", chunk, start)
            cm = part("wrap", chunk, start)
            mass = doubled(cm, True)
            stiff = doubled(part("stiff", chunk, start % (nrow // 2)), start >= nrow // 2)
            wrap = jnp.where(even, cm, is_zero * pltpu.roll(cm, 1, 0))
            d_self = jnp.where(even, a_even, a_odd) * mass + stiff
            d_other = jnp.where(even, a_odd, a_even) * mass + stiff
            cross = jnp.where(even, b_even, -b_even) * mass
            inv = 1.0 / (d_self * d_other + cross * cross)
            e_ref[rows] = d_other * inv
            c_ref[rows] = cross * inv
            rhs[rows] = part("force", chunk, start) + wrap - (d_self * state + cross * swapped(state))

        def precondition(res):
            xs[...] = e_ref[...] * res - c_ref[...] * swapped(res)

        mult = part("mult", crow)
        shalf = part("stab", crow // 2)
        stab = jnp.concatenate([doubled(shalf, False), doubled(shalf, True)], axis=0)
        istab[...] = 1.0 / stab
        products(part("state", nrow), (w1, w2), p_ref, prepare)
        copy.wait()
        products(mult, (v1, v2), q_ref, couple)
        constrain()
        scatter()
        spec = rhs[...] - coupled()
        rhs[...] = spec
        sc[...] = stab * mult - gy[...]
        precondition(spec)

        def sweep(_, carry):
            products(xs[...], (w1, w2), p_ref, lambda i: None)
            constrain()
            products((gy[...] - sc[...]) * istab[...], (v1, v2), q_ref, couple)
            scatter()
            precondition(rhs[...] - coupled())
            return carry

        lax.fori_loop(0, SWEEPS - 1, sweep, 0)
        own = own_ref[0]
        parts = out_ref.shape[0] // (2 * nb)
        for b in range(nb):
            value = xs[pl.ds((b * co + own) * 2, 2), :]
            for z in range(parts):
                row = (b * parts + z) * 2
                out_ref[row : row + 2] = value

    return kernel, [
        pltpu.VMEM((prow + 8, BLK), F32),
        pltpu.VMEM((tiles * crow, BLK), F32),
        pltpu.VMEM((nrow, BLK), F32),
        pltpu.VMEM((ncb, nrow, BLK), F32),
        pltpu.VMEM((nrow, BLK), F32),
        pltpu.VMEM((nrow, BLK), F32),
        pltpu.VMEM((nrow, BLK), F32),
        pltpu.VMEM((nrow, BLK), F32),
        pltpu.VMEM((crow, BLK), F32),
        pltpu.VMEM((crow, BLK), F32),
        pltpu.VMEM((crow, BLK), F32),
        pltpu.VMEM((3 * nidx, BLK), jnp.int32),
        pltpu.SMEM((3 * nidx, BLK), jnp.int32),
        pltpu.SemaphoreType.DMA(()),
    ]


VM = pl.BlockSpec(memory_space=pltpu.VMEM)
SM = pl.BlockSpec(memory_space=pltpu.SMEM)


def layout(nb, ncb):
    state, force, mult = 0, nb, 2 * nb
    wrap = mult + ncb
    stiff = wrap + nb
    stab = stiff + nb // 2
    idx = stab + ncb // 2
    return {"state": state, "force": force, "mult": mult, "wrap": wrap, "stiff": stiff, "stab": stab, "idx": idx}


def solve_call(fac, own, recv, mats, nb, ncb, co, tiles, knb, gnb, lay, parts):
    kernel, scratch = make_solve(nb, ncb, co, tiles, knb, gnb, lay)
    return pl.pallas_call(
        kernel,
        out_shape=jax.ShapeDtypeStruct((2 * nb * parts, BLK), F32),
        in_specs=[SM, SM] + [VM] * 5,
        out_specs=VM,
        scratch_shapes=scratch,
        name="solve",
    )(fac, own, recv, *mats)


def bank_call(bank):
    shape = jax.ShapeDtypeStruct(bank.shape, BF16)
    return pl.pallas_call(
        bank_kernel, out_shape=[shape] * 4, in_specs=[VM], out_specs=[VM] * 4, name="bank"
    )(bank)


def gather_call(state, force, mult, count):
    hbm = pl.BlockSpec(memory_space=pl.ANY)
    return pl.pallas_call(
        gather_kernel,
        out_shape=jax.ShapeDtypeStruct((count, 2, BLK), F32),
        in_specs=[hbm] * 3,
        out_specs=hbm,
        scratch_shapes=[pltpu.VMEM(v.shape, F32) for v in (state, force, mult)]
        + [pltpu.SemaphoreType.DMA((3,)), pltpu.SemaphoreType.DMA((8,))],
        name="gather",
    )(state, force, mult)


def extra_call(at, initial, mass, stiff, stab, offs, ktiles, cols, gtiles, rows):
    return pl.pallas_call(
        extra_kernel,
        out_shape=jax.ShapeDtypeStruct((2, BLK), F32),
        in_specs=[SM] + [VM] * 8,
        out_specs=VM,
        scratch_shapes=[pltpu.VMEM((rows, BLK), F32)],
        name="extra",
    )(at, initial, mass, stiff, stab, offs, ktiles, cols, gtiles)


def spread_call(at, columns, extra, pieces, co, wraps):
    return pl.pallas_call(
        functools.partial(spread_kernel, wraps=wraps),
        out_shape=jax.ShapeDtypeStruct((columns.shape[0] * co, BLK), F32),
        in_specs=[SM] + [VM] * 5,
        out_specs=VM,
        name="spread",
    )(at, columns, extra, *pieces)


def finish_call(cols, tiles, state, mult, stab, update, w1, w2):
    return pl.pallas_call(
        finish_kernel,
        out_shape=[
            jax.ShapeDtypeStruct(state.shape, F32),
            jax.ShapeDtypeStruct(mult.shape, F32),
        ],
        in_specs=[SM, SM] + [VM] * 6,
        out_specs=[VM, VM],
        name="finish",
    )(cols, tiles, state, mult, stab, update, w1, w2)


def make_local(forward, inverse, factors, low):
    steps = forward[0].shape[0]
    group = ("high", "low")

    def blocks(value):
        return value.reshape(value.shape[0], -1, BLK).transpose(1, 0, 2)

    def local(
        state, multiplier, force, initial, mass, stiff_diag, stab,
        bank, k_offsets, k_tiles, g_cols, g_tiles,
    ):
        nb = state.shape[1] // BLK
        ncb = multiplier.shape[1] // BLK
        tiles = bank.shape[0]
        tm = lax.axis_size(group)
        co = lax.axis_size("coord")
        high = tm // low
        t = lax.axis_index(group)
        o = lax.axis_index("coord")
        lay = layout(nb, ncb)
        sent = gather_call(blocks(state), blocks(force), blocks(multiplier), tm)
        columns = lax.all_to_all(sent, group, split_axis=0, concat_axis=0, tiled=True)
        columns = pltpu.with_memory_space_constraint(columns.reshape(steps, BLK), pltpu.VMEM)
        at = t - lay["wrap"]
        count = 2 * (tm - lay["wrap"])
        extra = extra_call(
            jnp.clip(2 * at, 0, count - 2).reshape(1),
            initial.reshape(nb, BLK),
            mass.reshape(nb, BLK),
            stiff_diag.reshape(nb, BLK),
            stab.reshape(ncb, BLK),
            k_offsets.T,
            k_tiles.T,
            g_cols,
            g_tiles,
            -(-count // 8) * 8,
        )
        pieces = [pltpu.with_memory_space_constraint(jnp.asarray(p), pltpu.VMEM) for p in forward]
        spread = spread_call(at.reshape(1), columns, extra, pieces, co, nb)
        spread = spread.reshape(tm * co, 2, BLK)
        recv = lax.all_to_all(
            spread, group + ("coord",), split_axis=0, concat_axis=0, tiled=True
        ).reshape(tm * co * 2, BLK)

        mats = bank_call(bank)
        recv = pltpu.with_memory_space_constraint(recv, pltpu.VMEM)
        fac = lax.dynamic_index_in_dim(jnp.asarray(factors), t, 0, keepdims=False)
        solved = solve_call(
            fac, o.reshape(1).astype(jnp.int32), recv, mats,
            nb, ncb, co, tiles, k_tiles.shape[1], g_tiles.shape[1], lay, low,
        )
        slots = lax.all_to_all(
            solved.reshape(tm, 2, BLK), group, split_axis=0, concat_axis=0, tiled=True
        ).reshape(steps, BLK)
        table = lax.dynamic_slice_in_dim(
            jnp.asarray(inverse), lax.axis_index("low") * (2 * high), 2 * high, axis=0
        )
        table = lax.optimization_barrier(table)
        rows = lax.optimization_barrier(jnp.dot(table, slots, precision=HIGHEST))
        rows = lax.all_to_all(
            rows.reshape(high, 2, BLK), "high", split_axis=0, concat_axis=0, tiled=True
        ).reshape(2 * nb, BLK)
        new_state, new_mult = finish_call(
            g_cols,
            g_tiles,
            blocks(state).reshape(2 * nb, BLK),
            blocks(multiplier).reshape(2 * ncb, BLK),
            stab.reshape(ncb, BLK),
            pltpu.with_memory_space_constraint(rows, pltpu.VMEM),
            *[pltpu.with_memory_space_constraint(m, pltpu.VMEM) for m in mats[:2]],
        )

        def lines(value):
            return value.reshape(-1, 2, BLK).transpose(1, 0, 2).reshape(2, -1)

        return lines(new_state), lines(new_mult)

    return local


def solution(mesh):
    tm, co = mesh.shape["tm"], mesh.shape["coord"]
    low = 4
    split = Mesh(mesh.devices.reshape(tm // low, low, co), ("high", "low", "coord"))
    forward, inverse, factors = tables(2 * tm, low)
    time = ("high", "low")
    return jax.shard_map(
        make_local(forward, inverse, factors, low),
        mesh=split,
        in_specs=(
            P(time, "coord"),
            P(time, "coord"),
            P(time, "coord"),
            P("coord"),
            P("coord"),
            P("coord"),
            P("coord"),
            P(),
            P("coord", None),
            P("coord", None),
            P("coord", None),
            P("coord", None),
        ),
        out_specs=(P(time, "coord"), P(time, "coord")),
        check_vma=False,
    )
```

```python
import functools
import math

import jax
import jax.numpy as jnp
import ml_dtypes
import numpy as np
from jax import lax
from jax.experimental import pallas as pl
from jax.experimental.pallas import tpu as pltpu
from jax.sharding import Mesh, PartitionSpec as P

BLK = 128
REACH = 2
SWEEPS = 8
ALPHA = 0.001
HIGHEST = lax.Precision.HIGHEST
F32 = jnp.float32
BF16 = jnp.bfloat16


def tables(steps, low):
    ids = np.arange(steps)
    frequency = np.where(ids == 1, steps // 2, ids // 2)
    angles = 2.0 * np.pi / steps * ((frequency[:, None] * ids[None, :]) % steps)
    is_sine = (ids % 2 == 1) & (ids > 1)
    wave = np.where(is_sine[:, None], -np.sin(angles), np.cos(angles))
    scale = np.exp(math.log(ALPHA) * ids / steps)
    forward = wave * scale[None, :]
    weights = np.where(ids < 2, 1.0, 2.0) / steps
    inverse = (wave * weights[:, None]).T / scale[:, None]
    inverse = inverse.reshape(steps // (2 * low), low, 2, steps).swapaxes(0, 1).reshape(steps, steps)
    beta = math.exp(math.log(ALPHA) / steps)
    pair = np.arange(steps // 2)
    theta = 2.0 * np.pi * pair / steps
    zero = pair == 0
    a_even = np.where(zero, 1.0 - beta, 1.0 - beta * np.cos(theta))
    a_odd = np.where(zero, 1.0 + beta, 1.0 - beta * np.cos(theta))
    b_even = np.where(zero, 0.0, -beta * np.sin(theta))
    factors = np.stack([a_even, a_odd, b_even, zero.astype(np.float64)], axis=1)
    return pieces_of(forward), inverse.astype(np.float32), factors.astype(np.float32)


def pieces_of(table):
    rest, pieces = table.astype(np.float32), []
    for _ in range(3):
        pieces.append(rest.astype(ml_dtypes.bfloat16))
        rest = rest - pieces[-1].astype(np.float32)
    return pieces


def split3(value):
    high = value.astype(BF16)
    rest = value - high.astype(F32)
    mid = rest.astype(BF16)
    return high, mid, (rest - mid.astype(F32)).astype(BF16)


def bank_kernel(bank_ref, w1, w2, v1, v2):
    for tile in range(bank_ref.shape[0]):
        value = bank_ref[tile]
        for mat, outs in ((value, (w1, w2)), (value.T, (v1, v2))):
            for out, piece in zip(outs, split3(mat)):
                out[tile] = piece


def gather_kernel(state, force, mult, out, sbuf, fbuf, mbuf, sin, sout):
    ns, nm = sbuf.shape[0], mbuf.shape[0]
    pairs = [(state, sbuf), (force, fbuf), (mult, mbuf)]
    loads = [pltpu.make_async_copy(a, b, sin.at[i]) for i, (a, b) in enumerate(pairs)]
    for load in loads:
        load.start()
    targets = [(sbuf, 0, ns), (fbuf, ns, ns), (mbuf, 2 * ns, nm), (sbuf, 2 * ns + nm, ns)]
    end = 3 * ns + nm
    while end < out.shape[0]:
        count = min(ns, out.shape[0] - end)
        targets.append((fbuf, end, count))
        end += count
    stores = []
    for load, (_, buf) in zip(loads, pairs):
        load.wait()
        for src, start, count in targets:
            if src is buf:
                stores.append(
                    pltpu.make_async_copy(
                        buf.at[pl.ds(0, count)], out.at[pl.ds(start, count)], sout.at[len(stores)]
                    )
                )
                stores[-1].start()
    for store in stores:
        store.wait()


def extra_kernel(at_ref, initial, mass, stiff, stab, offs, ktiles, cols, gtiles, out, buf):
    nb, ncb = mass.shape[0], stab.shape[0]
    buf[...] = jnp.zeros(buf.shape, F32)
    start = 0
    for first, second in (
        (initial[...], mass[...]),
        (stiff[: nb // 2], stiff[nb // 2 :]),
        (stab[: ncb // 2], stab[ncb // 2 :]),
        (offs[...].astype(F32), ktiles[...].astype(F32)),
        (cols[...].astype(F32), gtiles[...].astype(F32)),
    ):
        count, width = first.shape
        buf[pl.ds(start, count, stride=2), :width] = first
        buf[pl.ds(start + 1, count, stride=2), :width] = second
        start += 2 * count
    out[...] = buf[pl.ds(at_ref[0], 2), :]


def spread_kernel(at_ref, x_ref, extra, t1, t2, t3, out, buf, sems, *, wraps):
    rows = x_ref.shape[0]
    at = at_ref[0]

    @pl.when(at < 0)
    def _():
        high, mid, low = split3(x_ref[...])
        two = jnp.concatenate([high, mid], axis=1)
        res = jnp.dot(t2[...], two, preferred_element_type=F32)
        low_part = jnp.dot(t3[...], high, preferred_element_type=F32)
        low_part += jnp.dot(t1[...], low, preferred_element_type=F32)
        res += jnp.dot(t1[...], two, preferred_element_type=F32)
        res = res[:, :BLK] + (res[:, BLK:] + low_part)
        buf[...] = res.reshape(buf.shape)

    @pl.when(at >= 0)
    def _():
        first, second = extra[0:1], extra[1:2]
        wrap = second * (first - ALPHA * x_ref[rows - 1 : rows])
        first = jnp.where(at < wraps, wrap, first)
        even = lax.broadcasted_iota(jnp.int32, (2, BLK), 0) == 0
        buf[...] = jnp.broadcast_to(jnp.where(even, first, second)[None], buf.shape)

    copies = [
        pltpu.make_async_copy(buf, out.at[:, o], sems.at[o]) for o in range(out.shape[1])
    ]
    for copy in copies:
        copy.start()
    for copy in copies:
        copy.wait()


def finish_kernel(cols_ref, tiles_ref, state, mult, stab, update, w1, w2, new_state, new_mult):
    ncb, gnb = cols_ref.shape
    new_state[...] = state[...] + update[...]
    owner = lax.broadcasted_iota(jnp.int32, mult.shape, 0) // 2
    total = jnp.zeros(mult.shape, F32)
    for j in range(gnb):
        value = jnp.concatenate(
            [new_state[pl.ds(cols_ref[c, j] * 2, 2), :] for c in range(ncb)], axis=0
        )
        high, mid, _ = split3(value)
        two = jnp.concatenate([high, mid], axis=1)
        for c in range(ncb):
            b1, b2 = w1[tiles_ref[c, j]], w2[tiles_ref[c, j]]
            res = jnp.dot(two, jnp.concatenate([b1, b1]), preferred_element_type=F32)
            res += jnp.dot(two, jnp.concatenate([b2, b2]), preferred_element_type=F32)
            total += jnp.where(owner == c, res, 0.0)
    weight = jnp.zeros(mult.shape, F32)
    for c in range(ncb):
        weight = jnp.where(owner == c, stab[c : c + 1], weight)
    new_mult[...] = mult[...] + (total - weight * mult[...]) / weight


def swapped(value):
    rows = value.shape[0]
    even = lax.broadcasted_iota(jnp.int32, value.shape, 0) % 2 == 0
    return jnp.where(even, pltpu.roll(value, rows - 1, 0), pltpu.roll(value, 1, 0))


def doubled(value, odd):
    rows = value.shape[0]
    even = lax.broadcasted_iota(jnp.int32, value.shape, 0) % 2 == 0
    if odd:
        return jnp.where(even, pltpu.roll(value, rows - 1, 0), value)
    return jnp.where(even, value, pltpu.roll(value, 1, 0))


def make_solve(nb, ncb, co, tiles, knb, gnb, lay):
    nrow = 2 * nb * co
    crow = 2 * ncb * co
    prow = tiles * nrow
    nidx = 2 * co * (knb + ncb)

    def kernel(
        fac_ref, own_ref, r_ref, w1, w2, v1, v2, out_ref,
        p_ref, q_ref, acc, gts, xs, rhs, e_ref, c_ref, xt, xl, gy, sc, istab, wide, idxv, idxs, sem,
    ):
        a_even, a_odd, b_even, is_zero = fac_ref[0], fac_ref[1], fac_ref[2], fac_ref[3]

        def part(name, rows, start=0):
            start += lay[name] * 2 * co
            return r_ref[start : start + rows]

        raw = part("idx", nidx).astype(jnp.int32)
        lane = lax.broadcasted_iota(jnp.int32, raw.shape, 1)
        line = lax.broadcasted_iota(jnp.int32, raw.shape, 0)
        coord = (line >> 1) & (co - 1)
        column, tile = raw, pltpu.roll(raw, nidx - 1, 0)
        block = coord * nb + lane + column - REACH
        inside = (block >= 0) & (block < nb * co)
        k_row = ((block & (nb - 1)) * co + (block >> (nb.bit_length() - 1))) * 2
        k_row = jnp.where(inside, tile * nrow + k_row, prow)
        g_row = (column * co + coord) * 2
        q_row = tile * crow + line - 2 * knb * co
        q_row = pltpu.roll(q_row, gnb, 1)
        g_rows = jnp.where(lane < gnb, tile * nrow + g_row, pltpu.roll(g_row, 2 * gnb, 1))
        g_rows = jnp.where((lane >= gnb) & (lane < 2 * gnb), q_row, g_rows)
        wide[...] = jnp.where(line < 2 * knb * co, k_row, g_rows)
        idxv[...] = jnp.zeros(idxv.shape, jnp.int32)
        idxv[: nidx // 2] = wide[pl.ds(0, nidx // 2, stride=2), :]
        copy = pltpu.make_async_copy(idxv, idxs, sem)
        copy.start()
        p_ref[prow : prow + 8] = jnp.zeros((8, BLK), F32)
        gts[...] = jnp.zeros(gts.shape, F32)

        def products(x1, x2, x3, mats, dst, beside):
            rows = x1.shape[0]
            pairs = ((x1, x1), (x2, x2), (x3, jnp.zeros_like(x3)))
            stack = jnp.concatenate([jnp.concatenate(p, axis=1) for p in pairs], axis=0)
            m1, m2 = mats
            for pair in range(tiles // 2):
                b1 = jnp.concatenate([m1[2 * pair], m1[2 * pair + 1]], axis=1)
                b2 = jnp.concatenate([m2[2 * pair], m2[2 * pair + 1]], axis=1)
                res = jnp.dot(stack, jnp.concatenate([b1, b2]), preferred_element_type=F32)
                res = res[:rows] + (res[rows : 2 * rows] + res[2 * rows :])
                for side in range(2):
                    start = (2 * pair + side) * rows
                    dst[start : start + rows] = res[:, side * BLK : side * BLK + BLK]
                beside(pair)

        def couple(i):
            count = nb // (tiles // 2)
            for b in range(i * count, (i + 1) * count):
                for o in range(co):
                    row = (b * co + o) * 2
                    total = p_ref[pl.ds(idxs[o, b], 2), :]
                    for k in range(1, knb):
                        total = total + p_ref[pl.ds(idxs[k * co + o, b], 2), :]
                    acc[row : row + 2] = total

        def constrain():
            for c in range(ncb):
                for o in range(co):
                    row = (c * co + o) * 2
                    at = (knb + c) * co + o
                    total = p_ref[pl.ds(idxs[at, 0], 2), :]
                    for j in range(1, gnb):
                        total = total + p_ref[pl.ds(idxs[at, j], 2), :]
                    gy[row : row + 2] = total

        def scatter():
            for c in range(ncb):
                for o in range(co):
                    at = (knb + c) * co + o
                    for j in range(gnb):
                        src, dst = idxs[at, gnb + j], idxs[at, 2 * gnb + j]
                        gts[c, pl.ds(dst, 2), :] = q_ref[pl.ds(src, 2), :]

        def coupled(rows):
            total = acc[rows]
            for c in range(ncb):
                total = total + gts[c, rows]
            return total

        chunk = nrow // (tiles // 2)
        even = lax.broadcasted_iota(jnp.int32, (chunk, BLK), 0) % 2 == 0

        def prepare(i):
            start = i * chunk
            rows = slice(start, start + chunk)
            state = part("state", chunk, start)
            cm = part("wrap", chunk, start)
            mass = doubled(cm, True)
            stiff = doubled(part("stiff", chunk, start % (nrow // 2)), start >= nrow // 2)
            wrap = jnp.where(even, cm, is_zero * pltpu.roll(cm, 1, 0))
            d_self = jnp.where(even, a_even, a_odd) * mass + stiff
            d_other = jnp.where(even, a_odd, a_even) * mass + stiff
            cross = jnp.where(even, b_even, -b_even) * mass
            inv = 1.0 / (d_self * d_other + cross * cross)
            e_ref[rows] = d_other * inv
            c_ref[rows] = cross * inv
            rhs[rows] = part("force", chunk, start) + wrap - (d_self * state + cross * swapped(state))

        def advance(first):
            for i in range(nrow // chunk):
                rows = slice(i * chunk, i * chunk + chunk)
                res = rhs[rows] - coupled(rows)
                if first:
                    rhs[rows] = res
                value = e_ref[rows] * res - c_ref[rows] * swapped(res)
                xs[rows] = value
                xt[rows, :BLK], xt[rows, BLK:], xl[rows] = split3(value)

        mult = part("mult", crow)
        shalf = part("stab", crow // 2)
        stab = jnp.concatenate([doubled(shalf, False), doubled(shalf, True)], axis=0)
        istab[...] = 1.0 / stab
        products(*split3(part("state", nrow)), (w1, w2), p_ref, lambda i: None)
        copy.wait()

        def both(i):
            prepare(i)
            couple(i)

        products(*split3(mult), (v1, v2), q_ref, both)
        constrain()
        scatter()
        sc[...] = stab * mult - gy[...]
        advance(True)

        def sweep(_, carry):
            products(xt[:, :BLK], xt[:, BLK:], xl[...], (w1, w2), p_ref, lambda i: None)
            constrain()
            products(*split3((gy[...] - sc[...]) * istab[...]), (v1, v2), q_ref, couple)
            scatter()
            advance(False)
            return carry

        lax.fori_loop(0, SWEEPS - 1, sweep, 0)
        own = own_ref[0]
        parts = out_ref.shape[0] // (2 * nb)
        for b in range(nb):
            value = xs[pl.ds((b * co + own) * 2, 2), :]
            for z in range(parts):
                row = (b * parts + z) * 2
                out_ref[row : row + 2] = value

    return kernel, [
        pltpu.VMEM((prow + 8, BLK), F32),
        pltpu.VMEM((tiles * crow, BLK), F32),
        pltpu.VMEM((nrow, BLK), F32),
        pltpu.VMEM((ncb, nrow, BLK), F32),
        pltpu.VMEM((nrow, BLK), F32),
        pltpu.VMEM((nrow, BLK), F32),
        pltpu.VMEM((nrow, BLK), F32),
        pltpu.VMEM((nrow, BLK), F32),
        pltpu.VMEM((nrow, 2 * BLK), BF16),
        pltpu.VMEM((nrow, BLK), BF16),
        pltpu.VMEM((crow, BLK), F32),
        pltpu.VMEM((crow, BLK), F32),
        pltpu.VMEM((crow, BLK), F32),
        pltpu.VMEM((nidx, BLK), jnp.int32),
        pltpu.VMEM((-(-nidx // 16) * 8, BLK), jnp.int32),
        pltpu.SMEM((-(-nidx // 16) * 8, BLK), jnp.int32),
        pltpu.SemaphoreType.DMA(()),
    ]


VM = pl.BlockSpec(memory_space=pltpu.VMEM)
SM = pl.BlockSpec(memory_space=pltpu.SMEM)


def layout(nb, ncb):
    state, force, mult = 0, nb, 2 * nb
    wrap = mult + ncb
    stiff = wrap + nb
    stab = stiff + nb // 2
    idx = stab + ncb // 2
    return {"state": state, "force": force, "mult": mult, "wrap": wrap, "stiff": stiff, "stab": stab, "idx": idx}


def solve_call(fac, own, recv, mats, nb, ncb, co, tiles, knb, gnb, lay, parts):
    kernel, scratch = make_solve(nb, ncb, co, tiles, knb, gnb, lay)
    return pl.pallas_call(
        kernel,
        out_shape=jax.ShapeDtypeStruct((2 * nb * parts, BLK), F32),
        in_specs=[SM, SM] + [VM] * 5,
        out_specs=VM,
        scratch_shapes=scratch,
        name="solve",
    )(fac, own, recv, *mats)


def bank_call(bank):
    shape = jax.ShapeDtypeStruct(bank.shape, BF16)
    return pl.pallas_call(
        bank_kernel, out_shape=[shape] * 4, in_specs=[VM], out_specs=[VM] * 4, name="bank"
    )(bank)


def gather_call(state, force, mult, count):
    hbm = pl.BlockSpec(memory_space=pl.ANY)
    return pl.pallas_call(
        gather_kernel,
        out_shape=jax.ShapeDtypeStruct((count, 2, BLK), F32),
        in_specs=[hbm] * 3,
        out_specs=hbm,
        scratch_shapes=[pltpu.VMEM(v.shape, F32) for v in (state, force, mult)]
        + [pltpu.SemaphoreType.DMA((3,)), pltpu.SemaphoreType.DMA((8,))],
        name="gather",
    )(state, force, mult)


def extra_call(at, initial, mass, stiff, stab, offs, ktiles, cols, gtiles, rows):
    return pl.pallas_call(
        extra_kernel,
        out_shape=jax.ShapeDtypeStruct((2, BLK), F32),
        in_specs=[SM] + [VM] * 8,
        out_specs=VM,
        scratch_shapes=[pltpu.VMEM((rows, BLK), F32)],
        name="extra",
    )(at, initial, mass, stiff, stab, offs, ktiles, cols, gtiles)


def spread_call(at, columns, extra, pieces, co, wraps):
    return pl.pallas_call(
        functools.partial(spread_kernel, wraps=wraps),
        out_shape=jax.ShapeDtypeStruct((columns.shape[0] // 2, co, 2, BLK), F32),
        in_specs=[SM] + [VM] * 5,
        out_specs=pl.BlockSpec(memory_space=pl.ANY),
        scratch_shapes=[
            pltpu.VMEM((columns.shape[0] // 2, 2, BLK), F32),
            pltpu.SemaphoreType.DMA((co,)),
        ],
        name="spread",
    )(at, columns, extra, *pieces)


def finish_call(cols, tiles, state, mult, stab, update, w1, w2):
    return pl.pallas_call(
        finish_kernel,
        out_shape=[
            jax.ShapeDtypeStruct(state.shape, F32),
            jax.ShapeDtypeStruct(mult.shape, F32),
        ],
        in_specs=[SM, SM] + [VM] * 6,
        out_specs=[VM, VM],
        name="finish",
    )(cols, tiles, state, mult, stab, update, w1, w2)


def make_local(forward, inverse, factors, low):
    steps = forward[0].shape[0]
    group = ("high", "low")

    def blocks(value):
        return value.reshape(value.shape[0], -1, BLK).transpose(1, 0, 2)

    def local(
        state, multiplier, force, initial, mass, stiff_diag, stab,
        bank, k_offsets, k_tiles, g_cols, g_tiles,
    ):
        nb = state.shape[1] // BLK
        ncb = multiplier.shape[1] // BLK
        tiles = bank.shape[0]
        tm = lax.axis_size(group)
        co = lax.axis_size("coord")
        high = tm // low
        t = lax.axis_index(group)
        o = lax.axis_index("coord")
        lay = layout(nb, ncb)
        sent = gather_call(blocks(state), blocks(force), blocks(multiplier), tm)
        columns = lax.all_to_all(sent, group, split_axis=0, concat_axis=0, tiled=True)
        columns = pltpu.with_memory_space_constraint(columns.reshape(steps, BLK), pltpu.VMEM)
        at = t - lay["wrap"]
        count = 2 * (tm - lay["wrap"])
        extra = extra_call(
            jnp.clip(2 * at, 0, count - 2).reshape(1),
            initial.reshape(nb, BLK),
            mass.reshape(nb, BLK),
            stiff_diag.reshape(nb, BLK),
            stab.reshape(ncb, BLK),
            k_offsets.T,
            k_tiles.T,
            g_cols,
            g_tiles,
            -(-count // 8) * 8,
        )
        pieces = [pltpu.with_memory_space_constraint(jnp.asarray(p), pltpu.VMEM) for p in forward]
        spread = spread_call(at.reshape(1), columns, extra, pieces, co, nb)
        spread = spread.reshape(tm * co, 2, BLK)
        recv = lax.all_to_all(
            spread, group + ("coord",), split_axis=0, concat_axis=0, tiled=True
        ).reshape(tm * co * 2, BLK)

        mats = bank_call(bank)
        recv = pltpu.with_memory_space_constraint(recv, pltpu.VMEM)
        fac = lax.dynamic_index_in_dim(jnp.asarray(factors), t, 0, keepdims=False)
        solved = solve_call(
            fac, o.reshape(1).astype(jnp.int32), recv, mats,
            nb, ncb, co, tiles, k_tiles.shape[1], g_tiles.shape[1], lay, low,
        )
        slots = lax.all_to_all(
            solved.reshape(tm, 2, BLK), group, split_axis=0, concat_axis=0, tiled=True
        ).reshape(steps, BLK)
        table = lax.dynamic_slice_in_dim(
            jnp.asarray(inverse), lax.axis_index("low") * (2 * high), 2 * high, axis=0
        )
        table = lax.optimization_barrier(table)
        rows = lax.optimization_barrier(jnp.dot(table, slots, precision=HIGHEST))
        rows = lax.all_to_all(
            rows.reshape(high, 2, BLK), "high", split_axis=0, concat_axis=0, tiled=True
        ).reshape(2 * nb, BLK)
        new_state, new_mult = finish_call(
            g_cols,
            g_tiles,
            pltpu.with_memory_space_constraint(blocks(state).reshape(2 * nb, BLK), pltpu.VMEM),
            pltpu.with_memory_space_constraint(blocks(multiplier).reshape(2 * ncb, BLK), pltpu.VMEM),
            pltpu.with_memory_space_constraint(stab.reshape(ncb, BLK), pltpu.VMEM),
            pltpu.with_memory_space_constraint(rows, pltpu.VMEM),
            *[pltpu.with_memory_space_constraint(m, pltpu.VMEM) for m in mats[:2]],
        )

        def lines(value):
            return value.reshape(-1, 2, BLK).transpose(1, 0, 2).reshape(2, -1)

        return lines(new_state), lines(new_mult)

    return local


def solution(mesh):
    tm, co = mesh.shape["tm"], mesh.shape["coord"]
    low = 4
    split = Mesh(mesh.devices.reshape(tm // low, low, co), ("high", "low", "coord"))
    forward, inverse, factors = tables(2 * tm, low)
    time = ("high", "low")
    return jax.shard_map(
        make_local(forward, inverse, factors, low),
        mesh=split,
        in_specs=(
            P(time, "coord"),
            P(time, "coord"),
            P(time, "coord"),
            P("coord"),
            P("coord"),
            P("coord"),
            P("coord"),
            P(),
            P("coord", None),
            P("coord", None),
            P("coord", None),
            P("coord", None),
        ),
        out_specs=(P(time, "coord"), P(time, "coord")),
        check_vma=False,
    )
```

```python
import functools
import math

import jax
import jax.numpy as jnp
import ml_dtypes
import numpy as np
from jax import lax
from jax.experimental import pallas as pl
from jax.experimental.pallas import tpu as pltpu
from jax.sharding import Mesh, PartitionSpec as P

BLK = 128
REACH = 2
SWEEPS = 8
ALPHA = 0.001
HIGHEST = lax.Precision.HIGHEST
F32 = jnp.float32
BF16 = jnp.bfloat16


def tables(steps, low):
    ids = np.arange(steps)
    frequency = np.where(ids == 1, steps // 2, ids // 2)
    angles = 2.0 * np.pi / steps * ((frequency[:, None] * ids[None, :]) % steps)
    is_sine = (ids % 2 == 1) & (ids > 1)
    wave = np.where(is_sine[:, None], -np.sin(angles), np.cos(angles))
    scale = np.exp(math.log(ALPHA) * ids / steps)
    forward = wave * scale[None, :]
    weights = np.where(ids < 2, 1.0, 2.0) / steps
    inverse = (wave * weights[:, None]).T / scale[:, None]
    inverse = inverse.reshape(steps // (2 * low), low, 2, steps).swapaxes(0, 1).reshape(steps, steps)
    beta = math.exp(math.log(ALPHA) / steps)
    pair = np.arange(steps // 2)
    theta = 2.0 * np.pi * pair / steps
    zero = pair == 0
    a_even = np.where(zero, 1.0 - beta, 1.0 - beta * np.cos(theta))
    a_odd = np.where(zero, 1.0 + beta, 1.0 - beta * np.cos(theta))
    b_even = np.where(zero, 0.0, -beta * np.sin(theta))
    factors = np.stack([a_even, a_odd, b_even, zero.astype(np.float64)], axis=1)
    return pieces_of(forward), inverse.astype(np.float32), factors.astype(np.float32)


def pieces_of(table):
    rest, pieces = table.astype(np.float32), []
    for _ in range(3):
        pieces.append(rest.astype(ml_dtypes.bfloat16))
        rest = rest - pieces[-1].astype(np.float32)
    return pieces


def split3(value):
    high = value.astype(BF16)
    rest = value - high.astype(F32)
    mid = rest.astype(BF16)
    return high, mid, (rest - mid.astype(F32)).astype(BF16)


def bank_kernel(bank_ref, w1, w2, v1, v2):
    for tile in range(bank_ref.shape[0]):
        value = bank_ref[tile]
        for mat, outs in ((value, (w1, w2)), (value.T, (v1, v2))):
            for out, piece in zip(outs, split3(mat)):
                out[tile] = piece


def gather_kernel(state, force, mult, out, sbuf, fbuf, mbuf, sin, sout):
    ns, nm = sbuf.shape[0], mbuf.shape[0]
    pairs = [(state, sbuf), (force, fbuf), (mult, mbuf)]
    loads = [pltpu.make_async_copy(a, b, sin.at[i]) for i, (a, b) in enumerate(pairs)]
    for load in loads:
        load.start()
    targets = [(sbuf, 0, ns), (fbuf, ns, ns), (mbuf, 2 * ns, nm), (sbuf, 2 * ns + nm, ns)]
    end = 3 * ns + nm
    while end < out.shape[0]:
        count = min(ns, out.shape[0] - end)
        targets.append((fbuf, end, count))
        end += count
    stores = []
    for load, (_, buf) in zip(loads, pairs):
        load.wait()
        for src, start, count in targets:
            if src is buf:
                stores.append(
                    pltpu.make_async_copy(
                        buf.at[pl.ds(0, count)], out.at[pl.ds(start, count)], sout.at[len(stores)]
                    )
                )
                stores[-1].start()
    for store in stores:
        store.wait()


def extra_kernel(at_ref, initial, mass, stiff, stab, offs, ktiles, cols, gtiles, out, buf):
    nb, ncb = mass.shape[0], stab.shape[0]
    buf[...] = jnp.zeros(buf.shape, F32)
    start = 0
    for first, second in (
        (initial[...], mass[...]),
        (stiff[: nb // 2], stiff[nb // 2 :]),
        (stab[: ncb // 2], stab[ncb // 2 :]),
        (offs[...].astype(F32), ktiles[...].astype(F32)),
        (cols[...].astype(F32), gtiles[...].astype(F32)),
    ):
        count, width = first.shape
        buf[pl.ds(start, count, stride=2), :width] = first
        buf[pl.ds(start + 1, count, stride=2), :width] = second
        start += 2 * count
    out[...] = buf[pl.ds(at_ref[0], 2), :]


def spread_kernel(at_ref, x_ref, extra, t1, t2, t3, out, buf, wide, sems, *, wraps):
    rows = x_ref.shape[0]
    at = at_ref[0]

    @pl.when(at < 0)
    def _():
        high, mid, low = split3(x_ref[...])
        two = jnp.concatenate([high, mid], axis=1)
        res = jnp.dot(t2[...], two, preferred_element_type=F32)
        low_part = jnp.dot(t3[...], high, preferred_element_type=F32)
        low_part += jnp.dot(t1[...], low, preferred_element_type=F32)
        res += jnp.dot(t1[...], two, preferred_element_type=F32)
        buf[...] = res[:, :BLK] + (res[:, BLK:] + low_part)

    @pl.when(at >= 0)
    def _():
        first, second = extra[0:1], extra[1:2]
        wrap = second * (first - ALPHA * x_ref[rows - 1 : rows])
        first = jnp.where(at < wraps, wrap, first)
        even = lax.broadcasted_iota(jnp.int32, buf.shape, 0) % 2 == 0
        buf[...] = jnp.where(even, first, second)

    each = out.shape[0] // (rows // 2)
    even = lax.broadcasted_iota(jnp.int32, (each, BLK), 0) % 2 == 0
    parts = sems.shape[0]
    size = out.shape[0] // parts
    copies = []
    for part in range(parts):
        for p in range(part * rows // (2 * parts), (part + 1) * rows // (2 * parts)):
            wide[p * each : (p + 1) * each] = jnp.where(
                even, buf[2 * p : 2 * p + 1], buf[2 * p + 1 : 2 * p + 2]
            )
        span = pl.ds(part * size, size)
        copies.append(pltpu.make_async_copy(wide.at[span], out.at[span], sems.at[part]))
        copies[-1].start()
    for copy in copies:
        copy.wait()


def finish_kernel(
    cols_ref, tiles_ref, state, mult, stab, update, w1, w2, out_state, new_mult, new_state, sem
):
    ncb, gnb = cols_ref.shape
    new_state[...] = state[...] + update[...]
    copy = pltpu.make_async_copy(new_state, out_state, sem)
    copy.start()
    owner = lax.broadcasted_iota(jnp.int32, mult.shape, 0) // 2
    total = jnp.zeros(mult.shape, F32)
    for j in range(gnb):
        value = jnp.concatenate(
            [new_state[pl.ds(cols_ref[c, j] * 2, 2), :] for c in range(ncb)], axis=0
        )
        high, mid, _ = split3(value)
        two = jnp.concatenate([high, mid], axis=1)
        for c in range(ncb):
            b1, b2 = w1[tiles_ref[c, j]], w2[tiles_ref[c, j]]
            res = jnp.dot(two, jnp.concatenate([b1, b1]), preferred_element_type=F32)
            res += jnp.dot(two, jnp.concatenate([b2, b2]), preferred_element_type=F32)
            total += jnp.where(owner == c, res, 0.0)
    weight = jnp.zeros(mult.shape, F32)
    for c in range(ncb):
        weight = jnp.where(owner == c, stab[c : c + 1], weight)
    new_mult[...] = mult[...] + (total - weight * mult[...]) / weight
    copy.wait()


def swapped(value):
    rows = value.shape[0]
    even = lax.broadcasted_iota(jnp.int32, value.shape, 0) % 2 == 0
    return jnp.where(even, pltpu.roll(value, rows - 1, 0), pltpu.roll(value, 1, 0))


def doubled(value, odd):
    rows = value.shape[0]
    even = lax.broadcasted_iota(jnp.int32, value.shape, 0) % 2 == 0
    if odd:
        return jnp.where(even, pltpu.roll(value, rows - 1, 0), value)
    return jnp.where(even, value, pltpu.roll(value, 1, 0))


def make_solve(nb, ncb, co, tiles, knb, gnb, lay):
    nrow = 2 * nb * co
    crow = 2 * ncb * co
    prow = tiles * nrow
    nidx = 2 * co * (knb + ncb)

    def kernel(
        fac_ref, own_ref, r_ref, w1, w2, v1, v2, out_ref,
        p_ref, q_ref, acc, gts, xs, rhs, e_ref, c_ref, xt, xl, gy, sc, istab, wide, idxv, idxs, sem,
    ):
        a_even, a_odd, b_even, is_zero = fac_ref[0], fac_ref[1], fac_ref[2], fac_ref[3]

        def part(name, rows, start=0):
            start += lay[name] * 2 * co
            return r_ref[start : start + rows]

        raw = part("idx", nidx).astype(jnp.int32)
        lane = lax.broadcasted_iota(jnp.int32, raw.shape, 1)
        line = lax.broadcasted_iota(jnp.int32, raw.shape, 0)
        coord = (line >> 1) & (co - 1)
        column, tile = raw, pltpu.roll(raw, nidx - 1, 0)
        block = coord * nb + lane + column - REACH
        inside = (block >= 0) & (block < nb * co)
        k_row = ((block & (nb - 1)) * co + (block >> (nb.bit_length() - 1))) * 2
        k_row = jnp.where(inside, tile * nrow + k_row, prow)
        g_row = (column * co + coord) * 2
        q_row = tile * crow + line - 2 * knb * co
        q_row = pltpu.roll(q_row, gnb, 1)
        g_rows = jnp.where(lane < gnb, tile * nrow + g_row, pltpu.roll(g_row, 2 * gnb, 1))
        g_rows = jnp.where((lane >= gnb) & (lane < 2 * gnb), q_row, g_rows)
        wide[...] = jnp.where(line < 2 * knb * co, k_row, g_rows)
        idxv[...] = jnp.zeros(idxv.shape, jnp.int32)
        idxv[: nidx // 2] = wide[pl.ds(0, nidx // 2, stride=2), :]
        copy = pltpu.make_async_copy(idxv, idxs, sem)
        copy.start()
        p_ref[prow : prow + 8] = jnp.zeros((8, BLK), F32)
        gts[...] = jnp.zeros(gts.shape, F32)

        def products(x1, x2, x3, mats, dst, beside):
            rows = x1.shape[0]
            pairs = ((x1, x1), (x2, x2), (x3, jnp.zeros_like(x3)))
            stack = jnp.concatenate([jnp.concatenate(p, axis=1) for p in pairs], axis=0)
            m1, m2 = mats
            for pair in range(tiles // 2):
                b1 = jnp.concatenate([m1[2 * pair], m1[2 * pair + 1]], axis=1)
                b2 = jnp.concatenate([m2[2 * pair], m2[2 * pair + 1]], axis=1)
                res = jnp.dot(stack, jnp.concatenate([b1, b2]), preferred_element_type=F32)
                res = res[:rows] + (res[rows : 2 * rows] + res[2 * rows :])
                for side in range(2):
                    start = (2 * pair + side) * rows
                    dst[start : start + rows] = res[:, side * BLK : side * BLK + BLK]
                beside(pair)

        def couple(i):
            count = nb // (tiles // 2)
            for b in range(i * count, (i + 1) * count):
                for o in range(co):
                    row = (b * co + o) * 2
                    total = p_ref[pl.ds(idxs[o, b], 2), :]
                    for k in range(1, knb):
                        total = total + p_ref[pl.ds(idxs[k * co + o, b], 2), :]
                    acc[row : row + 2] = total

        def constrain():
            for c in range(ncb):
                for o in range(co):
                    row = (c * co + o) * 2
                    at = (knb + c) * co + o
                    total = p_ref[pl.ds(idxs[at, 0], 2), :]
                    for j in range(1, gnb):
                        total = total + p_ref[pl.ds(idxs[at, j], 2), :]
                    gy[row : row + 2] = total

        def scatter():
            for c in range(ncb):
                for o in range(co):
                    at = (knb + c) * co + o
                    for j in range(gnb):
                        src, dst = idxs[at, gnb + j], idxs[at, 2 * gnb + j]
                        gts[c, pl.ds(dst, 2), :] = q_ref[pl.ds(src, 2), :]

        def coupled(rows):
            total = acc[rows]
            for c in range(ncb):
                total = total + gts[c, rows]
            return total

        chunk = nrow // (tiles // 2)
        even = lax.broadcasted_iota(jnp.int32, (chunk, BLK), 0) % 2 == 0

        def prepare(i):
            start = i * chunk
            rows = slice(start, start + chunk)
            state = part("state", chunk, start)
            cm = part("wrap", chunk, start)
            mass = doubled(cm, True)
            stiff = doubled(part("stiff", chunk, start % (nrow // 2)), start >= nrow // 2)
            wrap = jnp.where(even, cm, is_zero * pltpu.roll(cm, 1, 0))
            d_self = jnp.where(even, a_even, a_odd) * mass + stiff
            d_other = jnp.where(even, a_odd, a_even) * mass + stiff
            cross = jnp.where(even, b_even, -b_even) * mass
            inv = 1.0 / (d_self * d_other + cross * cross)
            e_ref[rows] = d_other * inv
            c_ref[rows] = cross * inv
            rhs[rows] = part("force", chunk, start) + wrap - (d_self * state + cross * swapped(state))

        def advance(first):
            for i in range(nrow // chunk):
                rows = slice(i * chunk, i * chunk + chunk)
                res = rhs[rows] - coupled(rows)
                if first:
                    rhs[rows] = res
                value = e_ref[rows] * res - c_ref[rows] * swapped(res)
                xs[rows] = value
                xt[rows, :BLK], xt[rows, BLK:], xl[rows] = split3(value)

        mult = part("mult", crow)
        shalf = part("stab", crow // 2)
        stab = jnp.concatenate([doubled(shalf, False), doubled(shalf, True)], axis=0)
        istab[...] = 1.0 / stab
        products(*split3(part("state", nrow)), (w1, w2), p_ref, lambda i: None)
        copy.wait()

        def both(i):
            prepare(i)
            couple(i)

        products(*split3(mult), (v1, v2), q_ref, both)
        constrain()
        scatter()
        sc[...] = stab * mult - gy[...]
        advance(True)

        def sweep(_, carry):
            products(xt[:, :BLK], xt[:, BLK:], xl[...], (w1, w2), p_ref, lambda i: None)
            constrain()
            products(*split3((gy[...] - sc[...]) * istab[...]), (v1, v2), q_ref, couple)
            scatter()
            advance(False)
            return carry

        lax.fori_loop(0, SWEEPS - 1, sweep, 0)
        own = own_ref[0]
        parts = out_ref.shape[0] // (2 * nb)
        for b in range(nb):
            value = xs[pl.ds((b * co + own) * 2, 2), :]
            for z in range(parts):
                row = (b * parts + z) * 2
                out_ref[row : row + 2] = value

    return kernel, [
        pltpu.VMEM((prow + 8, BLK), F32),
        pltpu.VMEM((tiles * crow, BLK), F32),
        pltpu.VMEM((nrow, BLK), F32),
        pltpu.VMEM((ncb, nrow, BLK), F32),
        pltpu.VMEM((nrow, BLK), F32),
        pltpu.VMEM((nrow, BLK), F32),
        pltpu.VMEM((nrow, BLK), F32),
        pltpu.VMEM((nrow, BLK), F32),
        pltpu.VMEM((nrow, 2 * BLK), BF16),
        pltpu.VMEM((nrow, BLK), BF16),
        pltpu.VMEM((crow, BLK), F32),
        pltpu.VMEM((crow, BLK), F32),
        pltpu.VMEM((crow, BLK), F32),
        pltpu.VMEM((nidx, BLK), jnp.int32),
        pltpu.VMEM((-(-nidx // 16) * 8, BLK), jnp.int32),
        pltpu.SMEM((-(-nidx // 16) * 8, BLK), jnp.int32),
        pltpu.SemaphoreType.DMA(()),
    ]


VM = pl.BlockSpec(memory_space=pltpu.VMEM)
SM = pl.BlockSpec(memory_space=pltpu.SMEM)


def layout(nb, ncb):
    state, force, mult = 0, nb, 2 * nb
    wrap = mult + ncb
    stiff = wrap + nb
    stab = stiff + nb // 2
    idx = stab + ncb // 2
    return {"state": state, "force": force, "mult": mult, "wrap": wrap, "stiff": stiff, "stab": stab, "idx": idx}


def solve_call(fac, own, recv, mats, nb, ncb, co, tiles, knb, gnb, lay, parts):
    kernel, scratch = make_solve(nb, ncb, co, tiles, knb, gnb, lay)
    return pl.pallas_call(
        kernel,
        out_shape=jax.ShapeDtypeStruct((2 * nb * parts, BLK), F32),
        in_specs=[SM, SM] + [VM] * 5,
        out_specs=VM,
        scratch_shapes=scratch,
        name="solve",
    )(fac, own, recv, *mats)


def bank_call(bank):
    shape = jax.ShapeDtypeStruct(bank.shape, BF16)
    return pl.pallas_call(
        bank_kernel, out_shape=[shape] * 4, in_specs=[VM], out_specs=[VM] * 4, name="bank"
    )(bank)


def gather_call(state, force, mult, count):
    hbm = pl.BlockSpec(memory_space=pl.ANY)
    return pl.pallas_call(
        gather_kernel,
        out_shape=jax.ShapeDtypeStruct((count, 2, BLK), F32),
        in_specs=[hbm] * 3,
        out_specs=hbm,
        scratch_shapes=[pltpu.VMEM(v.shape, F32) for v in (state, force, mult)]
        + [pltpu.SemaphoreType.DMA((3,)), pltpu.SemaphoreType.DMA((8,))],
        name="gather",
    )(state, force, mult)


def extra_call(at, initial, mass, stiff, stab, offs, ktiles, cols, gtiles, rows):
    return pl.pallas_call(
        extra_kernel,
        out_shape=jax.ShapeDtypeStruct((2, BLK), F32),
        in_specs=[SM] + [VM] * 8,
        out_specs=VM,
        scratch_shapes=[pltpu.VMEM((rows, BLK), F32)],
        name="extra",
    )(at, initial, mass, stiff, stab, offs, ktiles, cols, gtiles)


def spread_call(at, columns, extra, pieces, co, wraps):
    return pl.pallas_call(
        functools.partial(spread_kernel, wraps=wraps),
        out_shape=jax.ShapeDtypeStruct((columns.shape[0] * co, BLK), F32),
        in_specs=[SM] + [VM] * 5,
        out_specs=pl.BlockSpec(memory_space=pl.ANY),
        scratch_shapes=[
            pltpu.VMEM(columns.shape, F32),
            pltpu.VMEM((columns.shape[0] * co, BLK), F32),
            pltpu.SemaphoreType.DMA((4,)),
        ],
        name="spread",
    )(at, columns, extra, *pieces)


def finish_call(cols, tiles, state, mult, stab, update, w1, w2):
    return pl.pallas_call(
        finish_kernel,
        out_shape=[
            jax.ShapeDtypeStruct(state.shape, F32),
            jax.ShapeDtypeStruct(mult.shape, F32),
        ],
        in_specs=[SM, SM] + [VM] * 6,
        out_specs=[pl.BlockSpec(memory_space=pl.ANY), VM],
        scratch_shapes=[pltpu.VMEM(state.shape, F32), pltpu.SemaphoreType.DMA(())],
        name="finish",
    )(cols, tiles, state, mult, stab, update, w1, w2)


def make_local(forward, inverse, factors, low):
    steps = forward[0].shape[0]
    group = ("high", "low")

    def blocks(value):
        return value.reshape(value.shape[0], -1, BLK).transpose(1, 0, 2)

    def local(
        state, multiplier, force, initial, mass, stiff_diag, stab,
        bank, k_offsets, k_tiles, g_cols, g_tiles,
    ):
        nb = state.shape[1] // BLK
        ncb = multiplier.shape[1] // BLK
        tiles = bank.shape[0]
        tm = lax.axis_size(group)
        co = lax.axis_size("coord")
        high = tm // low
        t = lax.axis_index(group)
        o = lax.axis_index("coord")
        lay = layout(nb, ncb)
        sent = gather_call(blocks(state), blocks(force), blocks(multiplier), tm)
        columns = lax.all_to_all(sent, group, split_axis=0, concat_axis=0, tiled=True)
        columns = pltpu.with_memory_space_constraint(columns.reshape(steps, BLK), pltpu.VMEM)
        at = t - lay["wrap"]
        count = 2 * (tm - lay["wrap"])
        extra = extra_call(
            jnp.clip(2 * at, 0, count - 2).reshape(1),
            initial.reshape(nb, BLK),
            mass.reshape(nb, BLK),
            stiff_diag.reshape(nb, BLK),
            stab.reshape(ncb, BLK),
            k_offsets.T,
            k_tiles.T,
            g_cols,
            g_tiles,
            -(-count // 8) * 8,
        )
        pieces = [pltpu.with_memory_space_constraint(jnp.asarray(p), pltpu.VMEM) for p in forward]
        spread = spread_call(at.reshape(1), columns, extra, pieces, co, nb)
        spread = spread.reshape(tm * co, 2, BLK)
        recv = lax.all_to_all(
            spread, group + ("coord",), split_axis=0, concat_axis=0, tiled=True
        ).reshape(tm * co * 2, BLK)

        mats = list(bank_call(bank))
        mats = [pltpu.with_memory_space_constraint(m, pltpu.VMEM) for m in mats[:2]] + mats[2:]
        recv = pltpu.with_memory_space_constraint(recv, pltpu.VMEM)
        fac = lax.dynamic_index_in_dim(jnp.asarray(factors), t, 0, keepdims=False)
        solved = solve_call(
            fac, o.reshape(1).astype(jnp.int32), recv, mats,
            nb, ncb, co, tiles, k_tiles.shape[1], g_tiles.shape[1], lay, low,
        )
        slots = lax.all_to_all(
            solved.reshape(tm, 2, BLK), group, split_axis=0, concat_axis=0, tiled=True
        ).reshape(steps, BLK)
        table = lax.dynamic_slice_in_dim(
            jnp.asarray(inverse), lax.axis_index("low") * (2 * high), 2 * high, axis=0
        )
        table = lax.optimization_barrier(table)
        kept = (
            blocks(state).reshape(2 * nb, BLK),
            blocks(multiplier).reshape(2 * ncb, BLK),
            stab.reshape(ncb, BLK),
        )
        kept = [pltpu.with_memory_space_constraint(v, pltpu.VMEM) for v in kept]
        rows, *kept = lax.optimization_barrier(
            (jnp.dot(table, slots, precision=HIGHEST), *kept)
        )
        rows = lax.all_to_all(
            rows.reshape(high, 2, BLK), "high", split_axis=0, concat_axis=0, tiled=True
        ).reshape(2 * nb, BLK)
        new_state, new_mult = finish_call(
            g_cols,
            g_tiles,
            *kept,
            pltpu.with_memory_space_constraint(rows, pltpu.VMEM),
            *mats[:2],
        )

        def lines(value):
            return value.reshape(-1, 2, BLK).transpose(1, 0, 2).reshape(2, -1)

        return lines(new_state), lines(new_mult)

    return local


def solution(mesh):
    tm, co = mesh.shape["tm"], mesh.shape["coord"]
    low = 4
    split = Mesh(mesh.devices.reshape(tm // low, low, co), ("high", "low", "coord"))
    forward, inverse, factors = tables(2 * tm, low)
    time = ("high", "low")
    return jax.shard_map(
        make_local(forward, inverse, factors, low),
        mesh=split,
        in_specs=(
            P(time, "coord"),
            P(time, "coord"),
            P(time, "coord"),
            P("coord"),
            P("coord"),
            P("coord"),
            P("coord"),
            P(),
            P("coord", None),
            P("coord", None),
            P("coord", None),
            P("coord", None),
        ),
        out_specs=(P(time, "coord"), P(time, "coord")),
        check_vma=False,
    )
```

```python
import math

import jax
import jax.numpy as jnp
import numpy as np
from jax import lax
from jax.experimental import pallas as pl
from jax.experimental.pallas import tpu as pltpu
from jax.sharding import Mesh, PartitionSpec as P

BLK = 128
REACH = 2
SWEEPS = 8
ALPHA = 0.001
HIGHEST = lax.Precision.HIGHEST
F32 = jnp.float32
BF16 = jnp.bfloat16


def tables(steps, low):
    ids = np.arange(steps)
    frequency = np.where(ids == 1, steps // 2, ids // 2)
    angles = 2.0 * np.pi / steps * ((frequency[:, None] * ids[None, :]) % steps)
    is_sine = (ids % 2 == 1) & (ids > 1)
    wave = np.where(is_sine[:, None], -np.sin(angles), np.cos(angles))
    scale = np.exp(math.log(ALPHA) * ids / steps)
    forward = wave * scale[None, :]
    weights = np.where(ids < 2, 1.0, 2.0) / steps
    inverse = (wave * weights[:, None]).T / scale[:, None]
    inverse = inverse.reshape(steps // (2 * low), low, 2, steps).swapaxes(0, 1).reshape(steps, steps)
    beta = math.exp(math.log(ALPHA) / steps)
    pair = np.arange(steps // 2)
    theta = 2.0 * np.pi * pair / steps
    zero = pair == 0
    a_even = np.where(zero, 1.0 - beta, 1.0 - beta * np.cos(theta))
    a_odd = np.where(zero, 1.0 + beta, 1.0 - beta * np.cos(theta))
    b_even = np.where(zero, 0.0, -beta * np.sin(theta))
    factors = np.stack([a_even, a_odd, b_even, zero.astype(np.float64)], axis=1)
    return forward.astype(np.float32), inverse.astype(np.float32), factors.astype(np.float32)


def split3(value):
    high = value.astype(BF16)
    rest = value - high.astype(F32)
    mid = rest.astype(BF16)
    return high, mid, (rest - mid.astype(F32)).astype(BF16)


def bank_kernel(bank_ref, w1, w2, v1, v2):
    for tile in range(bank_ref.shape[0]):
        value = bank_ref[tile]
        for mat, outs in ((value, (w1, w2)), (value.T, (v1, v2))):
            for out, piece in zip(outs, split3(mat)):
                out[tile] = piece


def gather_kernel(state, force, mult, out, sbuf, fbuf, mbuf, sin, sout):
    ns, nm = sbuf.shape[0], mbuf.shape[0]
    pairs = [(state, sbuf), (force, fbuf), (mult, mbuf)]
    loads = [pltpu.make_async_copy(a, b, sin.at[i]) for i, (a, b) in enumerate(pairs)]
    for load in loads:
        load.start()
    targets = [(sbuf, 0, ns), (fbuf, ns, ns), (mbuf, 2 * ns, nm), (sbuf, 2 * ns + nm, ns)]
    end = 3 * ns + nm
    while end < out.shape[0]:
        count = min(ns, out.shape[0] - end)
        targets.append((fbuf, end, count))
        end += count
    stores = []
    for load, (_, buf) in zip(loads, pairs):
        load.wait()
        for src, start, count in targets:
            if src is buf:
                stores.append(
                    pltpu.make_async_copy(
                        buf.at[pl.ds(0, count)], out.at[pl.ds(start, count)], sout.at[len(stores)]
                    )
                )
                stores[-1].start()
    for store in stores:
        store.wait()


def extra_kernel(at_ref, initial, mass, stiff, stab, offs, ktiles, cols, gtiles, out, buf):
    nb, ncb = mass.shape[0], stab.shape[0]
    buf[...] = jnp.zeros(buf.shape, F32)
    start = 0
    for first, second in (
        (initial[...], mass[...]),
        (stiff[: nb // 2], stiff[nb // 2 :]),
        (stab[: ncb // 2], stab[ncb // 2 :]),
        (offs[...].astype(F32), ktiles[...].astype(F32)),
        (cols[...].astype(F32), gtiles[...].astype(F32)),
    ):
        count, width = first.shape
        buf[pl.ds(start, count, stride=2), :width] = first
        buf[pl.ds(start + 1, count, stride=2), :width] = second
        start += 2 * count
    out[...] = buf[pl.ds(at_ref[0], 2), :]


def finish_kernel(cols_ref, tiles_ref, state, mult, stab, update, w1, w2, new_state, new_mult):
    ncb, gnb = cols_ref.shape
    new_state[...] = state[...] + update[...]
    owner = lax.broadcasted_iota(jnp.int32, mult.shape, 0) // 2
    total = jnp.zeros(mult.shape, F32)
    for j in range(gnb):
        value = jnp.concatenate(
            [new_state[pl.ds(cols_ref[c, j] * 2, 2), :] for c in range(ncb)], axis=0
        )
        high, mid, _ = split3(value)
        two = jnp.concatenate([high, mid], axis=1)
        for c in range(ncb):
            b1, b2 = w1[tiles_ref[c, j]], w2[tiles_ref[c, j]]
            res = jnp.dot(two, jnp.concatenate([b1, b1]), preferred_element_type=F32)
            res += jnp.dot(two, jnp.concatenate([b2, b2]), preferred_element_type=F32)
            total += jnp.where(owner == c, res, 0.0)
    weight = jnp.zeros(mult.shape, F32)
    for c in range(ncb):
        weight = jnp.where(owner == c, stab[c : c + 1], weight)
    new_mult[...] = mult[...] + (total - weight * mult[...]) / weight


def swapped(value):
    rows = value.shape[0]
    even = lax.broadcasted_iota(jnp.int32, value.shape, 0) % 2 == 0
    return jnp.where(even, pltpu.roll(value, rows - 1, 0), pltpu.roll(value, 1, 0))


def doubled(value, odd):
    rows = value.shape[0]
    even = lax.broadcasted_iota(jnp.int32, value.shape, 0) % 2 == 0
    if odd:
        return jnp.where(even, pltpu.roll(value, rows - 1, 0), value)
    return jnp.where(even, value, pltpu.roll(value, 1, 0))


def make_solve(nb, ncb, co, tiles, knb, gnb, lay):
    nrow = 2 * nb * co
    crow = 2 * ncb * co
    prow = tiles * nrow
    nidx = 2 * co * (knb + ncb)

    def kernel(
        fac_ref, own_ref, r_ref, w1, w2, v1, v2, out_ref,
        p_ref, q_ref, acc, gts, xs, rhs, e_ref, c_ref, xt, xl, gy, sc, istab, wide, idxv, idxs, sem,
    ):
        a_even, a_odd, b_even, is_zero = fac_ref[0], fac_ref[1], fac_ref[2], fac_ref[3]

        def part(name, rows, start=0):
            start += lay[name] * 2 * co
            return r_ref[start : start + rows]

        raw = part("idx", nidx).astype(jnp.int32)
        lane = lax.broadcasted_iota(jnp.int32, raw.shape, 1)
        line = lax.broadcasted_iota(jnp.int32, raw.shape, 0)
        coord = (line >> 1) & (co - 1)
        column, tile = raw, pltpu.roll(raw, nidx - 1, 0)
        block = coord * nb + lane + column - REACH
        inside = (block >= 0) & (block < nb * co)
        k_row = ((block & (nb - 1)) * co + (block >> (nb.bit_length() - 1))) * 2
        k_row = jnp.where(inside, tile * nrow + k_row, prow)
        g_row = (column * co + coord) * 2
        q_row = tile * crow + line - 2 * knb * co
        q_row = pltpu.roll(q_row, gnb, 1)
        g_rows = jnp.where(lane < gnb, tile * nrow + g_row, pltpu.roll(g_row, 2 * gnb, 1))
        g_rows = jnp.where((lane >= gnb) & (lane < 2 * gnb), q_row, g_rows)
        wide[...] = jnp.where(line < 2 * knb * co, k_row, g_rows)
        idxv[...] = jnp.zeros(idxv.shape, jnp.int32)
        idxv[: nidx // 2] = wide[pl.ds(0, nidx // 2, stride=2), :]
        copy = pltpu.make_async_copy(idxv, idxs, sem)
        copy.start()
        p_ref[prow : prow + 8] = jnp.zeros((8, BLK), F32)
        gts[...] = jnp.zeros(gts.shape, F32)

        def products(x1, x2, x3, mats, dst, beside):
            rows = x1.shape[0]
            pairs = ((x1, x1), (x2, x2), (x3, jnp.zeros_like(x3)))
            stack = jnp.concatenate([jnp.concatenate(p, axis=1) for p in pairs], axis=0)
            m1, m2 = mats
            for pair in range(tiles // 2):
                b1 = jnp.concatenate([m1[2 * pair], m1[2 * pair + 1]], axis=1)
                b2 = jnp.concatenate([m2[2 * pair], m2[2 * pair + 1]], axis=1)
                res = jnp.dot(stack, jnp.concatenate([b1, b2]), preferred_element_type=F32)
                res = res[:rows] + (res[rows : 2 * rows] + res[2 * rows :])
                for side in range(2):
                    start = (2 * pair + side) * rows
                    dst[start : start + rows] = res[:, side * BLK : side * BLK + BLK]
                beside(pair)

        def couple(i):
            count = nb // (tiles // 2)
            for b in range(i * count, (i + 1) * count):
                for o in range(co):
                    row = (b * co + o) * 2
                    total = p_ref[pl.ds(idxs[o, b], 2), :]
                    for k in range(1, knb):
                        total = total + p_ref[pl.ds(idxs[k * co + o, b], 2), :]
                    acc[row : row + 2] = total

        def constrain():
            for c in range(ncb):
                for o in range(co):
                    row = (c * co + o) * 2
                    at = (knb + c) * co + o
                    total = p_ref[pl.ds(idxs[at, 0], 2), :]
                    for j in range(1, gnb):
                        total = total + p_ref[pl.ds(idxs[at, j], 2), :]
                    gy[row : row + 2] = total

        def scatter():
            for c in range(ncb):
                for o in range(co):
                    at = (knb + c) * co + o
                    for j in range(gnb):
                        src, dst = idxs[at, gnb + j], idxs[at, 2 * gnb + j]
                        gts[c, pl.ds(dst, 2), :] = q_ref[pl.ds(src, 2), :]

        def coupled(rows):
            total = acc[rows]
            for c in range(ncb):
                total = total + gts[c, rows]
            return total

        chunk = nrow // (tiles // 2)
        even = lax.broadcasted_iota(jnp.int32, (chunk, BLK), 0) % 2 == 0

        def prepare(i):
            start = i * chunk
            rows = slice(start, start + chunk)
            state = part("state", chunk, start)
            cm = part("wrap", chunk, start)
            mass = doubled(cm, True)
            stiff = doubled(part("stiff", chunk, start % (nrow // 2)), start >= nrow // 2)
            wrap = jnp.where(even, cm, is_zero * pltpu.roll(cm, 1, 0))
            d_self = jnp.where(even, a_even, a_odd) * mass + stiff
            d_other = jnp.where(even, a_odd, a_even) * mass + stiff
            cross = jnp.where(even, b_even, -b_even) * mass
            inv = 1.0 / (d_self * d_other + cross * cross)
            e_ref[rows] = d_other * inv
            c_ref[rows] = cross * inv
            rhs[rows] = part("force", chunk, start) + wrap - (d_self * state + cross * swapped(state))

        def advance(first):
            for i in range(nrow // chunk):
                rows = slice(i * chunk, i * chunk + chunk)
                res = rhs[rows] - coupled(rows)
                if first:
                    rhs[rows] = res
                value = e_ref[rows] * res - c_ref[rows] * swapped(res)
                xs[rows] = value
                xt[rows, :BLK], xt[rows, BLK:], xl[rows] = split3(value)

        mult = part("mult", crow)
        shalf = part("stab", crow // 2)
        stab = jnp.concatenate([doubled(shalf, False), doubled(shalf, True)], axis=0)
        istab[...] = 1.0 / stab
        products(*split3(part("state", nrow)), (w1, w2), p_ref, lambda i: None)
        copy.wait()

        def both(i):
            prepare(i)
            couple(i)

        products(*split3(mult), (v1, v2), q_ref, both)
        constrain()
        scatter()
        sc[...] = stab * mult - gy[...]
        advance(True)

        def sweep(_, carry):
            products(xt[:, :BLK], xt[:, BLK:], xl[...], (w1, w2), p_ref, lambda i: None)
            constrain()
            products(*split3((gy[...] - sc[...]) * istab[...]), (v1, v2), q_ref, couple)
            scatter()
            advance(False)
            return carry

        lax.fori_loop(0, SWEEPS - 1, sweep, 0)
        own = own_ref[0]
        parts = out_ref.shape[0] // (2 * nb)
        for b in range(nb):
            value = xs[pl.ds((b * co + own) * 2, 2), :]
            for z in range(parts):
                row = (b * parts + z) * 2
                out_ref[row : row + 2] = value

    return kernel, [
        pltpu.VMEM((prow + 8, BLK), F32),
        pltpu.VMEM((tiles * crow, BLK), F32),
        pltpu.VMEM((nrow, BLK), F32),
        pltpu.VMEM((ncb, nrow, BLK), F32),
        pltpu.VMEM((nrow, BLK), F32),
        pltpu.VMEM((nrow, BLK), F32),
        pltpu.VMEM((nrow, BLK), F32),
        pltpu.VMEM((nrow, BLK), F32),
        pltpu.VMEM((nrow, 2 * BLK), BF16),
        pltpu.VMEM((nrow, BLK), BF16),
        pltpu.VMEM((crow, BLK), F32),
        pltpu.VMEM((crow, BLK), F32),
        pltpu.VMEM((crow, BLK), F32),
        pltpu.VMEM((nidx, BLK), jnp.int32),
        pltpu.VMEM((-(-nidx // 16) * 8, BLK), jnp.int32),
        pltpu.SMEM((-(-nidx // 16) * 8, BLK), jnp.int32),
        pltpu.SemaphoreType.DMA(()),
    ]


VM = pl.BlockSpec(memory_space=pltpu.VMEM)
SM = pl.BlockSpec(memory_space=pltpu.SMEM)


def layout(nb, ncb):
    state, force, mult = 0, nb, 2 * nb
    wrap = mult + ncb
    stiff = wrap + nb
    stab = stiff + nb // 2
    idx = stab + ncb // 2
    return {"state": state, "force": force, "mult": mult, "wrap": wrap, "stiff": stiff, "stab": stab, "idx": idx}


def solve_call(fac, own, recv, mats, nb, ncb, co, tiles, knb, gnb, lay, parts):
    kernel, scratch = make_solve(nb, ncb, co, tiles, knb, gnb, lay)
    return pl.pallas_call(
        kernel,
        out_shape=jax.ShapeDtypeStruct((2 * nb * parts, BLK), F32),
        in_specs=[SM, SM] + [VM] * 5,
        out_specs=VM,
        scratch_shapes=scratch,
        name="solve",
    )(fac, own, recv, *mats)


def bank_call(bank):
    shape = jax.ShapeDtypeStruct(bank.shape, BF16)
    return pl.pallas_call(
        bank_kernel, out_shape=[shape] * 4, in_specs=[VM], out_specs=[VM] * 4, name="bank"
    )(bank)


def gather_call(state, force, mult, count):
    hbm = pl.BlockSpec(memory_space=pl.ANY)
    return pl.pallas_call(
        gather_kernel,
        out_shape=jax.ShapeDtypeStruct((count, 2, BLK), F32),
        in_specs=[hbm] * 3,
        out_specs=hbm,
        scratch_shapes=[pltpu.VMEM(v.shape, F32) for v in (state, force, mult)]
        + [pltpu.SemaphoreType.DMA((3,)), pltpu.SemaphoreType.DMA((8,))],
        name="gather",
    )(state, force, mult)


def extra_call(at, initial, mass, stiff, stab, offs, ktiles, cols, gtiles, rows):
    return pl.pallas_call(
        extra_kernel,
        out_shape=jax.ShapeDtypeStruct((2, BLK), F32),
        in_specs=[SM] + [VM] * 8,
        out_specs=VM,
        scratch_shapes=[pltpu.VMEM((rows, BLK), F32)],
        name="extra",
    )(at, initial, mass, stiff, stab, offs, ktiles, cols, gtiles)


def finish_call(cols, tiles, state, mult, stab, update, w1, w2):
    return pl.pallas_call(
        finish_kernel,
        out_shape=[
            jax.ShapeDtypeStruct(state.shape, F32),
            jax.ShapeDtypeStruct(mult.shape, F32),
        ],
        in_specs=[SM, SM] + [VM] * 6,
        out_specs=[VM, VM],
        name="finish",
    )(cols, tiles, state, mult, stab, update, w1, w2)


def make_local(forward, inverse, factors, low):
    steps = forward.shape[0]
    group = ("high", "low")

    def blocks(value):
        return value.reshape(value.shape[0], -1, BLK).transpose(1, 0, 2)

    def local(
        state, multiplier, force, initial, mass, stiff_diag, stab,
        bank, k_offsets, k_tiles, g_cols, g_tiles,
    ):
        nb = state.shape[1] // BLK
        ncb = multiplier.shape[1] // BLK
        tiles = bank.shape[0]
        tm = lax.axis_size(group)
        co = lax.axis_size("coord")
        high = tm // low
        t = lax.axis_index(group)
        o = lax.axis_index("coord")
        lay = layout(nb, ncb)
        sent = gather_call(blocks(state), blocks(force), blocks(multiplier), tm)
        columns = lax.all_to_all(sent, group, split_axis=0, concat_axis=0, tiled=True)
        columns = columns.reshape(steps, BLK)
        at = t - lay["wrap"]
        count = 2 * (tm - lay["wrap"])
        extra = extra_call(
            jnp.clip(2 * at, 0, count - 2).reshape(1),
            initial.reshape(nb, BLK),
            mass.reshape(nb, BLK),
            stiff_diag.reshape(nb, BLK),
            stab.reshape(ncb, BLK),
            k_offsets.T,
            k_tiles.T,
            g_cols,
            g_tiles,
            -(-count // 8) * 8,
        )
        is_wrap = (at >= 0) & (at < nb)
        wrap = jnp.where(is_wrap, extra[1] * (extra[0] - ALPHA * columns[-1]), extra[0])
        extra = jnp.stack([wrap, extra[1]])
        spectrum = jnp.dot(forward, columns, precision=HIGHEST).reshape(tm, 2, BLK)
        spectrum = jnp.where(at < 0, spectrum, extra[None])
        spread = jnp.broadcast_to(spectrum[:, None], (tm, co, 2, BLK)).reshape(tm * co, 2, BLK)
        recv = lax.all_to_all(
            spread, group + ("coord",), split_axis=0, concat_axis=0, tiled=True
        ).reshape(tm * co * 2, BLK)

        mats = bank_call(bank)
        recv = pltpu.with_memory_space_constraint(recv, pltpu.VMEM)
        fac = lax.dynamic_index_in_dim(jnp.asarray(factors), t, 0, keepdims=False)
        solved = solve_call(
            fac, o.reshape(1).astype(jnp.int32), recv, mats,
            nb, ncb, co, tiles, k_tiles.shape[1], g_tiles.shape[1], lay, low,
        )
        slots = lax.all_to_all(
            solved.reshape(tm, 2, BLK), group, split_axis=0, concat_axis=0, tiled=True
        ).reshape(steps, BLK)
        table = lax.dynamic_slice_in_dim(
            jnp.asarray(inverse), lax.axis_index("low") * (2 * high), 2 * high, axis=0
        )
        table = lax.optimization_barrier(table)
        kept = (
            blocks(state).reshape(2 * nb, BLK),
            blocks(multiplier).reshape(2 * ncb, BLK),
            stab.reshape(ncb, BLK),
        )
        kept = [pltpu.with_memory_space_constraint(v, pltpu.VMEM) for v in kept]
        rows, *kept = lax.optimization_barrier(
            (jnp.dot(table, slots, precision=HIGHEST), *kept)
        )
        rows = lax.all_to_all(
            rows.reshape(high, 2, BLK), "high", split_axis=0, concat_axis=0, tiled=True
        ).reshape(2 * nb, BLK)
        new_state, new_mult = finish_call(
            g_cols,
            g_tiles,
            *kept,
            pltpu.with_memory_space_constraint(rows, pltpu.VMEM),
            *[pltpu.with_memory_space_constraint(m, pltpu.VMEM) for m in mats[:2]],
        )

        def lines(value):
            return value.reshape(-1, 2, BLK).transpose(1, 0, 2).reshape(2, -1)

        return lines(new_state), lines(new_mult)

    return local


def solution(mesh):
    tm, co = mesh.shape["tm"], mesh.shape["coord"]
    low = 4
    split = Mesh(mesh.devices.reshape(tm // low, low, co), ("high", "low", "coord"))
    forward, inverse, factors = tables(2 * tm, low)
    time = ("high", "low")
    return jax.shard_map(
        make_local(forward, inverse, factors, low),
        mesh=split,
        in_specs=(
            P(time, "coord"),
            P(time, "coord"),
            P(time, "coord"),
            P("coord"),
            P("coord"),
            P("coord"),
            P("coord"),
            P(),
            P("coord", None),
            P("coord", None),
            P("coord", None),
            P("coord", None),
        ),
        out_specs=(P(time, "coord"), P(time, "coord")),
        check_vma=False,
    )
```

```python
import math

import jax
import jax.numpy as jnp
import numpy as np
from jax import lax
from jax.experimental import pallas as pl
from jax.experimental.pallas import tpu as pltpu
from jax.sharding import Mesh, PartitionSpec as P

BLK = 128
REACH = 2
SWEEPS = 8
FULL = 3
ALPHA = 0.001
HIGHEST = lax.Precision.HIGHEST
F32 = jnp.float32
BF16 = jnp.bfloat16


def tables(steps, low):
    ids = np.arange(steps)
    frequency = np.where(ids == 1, steps // 2, ids // 2)
    angles = 2.0 * np.pi / steps * ((frequency[:, None] * ids[None, :]) % steps)
    is_sine = (ids % 2 == 1) & (ids > 1)
    wave = np.where(is_sine[:, None], -np.sin(angles), np.cos(angles))
    scale = np.exp(math.log(ALPHA) * ids / steps)
    forward = wave * scale[None, :]
    weights = np.where(ids < 2, 1.0, 2.0) / steps
    inverse = (wave * weights[:, None]).T / scale[:, None]
    inverse = inverse.reshape(steps // (2 * low), low, 2, steps).swapaxes(0, 1).reshape(steps, steps)
    beta = math.exp(math.log(ALPHA) / steps)
    pair = np.arange(steps // 2)
    theta = 2.0 * np.pi * pair / steps
    zero = pair == 0
    a_even = np.where(zero, 1.0 - beta, 1.0 - beta * np.cos(theta))
    a_odd = np.where(zero, 1.0 + beta, 1.0 - beta * np.cos(theta))
    b_even = np.where(zero, 0.0, -beta * np.sin(theta))
    factors = np.stack([a_even, a_odd, b_even, zero.astype(np.float64)], axis=1)
    return forward.astype(np.float32), inverse.astype(np.float32), factors.astype(np.float32)


def split3(value):
    high = value.astype(BF16)
    rest = value - high.astype(F32)
    mid = rest.astype(BF16)
    return high, mid, (rest - mid.astype(F32)).astype(BF16)


def bank_kernel(bank_ref, w1, w2, v1, v2):
    for tile in range(bank_ref.shape[0]):
        value = bank_ref[tile]
        for mat, outs in ((value, (w1, w2)), (value.T, (v1, v2))):
            for out, piece in zip(outs, split3(mat)):
                out[tile] = piece


def gather_kernel(state, force, mult, out, sbuf, fbuf, mbuf, sin, sout):
    ns, nm = sbuf.shape[0], mbuf.shape[0]
    pairs = [(state, sbuf), (force, fbuf), (mult, mbuf)]
    loads = [pltpu.make_async_copy(a, b, sin.at[i]) for i, (a, b) in enumerate(pairs)]
    for load in loads:
        load.start()
    targets = [(sbuf, 0, ns), (fbuf, ns, ns), (mbuf, 2 * ns, nm), (sbuf, 2 * ns + nm, ns)]
    end = 3 * ns + nm
    while end < out.shape[0]:
        count = min(ns, out.shape[0] - end)
        targets.append((fbuf, end, count))
        end += count
    stores = []
    for load, (_, buf) in zip(loads, pairs):
        load.wait()
        for src, start, count in targets:
            if src is buf:
                stores.append(
                    pltpu.make_async_copy(
                        buf.at[pl.ds(0, count)], out.at[pl.ds(start, count)], sout.at[len(stores)]
                    )
                )
                stores[-1].start()
    for store in stores:
        store.wait()


def extra_kernel(at_ref, initial, mass, stiff, stab, offs, ktiles, cols, gtiles, out, buf):
    nb, ncb = mass.shape[0], stab.shape[0]
    buf[...] = jnp.zeros(buf.shape, F32)
    start = 0
    for first, second in (
        (initial[...], mass[...]),
        (stiff[: nb // 2], stiff[nb // 2 :]),
        (stab[: ncb // 2], stab[ncb // 2 :]),
        (offs[...].astype(F32), ktiles[...].astype(F32)),
        (cols[...].astype(F32), gtiles[...].astype(F32)),
    ):
        count, width = first.shape
        buf[pl.ds(start, count, stride=2), :width] = first
        buf[pl.ds(start + 1, count, stride=2), :width] = second
        start += 2 * count
    out[...] = buf[pl.ds(at_ref[0], 2), :]


def finish_kernel(cols_ref, tiles_ref, state, mult, stab, update, w1, w2, new_state, new_mult):
    ncb, gnb = cols_ref.shape
    new_state[...] = state[...] + update[...]
    owner = lax.broadcasted_iota(jnp.int32, mult.shape, 0) // 2
    total = jnp.zeros(mult.shape, F32)
    for j in range(gnb):
        value = jnp.concatenate(
            [new_state[pl.ds(cols_ref[c, j] * 2, 2), :] for c in range(ncb)], axis=0
        )
        high, mid, _ = split3(value)
        two = jnp.concatenate([high, mid], axis=1)
        for c in range(ncb):
            b1, b2 = w1[tiles_ref[c, j]], w2[tiles_ref[c, j]]
            res = jnp.dot(two, jnp.concatenate([b1, b1]), preferred_element_type=F32)
            res += jnp.dot(two, jnp.concatenate([b2, b2]), preferred_element_type=F32)
            total += jnp.where(owner == c, res, 0.0)
    weight = jnp.zeros(mult.shape, F32)
    for c in range(ncb):
        weight = jnp.where(owner == c, stab[c : c + 1], weight)
    new_mult[...] = mult[...] + (total - weight * mult[...]) / weight


def swapped(value):
    rows = value.shape[0]
    even = lax.broadcasted_iota(jnp.int32, value.shape, 0) % 2 == 0
    return jnp.where(even, pltpu.roll(value, rows - 1, 0), pltpu.roll(value, 1, 0))


def doubled(value, odd):
    rows = value.shape[0]
    even = lax.broadcasted_iota(jnp.int32, value.shape, 0) % 2 == 0
    if odd:
        return jnp.where(even, pltpu.roll(value, rows - 1, 0), value)
    return jnp.where(even, value, pltpu.roll(value, 1, 0))


def make_solve(nb, ncb, co, tiles, knb, gnb, lay):
    nrow = 2 * nb * co
    crow = 2 * ncb * co
    prow = tiles * nrow
    nidx = 2 * co * (knb + ncb)

    def kernel(
        fac_ref, own_ref, r_ref, w1_hbm, w2_hbm, v1_hbm, v2_hbm, out_ref,
        p_ref, q_ref, acc, gts, xs, rhs, e_ref, c_ref, xt, xl, gy, sc, istab, wide, idxv, idxs, sem,
        w1, w2, v1, v2, sems,
    ):
        a_even, a_odd, b_even, is_zero = fac_ref[0], fac_ref[1], fac_ref[2], fac_ref[3]

        def part(name, rows, start=0):
            start += lay[name] * 2 * co
            return r_ref[start : start + rows]

        loads = [
            pltpu.make_async_copy(src, dst, sems.at[i])
            for i, (src, dst) in enumerate(
                ((w1_hbm, w1), (w2_hbm, w2), (v1_hbm, v1), (v2_hbm, v2))
            )
        ]
        for load in loads:
            load.start()
        raw = part("idx", nidx).astype(jnp.int32)
        lane = lax.broadcasted_iota(jnp.int32, raw.shape, 1)
        line = lax.broadcasted_iota(jnp.int32, raw.shape, 0)
        coord = (line >> 1) & (co - 1)
        column, tile = raw, pltpu.roll(raw, nidx - 1, 0)
        block = coord * nb + lane + column - REACH
        inside = (block >= 0) & (block < nb * co)
        k_row = ((block & (nb - 1)) * co + (block >> (nb.bit_length() - 1))) * 2
        k_row = jnp.where(inside, tile * nrow + k_row, prow)
        g_row = (column * co + coord) * 2
        q_row = tile * crow + line - 2 * knb * co
        q_row = pltpu.roll(q_row, gnb, 1)
        g_rows = jnp.where(lane < gnb, tile * nrow + g_row, pltpu.roll(g_row, 2 * gnb, 1))
        g_rows = jnp.where((lane >= gnb) & (lane < 2 * gnb), q_row, g_rows)
        wide[...] = jnp.where(line < 2 * knb * co, k_row, g_rows)
        idxv[...] = jnp.zeros(idxv.shape, jnp.int32)
        idxv[: nidx // 2] = wide[pl.ds(0, nidx // 2, stride=2), :]
        copy = pltpu.make_async_copy(idxv, idxs, sem)
        copy.start()
        p_ref[prow : prow + 8] = jnp.zeros((8, BLK), F32)
        gts[...] = jnp.zeros(gts.shape, F32)

        def products(x1, x2, x3, mats, dst, beside):
            rows = x1.shape[0]
            pairs = [(x1, x1), (x2, x2)]
            if x3 is not None:
                pairs.append((x3, jnp.zeros_like(x3)))
            stack = jnp.concatenate([jnp.concatenate(p, axis=1) for p in pairs], axis=0)
            m1, m2 = mats
            for pair in range(tiles // 2):
                b1 = jnp.concatenate([m1[2 * pair], m1[2 * pair + 1]], axis=1)
                b2 = jnp.concatenate([m2[2 * pair], m2[2 * pair + 1]], axis=1)
                res = jnp.dot(stack, jnp.concatenate([b1, b2]), preferred_element_type=F32)
                low = res[rows : 2 * rows]
                if x3 is not None:
                    low = low + res[2 * rows :]
                res = res[:rows] + low
                for side in range(2):
                    start = (2 * pair + side) * rows
                    dst[start : start + rows] = res[:, side * BLK : side * BLK + BLK]
                beside(pair)

        def couple(i):
            count = nb // (tiles // 2)
            for b in range(i * count, (i + 1) * count):
                for o in range(co):
                    row = (b * co + o) * 2
                    total = p_ref[pl.ds(idxs[o, b], 2), :]
                    for k in range(1, knb):
                        total = total + p_ref[pl.ds(idxs[k * co + o, b], 2), :]
                    acc[row : row + 2] = total

        def constrain():
            for c in range(ncb):
                for o in range(co):
                    row = (c * co + o) * 2
                    at = (knb + c) * co + o
                    total = p_ref[pl.ds(idxs[at, 0], 2), :]
                    for j in range(1, gnb):
                        total = total + p_ref[pl.ds(idxs[at, j], 2), :]
                    gy[row : row + 2] = total

        def scatter():
            for c in range(ncb):
                for o in range(co):
                    at = (knb + c) * co + o
                    for j in range(gnb):
                        src, dst = idxs[at, gnb + j], idxs[at, 2 * gnb + j]
                        gts[c, pl.ds(dst, 2), :] = q_ref[pl.ds(src, 2), :]

        def coupled(rows):
            total = acc[rows]
            for c in range(ncb):
                total = total + gts[c, rows]
            return total

        chunk = nrow // (tiles // 2)
        even = lax.broadcasted_iota(jnp.int32, (chunk, BLK), 0) % 2 == 0

        def prepare(i):
            start = i * chunk
            rows = slice(start, start + chunk)
            state = part("state", chunk, start)
            cm = part("wrap", chunk, start)
            mass = doubled(cm, True)
            stiff = doubled(part("stiff", chunk, start % (nrow // 2)), start >= nrow // 2)
            wrap = jnp.where(even, cm, is_zero * pltpu.roll(cm, 1, 0))
            d_self = jnp.where(even, a_even, a_odd) * mass + stiff
            d_other = jnp.where(even, a_odd, a_even) * mass + stiff
            cross = jnp.where(even, b_even, -b_even) * mass
            inv = 1.0 / (d_self * d_other + cross * cross)
            e_ref[rows] = d_other * inv
            c_ref[rows] = cross * inv
            rhs[rows] = part("force", chunk, start) + wrap - (d_self * state + cross * swapped(state))

        def advance(first):
            for i in range(nrow // chunk):
                rows = slice(i * chunk, i * chunk + chunk)
                res = rhs[rows] - coupled(rows)
                if first:
                    rhs[rows] = res
                value = e_ref[rows] * res - c_ref[rows] * swapped(res)
                xs[rows] = value
                xt[rows, :BLK], xt[rows, BLK:], xl[rows] = split3(value)

        mult = part("mult", crow)
        shalf = part("stab", crow // 2)
        stab = jnp.concatenate([doubled(shalf, False), doubled(shalf, True)], axis=0)
        istab[...] = 1.0 / stab
        for i in range(nrow // chunk):
            prepare(i)
        for load in loads[:2]:
            load.wait()
        products(*split3(part("state", nrow)), (w1, w2), p_ref, lambda i: None)
        copy.wait()
        for load in loads[2:]:
            load.wait()
        products(*split3(mult), (v1, v2), q_ref, couple)
        constrain()
        scatter()
        sc[...] = stab * mult - gy[...]
        advance(True)

        def sweep(low):
            x3 = xl[...] if low else None
            products(xt[:, :BLK], xt[:, BLK:], x3, (w1, w2), p_ref, lambda i: None)
            constrain()
            products(*split3((gy[...] - sc[...]) * istab[...]), (v1, v2), q_ref, couple)
            scatter()
            advance(False)

        def loop(count, low):
            lax.fori_loop(0, count, lambda i, carry: (sweep(low), carry)[1], 0)

        loop(SWEEPS - 1 - FULL, False)
        loop(FULL, True)
        own = own_ref[0]
        parts = out_ref.shape[0] // (2 * nb)
        for b in range(nb):
            value = xs[pl.ds((b * co + own) * 2, 2), :]
            for z in range(parts):
                row = (b * parts + z) * 2
                out_ref[row : row + 2] = value

    return kernel, [
        pltpu.VMEM((prow + 8, BLK), F32),
        pltpu.VMEM((tiles * crow, BLK), F32),
        pltpu.VMEM((nrow, BLK), F32),
        pltpu.VMEM((ncb, nrow, BLK), F32),
        pltpu.VMEM((nrow, BLK), F32),
        pltpu.VMEM((nrow, BLK), F32),
        pltpu.VMEM((nrow, BLK), F32),
        pltpu.VMEM((nrow, BLK), F32),
        pltpu.VMEM((nrow, 2 * BLK), BF16),
        pltpu.VMEM((nrow, BLK), BF16),
        pltpu.VMEM((crow, BLK), F32),
        pltpu.VMEM((crow, BLK), F32),
        pltpu.VMEM((crow, BLK), F32),
        pltpu.VMEM((nidx, BLK), jnp.int32),
        pltpu.VMEM((-(-nidx // 16) * 8, BLK), jnp.int32),
        pltpu.SMEM((-(-nidx // 16) * 8, BLK), jnp.int32),
        pltpu.SemaphoreType.DMA(()),
        pltpu.VMEM((tiles, BLK, BLK), BF16),
        pltpu.VMEM((tiles, BLK, BLK), BF16),
        pltpu.VMEM((tiles, BLK, BLK), BF16),
        pltpu.VMEM((tiles, BLK, BLK), BF16),
        pltpu.SemaphoreType.DMA((4,)),
    ]


VM = pl.BlockSpec(memory_space=pltpu.VMEM)
SM = pl.BlockSpec(memory_space=pltpu.SMEM)


def layout(nb, ncb):
    state, force, mult = 0, nb, 2 * nb
    wrap = mult + ncb
    stiff = wrap + nb
    stab = stiff + nb // 2
    idx = stab + ncb // 2
    return {"state": state, "force": force, "mult": mult, "wrap": wrap, "stiff": stiff, "stab": stab, "idx": idx}


def solve_call(fac, own, recv, mats, nb, ncb, co, tiles, knb, gnb, lay, parts):
    kernel, scratch = make_solve(nb, ncb, co, tiles, knb, gnb, lay)
    return pl.pallas_call(
        kernel,
        out_shape=jax.ShapeDtypeStruct((2 * nb * parts, BLK), F32),
        in_specs=[SM, SM, VM] + [pl.BlockSpec(memory_space=pl.ANY)] * 4,
        out_specs=VM,
        scratch_shapes=scratch,
        name="solve",
    )(fac, own, recv, *mats)


def bank_call(bank):
    shape = jax.ShapeDtypeStruct(bank.shape, BF16)
    return pl.pallas_call(
        bank_kernel, out_shape=[shape] * 4, in_specs=[VM], out_specs=[VM] * 4, name="bank"
    )(bank)


def gather_call(state, force, mult, count):
    hbm = pl.BlockSpec(memory_space=pl.ANY)
    return pl.pallas_call(
        gather_kernel,
        out_shape=jax.ShapeDtypeStruct((count, 2, BLK), F32),
        in_specs=[hbm] * 3,
        out_specs=hbm,
        scratch_shapes=[pltpu.VMEM(v.shape, F32) for v in (state, force, mult)]
        + [pltpu.SemaphoreType.DMA((3,)), pltpu.SemaphoreType.DMA((8,))],
        name="gather",
    )(state, force, mult)


def extra_call(at, initial, mass, stiff, stab, offs, ktiles, cols, gtiles, rows):
    return pl.pallas_call(
        extra_kernel,
        out_shape=jax.ShapeDtypeStruct((2, BLK), F32),
        in_specs=[SM] + [VM] * 8,
        out_specs=VM,
        scratch_shapes=[pltpu.VMEM((rows, BLK), F32)],
        name="extra",
    )(at, initial, mass, stiff, stab, offs, ktiles, cols, gtiles)


def finish_call(cols, tiles, state, mult, stab, update, w1, w2):
    return pl.pallas_call(
        finish_kernel,
        out_shape=[
            jax.ShapeDtypeStruct(state.shape, F32),
            jax.ShapeDtypeStruct(mult.shape, F32),
        ],
        in_specs=[SM, SM] + [VM] * 6,
        out_specs=[VM, VM],
        name="finish",
    )(cols, tiles, state, mult, stab, update, w1, w2)


def make_local(forward, inverse, factors, low):
    steps = forward.shape[0]
    group = ("high", "low")

    def blocks(value):
        return value.reshape(value.shape[0], -1, BLK).transpose(1, 0, 2)

    def local(
        state, multiplier, force, initial, mass, stiff_diag, stab,
        bank, k_offsets, k_tiles, g_cols, g_tiles,
    ):
        nb = state.shape[1] // BLK
        ncb = multiplier.shape[1] // BLK
        tiles = bank.shape[0]
        tm = lax.axis_size(group)
        co = lax.axis_size("coord")
        high = tm // low
        t = lax.axis_index(group)
        o = lax.axis_index("coord")
        lay = layout(nb, ncb)
        sent = gather_call(blocks(state), blocks(force), blocks(multiplier), tm)
        columns = lax.all_to_all(sent, group, split_axis=0, concat_axis=0, tiled=True)
        columns = columns.reshape(steps, BLK)
        at = t - lay["wrap"]
        count = 2 * (tm - lay["wrap"])
        extra = extra_call(
            jnp.clip(2 * at, 0, count - 2).reshape(1),
            initial.reshape(nb, BLK),
            mass.reshape(nb, BLK),
            stiff_diag.reshape(nb, BLK),
            stab.reshape(ncb, BLK),
            k_offsets.T,
            k_tiles.T,
            g_cols,
            g_tiles,
            -(-count // 8) * 8,
        )
        is_wrap = (at >= 0) & (at < nb)
        wrap = jnp.where(is_wrap, extra[1] * (extra[0] - ALPHA * columns[-1]), extra[0])
        extra = jnp.stack([wrap, extra[1]])
        spectrum = jnp.dot(forward, columns, precision=HIGHEST).reshape(tm, 2, BLK)
        spectrum = jnp.where(at < 0, spectrum, extra[None])
        spread = jnp.broadcast_to(spectrum[:, None], (tm, co, 2, BLK)).reshape(tm * co, 2, BLK)
        recv = lax.all_to_all(
            spread, group + ("coord",), split_axis=0, concat_axis=0, tiled=True
        ).reshape(tm * co * 2, BLK)

        mats = bank_call(bank)
        recv = pltpu.with_memory_space_constraint(recv, pltpu.VMEM)
        fac = lax.dynamic_index_in_dim(jnp.asarray(factors), t, 0, keepdims=False)
        solved = solve_call(
            fac, o.reshape(1).astype(jnp.int32), recv, mats,
            nb, ncb, co, tiles, k_tiles.shape[1], g_tiles.shape[1], lay, low,
        )
        slots = lax.all_to_all(
            solved.reshape(tm, 2, BLK), group, split_axis=0, concat_axis=0, tiled=True
        ).reshape(steps, BLK)
        table = lax.dynamic_slice_in_dim(
            jnp.asarray(inverse), lax.axis_index("low") * (2 * high), 2 * high, axis=0
        )
        table = lax.optimization_barrier(table)
        kept = (
            blocks(state).reshape(2 * nb, BLK),
            blocks(multiplier).reshape(2 * ncb, BLK),
            stab.reshape(ncb, BLK),
        )
        kept = [pltpu.with_memory_space_constraint(v, pltpu.VMEM) for v in kept]
        rows, *kept = lax.optimization_barrier(
            (jnp.dot(table, slots, precision=HIGHEST), *kept)
        )
        rows = lax.all_to_all(
            rows.reshape(high, 2, BLK), "high", split_axis=0, concat_axis=0, tiled=True
        ).reshape(2 * nb, BLK)
        new_state, new_mult = finish_call(
            g_cols,
            g_tiles,
            *kept,
            pltpu.with_memory_space_constraint(rows, pltpu.VMEM),
            *[pltpu.with_memory_space_constraint(m, pltpu.VMEM) for m in mats[:2]],
        )

        def lines(value):
            return value.reshape(-1, 2, BLK).transpose(1, 0, 2).reshape(2, -1)

        return lines(new_state), lines(new_mult)

    return local


def solution(mesh):
    tm, co = mesh.shape["tm"], mesh.shape["coord"]
    low = 4
    split = Mesh(mesh.devices.reshape(tm // low, low, co), ("high", "low", "coord"))
    forward, inverse, factors = tables(2 * tm, low)
    time = ("high", "low")
    return jax.shard_map(
        make_local(forward, inverse, factors, low),
        mesh=split,
        in_specs=(
            P(time, "coord"),
            P(time, "coord"),
            P(time, "coord"),
            P("coord"),
            P("coord"),
            P("coord"),
            P("coord"),
            P(),
            P("coord", None),
            P("coord", None),
            P("coord", None),
            P("coord", None),
        ),
        out_specs=(P(time, "coord"), P(time, "coord")),
        check_vma=False,
    )
```

```python
import math

import jax
import jax.numpy as jnp
import numpy as np
from jax import lax
from jax.experimental import pallas as pl
from jax.experimental.pallas import tpu as pltpu
from jax.sharding import Mesh, PartitionSpec as P

BLK = 128
REACH = 2
SWEEPS = 8
FULL = 3
ALPHA = 0.001
HIGHEST = lax.Precision.HIGHEST
F32 = jnp.float32
BF16 = jnp.bfloat16


def tables(steps, low):
    ids = np.arange(steps)
    frequency = np.where(ids == 1, steps // 2, ids // 2)
    angles = 2.0 * np.pi / steps * ((frequency[:, None] * ids[None, :]) % steps)
    is_sine = (ids % 2 == 1) & (ids > 1)
    wave = np.where(is_sine[:, None], -np.sin(angles), np.cos(angles))
    scale = np.exp(math.log(ALPHA) * ids / steps)
    forward = wave * scale[None, :]
    weights = np.where(ids < 2, 1.0, 2.0) / steps
    inverse = (wave * weights[:, None]).T / scale[:, None]
    inverse = inverse.reshape(steps // (2 * low), low, 2, steps).swapaxes(0, 1).reshape(steps, steps)
    beta = math.exp(math.log(ALPHA) / steps)
    pair = np.arange(steps // 2)
    theta = 2.0 * np.pi * pair / steps
    zero = pair == 0
    a_even = np.where(zero, 1.0 - beta, 1.0 - beta * np.cos(theta))
    a_odd = np.where(zero, 1.0 + beta, 1.0 - beta * np.cos(theta))
    b_even = np.where(zero, 0.0, -beta * np.sin(theta))
    factors = np.stack([a_even, a_odd, b_even, zero.astype(np.float64)], axis=1)
    return forward.astype(np.float32), inverse.astype(np.float32), factors.astype(np.float32)


def split3(value):
    high = value.astype(BF16)
    rest = value - high.astype(F32)
    mid = rest.astype(BF16)
    return high, mid, (rest - mid.astype(F32)).astype(BF16)


def bank_kernel(bank_ref, w1, w2, v1, v2):
    for tile in range(bank_ref.shape[0]):
        value = bank_ref[tile]
        for mat, outs in ((value, (w1, w2)), (value.T, (v1, v2))):
            for out, piece in zip(outs, split3(mat)):
                out[tile] = piece


def gather_kernel(state, force, mult, out, sbuf, fbuf, mbuf, sin, sout):
    ns, nm = sbuf.shape[0], mbuf.shape[0]
    pairs = [(state, sbuf), (force, fbuf), (mult, mbuf)]
    loads = [pltpu.make_async_copy(a, b, sin.at[i]) for i, (a, b) in enumerate(pairs)]
    for load in loads:
        load.start()
    targets = [(sbuf, 0, ns), (fbuf, ns, ns), (mbuf, 2 * ns, nm), (sbuf, 2 * ns + nm, ns)]
    end = 3 * ns + nm
    while end < out.shape[0]:
        count = min(ns, out.shape[0] - end)
        targets.append((fbuf, end, count))
        end += count
    stores = []
    for load, (_, buf) in zip(loads, pairs):
        load.wait()
        for src, start, count in targets:
            if src is buf:
                stores.append(
                    pltpu.make_async_copy(
                        buf.at[pl.ds(0, count)], out.at[pl.ds(start, count)], sout.at[len(stores)]
                    )
                )
                stores[-1].start()
    for store in stores:
        store.wait()


def extra_kernel(at_ref, initial, mass, stiff, stab, offs, ktiles, cols, gtiles, out, buf):
    nb, ncb = mass.shape[0], stab.shape[0]
    buf[...] = jnp.zeros(buf.shape, F32)
    start = 0
    for first, second in (
        (initial[...], mass[...]),
        (stiff[: nb // 2], stiff[nb // 2 :]),
        (stab[: ncb // 2], stab[ncb // 2 :]),
        (offs[...].astype(F32), ktiles[...].astype(F32)),
        (cols[...].astype(F32), gtiles[...].astype(F32)),
    ):
        count, width = first.shape
        buf[pl.ds(start, count, stride=2), :width] = first
        buf[pl.ds(start + 1, count, stride=2), :width] = second
        start += 2 * count
    out[...] = buf[pl.ds(at_ref[0], 2), :]


def finish_kernel(cols_ref, tiles_ref, state, mult, stab, update, w1, w2, new_state, new_mult):
    ncb, gnb = cols_ref.shape
    new_state[...] = state[...] + update[...]
    owner = lax.broadcasted_iota(jnp.int32, mult.shape, 0) // 2
    total = jnp.zeros(mult.shape, F32)
    for j in range(gnb):
        value = jnp.concatenate(
            [new_state[pl.ds(cols_ref[c, j] * 2, 2), :] for c in range(ncb)], axis=0
        )
        high, mid, _ = split3(value)
        stack = jnp.concatenate([high, mid], axis=0)
        stack = jnp.concatenate([stack, stack], axis=1)
        for c in range(ncb):
            both = jnp.concatenate([w1[tiles_ref[c, j]], w2[tiles_ref[c, j]]])
            res = jnp.dot(stack, both, preferred_element_type=F32)
            total += jnp.where(owner == c, res[: 2 * ncb] + res[2 * ncb :], 0.0)
    weight = jnp.zeros(mult.shape, F32)
    for c in range(ncb):
        weight = jnp.where(owner == c, stab[c : c + 1], weight)
    new_mult[...] = mult[...] + (total - weight * mult[...]) / weight


def swapped(value):
    rows = value.shape[0]
    even = lax.broadcasted_iota(jnp.int32, value.shape, 0) % 2 == 0
    return jnp.where(even, pltpu.roll(value, rows - 1, 0), pltpu.roll(value, 1, 0))


def doubled(value, odd):
    rows = value.shape[0]
    even = lax.broadcasted_iota(jnp.int32, value.shape, 0) % 2 == 0
    if odd:
        return jnp.where(even, pltpu.roll(value, rows - 1, 0), value)
    return jnp.where(even, value, pltpu.roll(value, 1, 0))


def make_solve(nb, ncb, co, tiles, knb, gnb, lay):
    nrow = 2 * nb * co
    crow = 2 * ncb * co
    prow = tiles * nrow
    nidx = 2 * co * (knb + ncb)

    def kernel(
        fac_ref, own_ref, r_ref, w1_hbm, w2_hbm, v1_hbm, v2_hbm, out_ref,
        p_ref, q_ref, acc, gts, xs, rhs, e_ref, c_ref, xt, xl, gy, sc, istab, wide, idxv, idxs, sem,
        w1, w2, v1, v2, sems,
    ):
        a_even, a_odd, b_even, is_zero = fac_ref[0], fac_ref[1], fac_ref[2], fac_ref[3]

        def part(name, rows, start=0):
            start += lay[name] * 2 * co
            return r_ref[start : start + rows]

        loads = [
            pltpu.make_async_copy(src, dst, sems.at[i])
            for i, (src, dst) in enumerate(
                ((w1_hbm, w1), (w2_hbm, w2), (v1_hbm, v1), (v2_hbm, v2))
            )
        ]
        for load in loads:
            load.start()
        raw = part("idx", nidx).astype(jnp.int32)
        lane = lax.broadcasted_iota(jnp.int32, raw.shape, 1)
        line = lax.broadcasted_iota(jnp.int32, raw.shape, 0)
        coord = (line >> 1) & (co - 1)
        column, tile = raw, pltpu.roll(raw, nidx - 1, 0)
        block = coord * nb + lane + column - REACH
        inside = (block >= 0) & (block < nb * co)
        k_row = ((block & (nb - 1)) * co + (block >> (nb.bit_length() - 1))) * 2
        k_row = jnp.where(inside, tile * nrow + k_row, prow)
        g_row = (column * co + coord) * 2
        q_row = tile * crow + line - 2 * knb * co
        q_row = pltpu.roll(q_row, gnb, 1)
        g_rows = jnp.where(lane < gnb, tile * nrow + g_row, pltpu.roll(g_row, 2 * gnb, 1))
        g_rows = jnp.where((lane >= gnb) & (lane < 2 * gnb), q_row, g_rows)
        wide[...] = jnp.where(line < 2 * knb * co, k_row, g_rows)
        idxv[...] = jnp.zeros(idxv.shape, jnp.int32)
        idxv[: nidx // 2] = wide[pl.ds(0, nidx // 2, stride=2), :]
        copy = pltpu.make_async_copy(idxv, idxs, sem)
        copy.start()
        p_ref[prow : prow + 8] = jnp.zeros((8, BLK), F32)
        gts[...] = jnp.zeros(gts.shape, F32)

        def products(x1, x2, x3, mats, dst, beside):
            rows = x1.shape[0]
            pairs = [(x1, x1), (x2, x2)]
            if x3 is not None:
                pairs.append((x3, jnp.zeros_like(x3)))
            stack = jnp.concatenate([jnp.concatenate(p, axis=1) for p in pairs], axis=0)
            m1, m2 = mats
            for pair in range(tiles // 2):
                b1 = jnp.concatenate([m1[2 * pair], m1[2 * pair + 1]], axis=1)
                b2 = jnp.concatenate([m2[2 * pair], m2[2 * pair + 1]], axis=1)
                res = jnp.dot(stack, jnp.concatenate([b1, b2]), preferred_element_type=F32)
                low = res[rows : 2 * rows]
                if x3 is not None:
                    low = low + res[2 * rows :]
                res = res[:rows] + low
                for side in range(2):
                    start = (2 * pair + side) * rows
                    dst[start : start + rows] = res[:, side * BLK : side * BLK + BLK]
                beside(pair)

        def couple(i):
            count = nb // (tiles // 2)
            for b in range(i * count, (i + 1) * count):
                for o in range(co):
                    row = (b * co + o) * 2
                    total = p_ref[pl.ds(idxs[o, b], 2), :]
                    for k in range(1, knb):
                        total = total + p_ref[pl.ds(idxs[k * co + o, b], 2), :]
                    acc[row : row + 2] = total

        def constrain():
            for c in range(ncb):
                for o in range(co):
                    row = (c * co + o) * 2
                    at = (knb + c) * co + o
                    total = p_ref[pl.ds(idxs[at, 0], 2), :]
                    for j in range(1, gnb):
                        total = total + p_ref[pl.ds(idxs[at, j], 2), :]
                    gy[row : row + 2] = total

        def scatter():
            for c in range(ncb):
                for o in range(co):
                    at = (knb + c) * co + o
                    for j in range(gnb):
                        src, dst = idxs[at, gnb + j], idxs[at, 2 * gnb + j]
                        gts[c, pl.ds(dst, 2), :] = q_ref[pl.ds(src, 2), :]

        def coupled(rows):
            total = acc[rows]
            for c in range(ncb):
                total = total + gts[c, rows]
            return total

        chunk = nrow // (tiles // 2)
        even = lax.broadcasted_iota(jnp.int32, (chunk, BLK), 0) % 2 == 0

        def prepare(i):
            start = i * chunk
            rows = slice(start, start + chunk)
            state = part("state", chunk, start)
            cm = part("wrap", chunk, start)
            mass = doubled(cm, True)
            stiff = doubled(part("stiff", chunk, start % (nrow // 2)), start >= nrow // 2)
            wrap = jnp.where(even, cm, is_zero * pltpu.roll(cm, 1, 0))
            d_self = jnp.where(even, a_even, a_odd) * mass + stiff
            d_other = jnp.where(even, a_odd, a_even) * mass + stiff
            cross = jnp.where(even, b_even, -b_even) * mass
            inv = 1.0 / (d_self * d_other + cross * cross)
            e_ref[rows] = d_other * inv
            c_ref[rows] = cross * inv
            rhs[rows] = part("force", chunk, start) + wrap - (d_self * state + cross * swapped(state))

        def advance(first, full):
            for i in range(nrow // chunk):
                rows = slice(i * chunk, i * chunk + chunk)
                res = rhs[rows] - coupled(rows)
                if first:
                    rhs[rows] = res
                value = e_ref[rows] * res - c_ref[rows] * swapped(res)
                xt[rows, :BLK], xt[rows, BLK:], low = split3(value)
                if full:
                    xs[rows] = value
                    xl[rows] = low

        mult = part("mult", crow)
        shalf = part("stab", crow // 2)
        stab = jnp.concatenate([doubled(shalf, False), doubled(shalf, True)], axis=0)
        istab[...] = 1.0 / stab
        for i in range(nrow // chunk):
            prepare(i)
        for load in loads[:2]:
            load.wait()
        products(*split3(part("state", nrow)), (w1, w2), p_ref, lambda i: None)
        copy.wait()
        for load in loads[2:]:
            load.wait()
        products(*split3(mult), (v1, v2), q_ref, couple)
        constrain()
        scatter()
        sc[...] = stab * mult - gy[...]
        advance(True, False)

        def sweep(low, full):
            x3 = xl[...] if low else None
            products(xt[:, :BLK], xt[:, BLK:], x3, (w1, w2), p_ref, lambda i: None)
            constrain()
            products(*split3((gy[...] - sc[...]) * istab[...]), (v1, v2), q_ref, couple)
            scatter()
            advance(False, full)

        def loop(count, low, full):
            lax.fori_loop(0, count, lambda i, carry: (sweep(low, full), carry)[1], 0)

        loop(SWEEPS - 2 - FULL, False, False)
        sweep(False, True)
        loop(FULL, True, True)
        own = own_ref[0]
        parts = out_ref.shape[0] // (2 * nb)
        for b in range(nb):
            value = xs[pl.ds((b * co + own) * 2, 2), :]
            for z in range(parts):
                row = (b * parts + z) * 2
                out_ref[row : row + 2] = value

    return kernel, [
        pltpu.VMEM((prow + 8, BLK), F32),
        pltpu.VMEM((tiles * crow, BLK), F32),
        pltpu.VMEM((nrow, BLK), F32),
        pltpu.VMEM((ncb, nrow, BLK), F32),
        pltpu.VMEM((nrow, BLK), F32),
        pltpu.VMEM((nrow, BLK), F32),
        pltpu.VMEM((nrow, BLK), F32),
        pltpu.VMEM((nrow, BLK), F32),
        pltpu.VMEM((nrow, 2 * BLK), BF16),
        pltpu.VMEM((nrow, BLK), BF16),
        pltpu.VMEM((crow, BLK), F32),
        pltpu.VMEM((crow, BLK), F32),
        pltpu.VMEM((crow, BLK), F32),
        pltpu.VMEM((nidx, BLK), jnp.int32),
        pltpu.VMEM((-(-nidx // 16) * 8, BLK), jnp.int32),
        pltpu.SMEM((-(-nidx // 16) * 8, BLK), jnp.int32),
        pltpu.SemaphoreType.DMA(()),
        pltpu.VMEM((tiles, BLK, BLK), BF16),
        pltpu.VMEM((tiles, BLK, BLK), BF16),
        pltpu.VMEM((tiles, BLK, BLK), BF16),
        pltpu.VMEM((tiles, BLK, BLK), BF16),
        pltpu.SemaphoreType.DMA((4,)),
    ]


VM = pl.BlockSpec(memory_space=pltpu.VMEM)
SM = pl.BlockSpec(memory_space=pltpu.SMEM)


def layout(nb, ncb):
    state, force, mult = 0, nb, 2 * nb
    wrap = mult + ncb
    stiff = wrap + nb
    stab = stiff + nb // 2
    idx = stab + ncb // 2
    return {"state": state, "force": force, "mult": mult, "wrap": wrap, "stiff": stiff, "stab": stab, "idx": idx}


def solve_call(fac, own, recv, mats, nb, ncb, co, tiles, knb, gnb, lay, parts):
    kernel, scratch = make_solve(nb, ncb, co, tiles, knb, gnb, lay)
    return pl.pallas_call(
        kernel,
        out_shape=jax.ShapeDtypeStruct((2 * nb * parts, BLK), F32),
        in_specs=[SM, SM, VM] + [pl.BlockSpec(memory_space=pl.ANY)] * 4,
        out_specs=VM,
        scratch_shapes=scratch,
        name="solve",
    )(fac, own, recv, *mats)


def bank_call(bank):
    shape = jax.ShapeDtypeStruct(bank.shape, BF16)
    return pl.pallas_call(
        bank_kernel, out_shape=[shape] * 4, in_specs=[VM], out_specs=[VM] * 4, name="bank"
    )(bank)


def gather_call(state, force, mult, count):
    hbm = pl.BlockSpec(memory_space=pl.ANY)
    return pl.pallas_call(
        gather_kernel,
        out_shape=jax.ShapeDtypeStruct((count, 2, BLK), F32),
        in_specs=[hbm] * 3,
        out_specs=hbm,
        scratch_shapes=[pltpu.VMEM(v.shape, F32) for v in (state, force, mult)]
        + [pltpu.SemaphoreType.DMA((3,)), pltpu.SemaphoreType.DMA((8,))],
        name="gather",
    )(state, force, mult)


def extra_call(at, initial, mass, stiff, stab, offs, ktiles, cols, gtiles, rows):
    return pl.pallas_call(
        extra_kernel,
        out_shape=jax.ShapeDtypeStruct((2, BLK), F32),
        in_specs=[SM] + [VM] * 8,
        out_specs=VM,
        scratch_shapes=[pltpu.VMEM((rows, BLK), F32)],
        name="extra",
    )(at, initial, mass, stiff, stab, offs, ktiles, cols, gtiles)


def finish_call(cols, tiles, state, mult, stab, update, w1, w2):
    return pl.pallas_call(
        finish_kernel,
        out_shape=[
            jax.ShapeDtypeStruct(state.shape, F32),
            jax.ShapeDtypeStruct(mult.shape, F32),
        ],
        in_specs=[SM, SM] + [VM] * 6,
        out_specs=[VM, VM],
        name="finish",
    )(cols, tiles, state, mult, stab, update, w1, w2)


def make_local(forward, inverse, factors, low):
    steps = forward.shape[0]
    group = ("high", "low")

    def blocks(value):
        return value.reshape(value.shape[0], -1, BLK).transpose(1, 0, 2)

    def local(
        state, multiplier, force, initial, mass, stiff_diag, stab,
        bank, k_offsets, k_tiles, g_cols, g_tiles,
    ):
        nb = state.shape[1] // BLK
        ncb = multiplier.shape[1] // BLK
        tiles = bank.shape[0]
        tm = lax.axis_size(group)
        co = lax.axis_size("coord")
        high = tm // low
        t = lax.axis_index(group)
        o = lax.axis_index("coord")
        lay = layout(nb, ncb)
        sent = gather_call(blocks(state), blocks(force), blocks(multiplier), tm)
        columns = lax.all_to_all(sent, group, split_axis=0, concat_axis=0, tiled=True)
        columns = columns.reshape(steps, BLK)
        at = t - lay["wrap"]
        count = 2 * (tm - lay["wrap"])
        extra = extra_call(
            jnp.clip(2 * at, 0, count - 2).reshape(1),
            initial.reshape(nb, BLK),
            mass.reshape(nb, BLK),
            stiff_diag.reshape(nb, BLK),
            stab.reshape(ncb, BLK),
            k_offsets.T,
            k_tiles.T,
            g_cols,
            g_tiles,
            -(-count // 8) * 8,
        )
        is_wrap = (at >= 0) & (at < nb)
        wrap = jnp.where(is_wrap, extra[1] * (extra[0] - ALPHA * columns[-1]), extra[0])
        extra = jnp.stack([wrap, extra[1]])
        spectrum = jnp.dot(forward, columns, precision=HIGHEST).reshape(tm, 2, BLK)
        spectrum = jnp.where(at < 0, spectrum, extra[None])
        spread = jnp.broadcast_to(spectrum[:, None], (tm, co, 2, BLK)).reshape(tm * co, 2, BLK)
        recv = lax.all_to_all(
            spread, group + ("coord",), split_axis=0, concat_axis=0, tiled=True
        ).reshape(tm * co * 2, BLK)

        mats = bank_call(bank)
        recv = pltpu.with_memory_space_constraint(recv, pltpu.VMEM)
        fac = lax.dynamic_index_in_dim(jnp.asarray(factors), t, 0, keepdims=False)
        solved = solve_call(
            fac, o.reshape(1).astype(jnp.int32), recv, mats,
            nb, ncb, co, tiles, k_tiles.shape[1], g_tiles.shape[1], lay, low,
        )
        slots = lax.all_to_all(
            solved.reshape(tm, 2, BLK), group, split_axis=0, concat_axis=0, tiled=True
        ).reshape(steps, BLK)
        table = lax.dynamic_slice_in_dim(
            jnp.asarray(inverse), lax.axis_index("low") * (2 * high), 2 * high, axis=0
        )
        table = lax.optimization_barrier(table)
        kept = (
            blocks(state).reshape(2 * nb, BLK),
            blocks(multiplier).reshape(2 * ncb, BLK),
            stab.reshape(ncb, BLK),
        )
        kept = [pltpu.with_memory_space_constraint(v, pltpu.VMEM) for v in kept]
        rows, *kept = lax.optimization_barrier(
            (jnp.dot(table, slots, precision=HIGHEST), *kept)
        )
        rows = lax.all_to_all(
            rows.reshape(high, 2, BLK), "high", split_axis=0, concat_axis=0, tiled=True
        ).reshape(2 * nb, BLK)
        new_state, new_mult = finish_call(
            g_cols,
            g_tiles,
            *kept,
            pltpu.with_memory_space_constraint(rows, pltpu.VMEM),
            *[pltpu.with_memory_space_constraint(m, pltpu.VMEM) for m in mats[:2]],
        )

        def lines(value):
            return value.reshape(-1, 2, BLK).transpose(1, 0, 2).reshape(2, -1)

        return lines(new_state), lines(new_mult)

    return local


def solution(mesh):
    tm, co = mesh.shape["tm"], mesh.shape["coord"]
    low = 4
    split = Mesh(mesh.devices.reshape(tm // low, low, co), ("high", "low", "coord"))
    forward, inverse, factors = tables(2 * tm, low)
    time = ("high", "low")
    return jax.shard_map(
        make_local(forward, inverse, factors, low),
        mesh=split,
        in_specs=(
            P(time, "coord"),
            P(time, "coord"),
            P(time, "coord"),
            P("coord"),
            P("coord"),
            P("coord"),
            P("coord"),
            P(),
            P("coord", None),
            P("coord", None),
            P("coord", None),
            P("coord", None),
        ),
        out_specs=(P(time, "coord"), P(time, "coord")),
        check_vma=False,
    )
```

```python
import math

import jax
import jax.numpy as jnp
import numpy as np
from jax import lax
from jax.experimental import pallas as pl
from jax.experimental.pallas import tpu as pltpu
from jax.sharding import Mesh, PartitionSpec as P

BLK = 128
REACH = 2
SWEEPS = 8
FULL = 2
ALPHA = 0.001
HIGHEST = lax.Precision.HIGHEST
F32 = jnp.float32
BF16 = jnp.bfloat16


def tables(steps, low):
    ids = np.arange(steps)
    frequency = np.where(ids == 1, steps // 2, ids // 2)
    angles = 2.0 * np.pi / steps * ((frequency[:, None] * ids[None, :]) % steps)
    is_sine = (ids % 2 == 1) & (ids > 1)
    wave = np.where(is_sine[:, None], -np.sin(angles), np.cos(angles))
    scale = np.exp(math.log(ALPHA) * ids / steps)
    forward = wave * scale[None, :]
    weights = np.where(ids < 2, 1.0, 2.0) / steps
    inverse = (wave * weights[:, None]).T / scale[:, None]
    inverse = inverse.reshape(steps // (2 * low), low, 2, steps).swapaxes(0, 1).reshape(steps, steps)
    beta = math.exp(math.log(ALPHA) / steps)
    pair = np.arange(steps // 2)
    theta = 2.0 * np.pi * pair / steps
    zero = pair == 0
    a_even = np.where(zero, 1.0 - beta, 1.0 - beta * np.cos(theta))
    a_odd = np.where(zero, 1.0 + beta, 1.0 - beta * np.cos(theta))
    b_even = np.where(zero, 0.0, -beta * np.sin(theta))
    factors = np.stack([a_even, a_odd, b_even, zero.astype(np.float64)], axis=1)
    return forward.astype(np.float32), inverse.astype(np.float32), factors.astype(np.float32)


def split3(value):
    high = value.astype(BF16)
    rest = value - high.astype(F32)
    mid = rest.astype(BF16)
    return high, mid, (rest - mid.astype(F32)).astype(BF16)


def bank_kernel(bank_ref, w1, w2, v1, v2):
    for tile in range(bank_ref.shape[0]):
        value = bank_ref[tile]
        for mat, outs in ((value, (w1, w2)), (value.T, (v1, v2))):
            for out, piece in zip(outs, split3(mat)):
                out[tile] = piece


def gather_kernel(state, force, mult, out, sbuf, fbuf, mbuf, sin, sout):
    ns, nm = sbuf.shape[0], mbuf.shape[0]
    pairs = [(state, sbuf), (force, fbuf), (mult, mbuf)]
    loads = [pltpu.make_async_copy(a, b, sin.at[i]) for i, (a, b) in enumerate(pairs)]
    for load in loads:
        load.start()
    targets = [(sbuf, 0, ns), (fbuf, ns, ns), (mbuf, 2 * ns, nm), (sbuf, 2 * ns + nm, ns)]
    end = 3 * ns + nm
    while end < out.shape[0]:
        count = min(ns, out.shape[0] - end)
        targets.append((fbuf, end, count))
        end += count
    stores = []
    for load, (_, buf) in zip(loads, pairs):
        load.wait()
        for src, start, count in targets:
            if src is buf:
                stores.append(
                    pltpu.make_async_copy(
                        buf.at[pl.ds(0, count)], out.at[pl.ds(start, count)], sout.at[len(stores)]
                    )
                )
                stores[-1].start()
    for store in stores:
        store.wait()


def extra_kernel(at_ref, initial, mass, stiff, stab, offs, ktiles, cols, gtiles, out, buf):
    nb, ncb = mass.shape[0], stab.shape[0]
    buf[...] = jnp.zeros(buf.shape, F32)
    start = 0
    for first, second in (
        (initial[...], mass[...]),
        (stiff[: nb // 2], stiff[nb // 2 :]),
        (stab[: ncb // 2], stab[ncb // 2 :]),
        (offs[...].astype(F32), ktiles[...].astype(F32)),
        (cols[...].astype(F32), gtiles[...].astype(F32)),
    ):
        count, width = first.shape
        buf[pl.ds(start, count, stride=2), :width] = first
        buf[pl.ds(start + 1, count, stride=2), :width] = second
        start += 2 * count
    out[...] = buf[pl.ds(at_ref[0], 2), :]


def finish_kernel(cols_ref, tiles_ref, state, mult, stab, update, w1, w2, new_state, new_mult):
    ncb, gnb = cols_ref.shape
    new_state[...] = state[...] + update[...]
    owner = lax.broadcasted_iota(jnp.int32, mult.shape, 0) // 2
    total = jnp.zeros(mult.shape, F32)
    for j in range(gnb):
        value = jnp.concatenate(
            [new_state[pl.ds(cols_ref[c, j] * 2, 2), :] for c in range(ncb)], axis=0
        )
        high, mid, _ = split3(value)
        stack = jnp.concatenate([high, mid], axis=0)
        stack = jnp.concatenate([stack, stack], axis=1)
        for c in range(ncb):
            both = jnp.concatenate([w1[tiles_ref[c, j]], w2[tiles_ref[c, j]]])
            res = jnp.dot(stack, both, preferred_element_type=F32)
            total += jnp.where(owner == c, res[: 2 * ncb] + res[2 * ncb :], 0.0)
    weight = jnp.zeros(mult.shape, F32)
    for c in range(ncb):
        weight = jnp.where(owner == c, stab[c : c + 1], weight)
    new_mult[...] = mult[...] + (total - weight * mult[...]) / weight


def swapped(value):
    rows = value.shape[0]
    even = lax.broadcasted_iota(jnp.int32, value.shape, 0) % 2 == 0
    return jnp.where(even, pltpu.roll(value, rows - 1, 0), pltpu.roll(value, 1, 0))


def doubled(value, odd):
    rows = value.shape[0]
    even = lax.broadcasted_iota(jnp.int32, value.shape, 0) % 2 == 0
    if odd:
        return jnp.where(even, pltpu.roll(value, rows - 1, 0), value)
    return jnp.where(even, value, pltpu.roll(value, 1, 0))


def make_solve(nb, ncb, co, tiles, knb, gnb, lay):
    nrow = 2 * nb * co
    crow = 2 * ncb * co
    prow = tiles * nrow
    nidx = 2 * co * (knb + ncb)

    def kernel(
        fac_ref, own_ref, r_ref, w1_hbm, w2_hbm, v1_hbm, v2_hbm, out_ref,
        p_ref, q_ref, acc, gts, xs, rhs, e_ref, c_ref, xt, xl, gy, sc, istab, wide, idxv, idxs, sem,
        w1, w2, v1, v2, sems,
    ):
        a_even, a_odd, b_even, is_zero = fac_ref[0], fac_ref[1], fac_ref[2], fac_ref[3]

        def part(name, rows, start=0):
            start += lay[name] * 2 * co
            return r_ref[start : start + rows]

        loads = [
            pltpu.make_async_copy(src, dst, sems.at[i])
            for i, (src, dst) in enumerate(
                ((w1_hbm, w1), (w2_hbm, w2), (v1_hbm, v1), (v2_hbm, v2))
            )
        ]
        for load in loads:
            load.start()
        raw = part("idx", nidx).astype(jnp.int32)
        lane = lax.broadcasted_iota(jnp.int32, raw.shape, 1)
        line = lax.broadcasted_iota(jnp.int32, raw.shape, 0)
        coord = (line >> 1) & (co - 1)
        column, tile = raw, pltpu.roll(raw, nidx - 1, 0)
        block = coord * nb + lane + column - REACH
        inside = (block >= 0) & (block < nb * co)
        k_row = ((block & (nb - 1)) * co + (block >> (nb.bit_length() - 1))) * 2
        k_row = jnp.where(inside, tile * nrow + k_row, prow)
        g_row = (column * co + coord) * 2
        q_row = tile * crow + line - 2 * knb * co
        q_row = pltpu.roll(q_row, gnb, 1)
        g_rows = jnp.where(lane < gnb, tile * nrow + g_row, pltpu.roll(g_row, 2 * gnb, 1))
        g_rows = jnp.where((lane >= gnb) & (lane < 2 * gnb), q_row, g_rows)
        wide[...] = jnp.where(line < 2 * knb * co, k_row, g_rows)
        idxv[...] = jnp.zeros(idxv.shape, jnp.int32)
        idxv[: nidx // 2] = wide[pl.ds(0, nidx // 2, stride=2), :]
        copy = pltpu.make_async_copy(idxv, idxs, sem)
        copy.start()
        p_ref[prow : prow + 8] = jnp.zeros((8, BLK), F32)
        gts[...] = jnp.zeros(gts.shape, F32)

        def products(x1, x2, x3, mats, dst, beside):
            rows = x1.shape[0]
            pairs = [(x1, x1), (x2, x2)]
            if x3 is not None:
                pairs.append((x3, jnp.zeros_like(x3)))
            stack = jnp.concatenate([jnp.concatenate(p, axis=1) for p in pairs], axis=0)
            m1, m2 = mats
            for pair in range(tiles // 2):
                b1 = jnp.concatenate([m1[2 * pair], m1[2 * pair + 1]], axis=1)
                b2 = jnp.concatenate([m2[2 * pair], m2[2 * pair + 1]], axis=1)
                res = jnp.dot(stack, jnp.concatenate([b1, b2]), preferred_element_type=F32)
                low = res[rows : 2 * rows]
                if x3 is not None:
                    low = low + res[2 * rows :]
                res = res[:rows] + low
                for side in range(2):
                    start = (2 * pair + side) * rows
                    dst[start : start + rows] = res[:, side * BLK : side * BLK + BLK]
                beside(pair)

        def couple(i):
            count = nb // (tiles // 2)
            for b in range(i * count, (i + 1) * count):
                for o in range(co):
                    row = (b * co + o) * 2
                    total = p_ref[pl.ds(idxs[o, b], 2), :]
                    for k in range(1, knb):
                        total = total + p_ref[pl.ds(idxs[k * co + o, b], 2), :]
                    acc[row : row + 2] = total

        def constrain():
            for c in range(ncb):
                for o in range(co):
                    row = (c * co + o) * 2
                    at = (knb + c) * co + o
                    total = p_ref[pl.ds(idxs[at, 0], 2), :]
                    for j in range(1, gnb):
                        total = total + p_ref[pl.ds(idxs[at, j], 2), :]
                    gy[row : row + 2] = total

        def scatter():
            for c in range(ncb):
                for o in range(co):
                    at = (knb + c) * co + o
                    for j in range(gnb):
                        src, dst = idxs[at, gnb + j], idxs[at, 2 * gnb + j]
                        gts[c, pl.ds(dst, 2), :] = q_ref[pl.ds(src, 2), :]

        def coupled(rows):
            total = acc[rows]
            for c in range(ncb):
                total = total + gts[c, rows]
            return total

        chunk = nrow // (tiles // 2)
        even = lax.broadcasted_iota(jnp.int32, (chunk, BLK), 0) % 2 == 0

        def prepare(i):
            start = i * chunk
            rows = slice(start, start + chunk)
            state = part("state", chunk, start)
            cm = part("wrap", chunk, start)
            mass = doubled(cm, True)
            stiff = doubled(part("stiff", chunk, start % (nrow // 2)), start >= nrow // 2)
            wrap = jnp.where(even, cm, is_zero * pltpu.roll(cm, 1, 0))
            d_self = jnp.where(even, a_even, a_odd) * mass + stiff
            d_other = jnp.where(even, a_odd, a_even) * mass + stiff
            cross = jnp.where(even, b_even, -b_even) * mass
            inv = 1.0 / (d_self * d_other + cross * cross)
            e_ref[rows] = d_other * inv
            c_ref[rows] = cross * inv
            rhs[rows] = part("force", chunk, start) + wrap - (d_self * state + cross * swapped(state))

        def advance(first, full):
            for i in range(nrow // chunk):
                rows = slice(i * chunk, i * chunk + chunk)
                res = rhs[rows] - coupled(rows)
                if first:
                    rhs[rows] = res
                value = e_ref[rows] * res - c_ref[rows] * swapped(res)
                xt[rows, :BLK], xt[rows, BLK:], low = split3(value)
                if full:
                    xs[rows] = value
                    xl[rows] = low

        mult = part("mult", crow)
        shalf = part("stab", crow // 2)
        stab = jnp.concatenate([doubled(shalf, False), doubled(shalf, True)], axis=0)
        istab[...] = 1.0 / stab
        for i in range(nrow // chunk):
            prepare(i)
        for load in loads[:2]:
            load.wait()
        products(*split3(part("state", nrow)), (w1, w2), p_ref, lambda i: None)
        copy.wait()
        for load in loads[2:]:
            load.wait()
        products(*split3(mult), (v1, v2), q_ref, couple)
        constrain()
        scatter()
        sc[...] = stab * mult - gy[...]
        advance(True, False)

        def sweep(low, full):
            x3 = xl[...] if low else None
            products(xt[:, :BLK], xt[:, BLK:], x3, (w1, w2), p_ref, lambda i: None)
            constrain()
            products(*split3((gy[...] - sc[...]) * istab[...]), (v1, v2), q_ref, couple)
            scatter()
            advance(False, full)

        def loop(count, low, full):
            lax.fori_loop(0, count, lambda i, carry: (sweep(low, full), carry)[1], 0)

        loop(SWEEPS - 2 - FULL, False, False)
        sweep(False, True)
        loop(FULL, True, True)
        own = own_ref[0]
        parts = out_ref.shape[0] // (2 * nb)
        for b in range(nb):
            value = xs[pl.ds((b * co + own) * 2, 2), :]
            for z in range(parts):
                row = (b * parts + z) * 2
                out_ref[row : row + 2] = value

    return kernel, [
        pltpu.VMEM((prow + 8, BLK), F32),
        pltpu.VMEM((tiles * crow, BLK), F32),
        pltpu.VMEM((nrow, BLK), F32),
        pltpu.VMEM((ncb, nrow, BLK), F32),
        pltpu.VMEM((nrow, BLK), F32),
        pltpu.VMEM((nrow, BLK), F32),
        pltpu.VMEM((nrow, BLK), F32),
        pltpu.VMEM((nrow, BLK), F32),
        pltpu.VMEM((nrow, 2 * BLK), BF16),
        pltpu.VMEM((nrow, BLK), BF16),
        pltpu.VMEM((crow, BLK), F32),
        pltpu.VMEM((crow, BLK), F32),
        pltpu.VMEM((crow, BLK), F32),
        pltpu.VMEM((nidx, BLK), jnp.int32),
        pltpu.VMEM((-(-nidx // 16) * 8, BLK), jnp.int32),
        pltpu.SMEM((-(-nidx // 16) * 8, BLK), jnp.int32),
        pltpu.SemaphoreType.DMA(()),
        pltpu.VMEM((tiles, BLK, BLK), BF16),
        pltpu.VMEM((tiles, BLK, BLK), BF16),
        pltpu.VMEM((tiles, BLK, BLK), BF16),
        pltpu.VMEM((tiles, BLK, BLK), BF16),
        pltpu.SemaphoreType.DMA((4,)),
    ]


VM = pl.BlockSpec(memory_space=pltpu.VMEM)
SM = pl.BlockSpec(memory_space=pltpu.SMEM)


def layout(nb, ncb):
    state, force, mult = 0, nb, 2 * nb
    wrap = mult + ncb
    stiff = wrap + nb
    stab = stiff + nb // 2
    idx = stab + ncb // 2
    return {"state": state, "force": force, "mult": mult, "wrap": wrap, "stiff": stiff, "stab": stab, "idx": idx}


def solve_call(fac, own, recv, mats, nb, ncb, co, tiles, knb, gnb, lay, parts):
    kernel, scratch = make_solve(nb, ncb, co, tiles, knb, gnb, lay)
    return pl.pallas_call(
        kernel,
        out_shape=jax.ShapeDtypeStruct((2 * nb * parts, BLK), F32),
        in_specs=[SM, SM, VM] + [pl.BlockSpec(memory_space=pl.ANY)] * 4,
        out_specs=VM,
        scratch_shapes=scratch,
        name="solve",
    )(fac, own, recv, *mats)


def bank_call(bank):
    shape = jax.ShapeDtypeStruct(bank.shape, BF16)
    return pl.pallas_call(
        bank_kernel, out_shape=[shape] * 4, in_specs=[VM], out_specs=[VM] * 4, name="bank"
    )(bank)


def gather_call(state, force, mult, count):
    hbm = pl.BlockSpec(memory_space=pl.ANY)
    return pl.pallas_call(
        gather_kernel,
        out_shape=jax.ShapeDtypeStruct((count, 2, BLK), F32),
        in_specs=[hbm] * 3,
        out_specs=hbm,
        scratch_shapes=[pltpu.VMEM(v.shape, F32) for v in (state, force, mult)]
        + [pltpu.SemaphoreType.DMA((3,)), pltpu.SemaphoreType.DMA((8,))],
        name="gather",
    )(state, force, mult)


def extra_call(at, initial, mass, stiff, stab, offs, ktiles, cols, gtiles, rows):
    return pl.pallas_call(
        extra_kernel,
        out_shape=jax.ShapeDtypeStruct((2, BLK), F32),
        in_specs=[SM] + [VM] * 8,
        out_specs=VM,
        scratch_shapes=[pltpu.VMEM((rows, BLK), F32)],
        name="extra",
    )(at, initial, mass, stiff, stab, offs, ktiles, cols, gtiles)


def finish_call(cols, tiles, state, mult, stab, update, w1, w2):
    return pl.pallas_call(
        finish_kernel,
        out_shape=[
            jax.ShapeDtypeStruct(state.shape, F32),
            jax.ShapeDtypeStruct(mult.shape, F32),
        ],
        in_specs=[SM, SM] + [VM] * 6,
        out_specs=[VM, VM],
        name="finish",
    )(cols, tiles, state, mult, stab, update, w1, w2)


def make_local(forward, inverse, factors, low):
    steps = forward.shape[0]
    group = ("high", "low")

    def blocks(value):
        return value.reshape(value.shape[0], -1, BLK).transpose(1, 0, 2)

    def local(
        state, multiplier, force, initial, mass, stiff_diag, stab,
        bank, k_offsets, k_tiles, g_cols, g_tiles,
    ):
        nb = state.shape[1] // BLK
        ncb = multiplier.shape[1] // BLK
        tiles = bank.shape[0]
        tm = lax.axis_size(group)
        co = lax.axis_size("coord")
        high = tm // low
        t = lax.axis_index(group)
        o = lax.axis_index("coord")
        lay = layout(nb, ncb)
        sent = gather_call(blocks(state), blocks(force), blocks(multiplier), tm)
        columns = lax.all_to_all(sent, group, split_axis=0, concat_axis=0, tiled=True)
        columns = columns.reshape(steps, BLK)
        at = t - lay["wrap"]
        count = 2 * (tm - lay["wrap"])
        extra = extra_call(
            jnp.clip(2 * at, 0, count - 2).reshape(1),
            initial.reshape(nb, BLK),
            mass.reshape(nb, BLK),
            stiff_diag.reshape(nb, BLK),
            stab.reshape(ncb, BLK),
            k_offsets.T,
            k_tiles.T,
            g_cols,
            g_tiles,
            -(-count // 8) * 8,
        )
        is_wrap = (at >= 0) & (at < nb)
        wrap = jnp.where(is_wrap, extra[1] * (extra[0] - ALPHA * columns[-1]), extra[0])
        extra = jnp.stack([wrap, extra[1]])
        spectrum = jnp.dot(forward, columns, precision=HIGHEST).reshape(tm, 2, BLK)
        spectrum = jnp.where(at < 0, spectrum, extra[None])
        spread = jnp.broadcast_to(spectrum[:, None], (tm, co, 2, BLK)).reshape(tm * co, 2, BLK)
        recv = lax.all_to_all(
            spread, group + ("coord",), split_axis=0, concat_axis=0, tiled=True
        ).reshape(tm * co * 2, BLK)

        mats = bank_call(bank)
        recv = pltpu.with_memory_space_constraint(recv, pltpu.VMEM)
        fac = lax.dynamic_index_in_dim(jnp.asarray(factors), t, 0, keepdims=False)
        solved = solve_call(
            fac, o.reshape(1).astype(jnp.int32), recv, mats,
            nb, ncb, co, tiles, k_tiles.shape[1], g_tiles.shape[1], lay, low,
        )
        slots = lax.all_to_all(
            solved.reshape(tm, 2, BLK), group, split_axis=0, concat_axis=0, tiled=True
        ).reshape(steps, BLK)
        table = lax.dynamic_slice_in_dim(
            jnp.asarray(inverse), lax.axis_index("low") * (2 * high), 2 * high, axis=0
        )
        table = lax.optimization_barrier(table)
        kept = (
            blocks(state).reshape(2 * nb, BLK),
            blocks(multiplier).reshape(2 * ncb, BLK),
            stab.reshape(ncb, BLK),
        )
        kept = [pltpu.with_memory_space_constraint(v, pltpu.VMEM) for v in kept]
        rows, *kept = lax.optimization_barrier(
            (jnp.dot(table, slots, precision=HIGHEST), *kept)
        )
        rows = lax.all_to_all(
            rows.reshape(high, 2, BLK), "high", split_axis=0, concat_axis=0, tiled=True
        ).reshape(2 * nb, BLK)
        new_state, new_mult = finish_call(
            g_cols,
            g_tiles,
            *kept,
            pltpu.with_memory_space_constraint(rows, pltpu.VMEM),
            *[pltpu.with_memory_space_constraint(m, pltpu.VMEM) for m in mats[:2]],
        )

        def lines(value):
            return value.reshape(-1, 2, BLK).transpose(1, 0, 2).reshape(2, -1)

        return lines(new_state), lines(new_mult)

    return local


def solution(mesh):
    tm, co = mesh.shape["tm"], mesh.shape["coord"]
    low = 4
    split = Mesh(mesh.devices.reshape(tm // low, low, co), ("high", "low", "coord"))
    forward, inverse, factors = tables(2 * tm, low)
    time = ("high", "low")
    return jax.shard_map(
        make_local(forward, inverse, factors, low),
        mesh=split,
        in_specs=(
            P(time, "coord"),
            P(time, "coord"),
            P(time, "coord"),
            P("coord"),
            P("coord"),
            P("coord"),
            P("coord"),
            P(),
            P("coord", None),
            P("coord", None),
            P("coord", None),
            P("coord", None),
        ),
        out_specs=(P(time, "coord"), P(time, "coord")),
        check_vma=False,
    )
```

```python
import math

import jax
import jax.numpy as jnp
import numpy as np
from jax import lax
from jax.experimental import pallas as pl
from jax.experimental.pallas import tpu as pltpu
from jax.sharding import Mesh, PartitionSpec as P

BLK = 128
REACH = 2
SWEEPS = 8
FULL = 2
ALPHA = 0.001
HIGHEST = lax.Precision.HIGHEST
F32 = jnp.float32
BF16 = jnp.bfloat16


def tables(steps, low):
    ids = np.arange(steps)
    frequency = np.where(ids == 1, steps // 2, ids // 2)
    angles = 2.0 * np.pi / steps * ((frequency[:, None] * ids[None, :]) % steps)
    is_sine = (ids % 2 == 1) & (ids > 1)
    wave = np.where(is_sine[:, None], -np.sin(angles), np.cos(angles))
    scale = np.exp(math.log(ALPHA) * ids / steps)
    forward = wave * scale[None, :]
    weights = np.where(ids < 2, 1.0, 2.0) / steps
    inverse = (wave * weights[:, None]).T / scale[:, None]
    inverse = inverse.reshape(steps // (2 * low), low, 2, steps).swapaxes(0, 1).reshape(steps, steps)
    beta = math.exp(math.log(ALPHA) / steps)
    pair = np.arange(steps // 2)
    theta = 2.0 * np.pi * pair / steps
    zero = pair == 0
    a_even = np.where(zero, 1.0 - beta, 1.0 - beta * np.cos(theta))
    a_odd = np.where(zero, 1.0 + beta, 1.0 - beta * np.cos(theta))
    b_even = np.where(zero, 0.0, -beta * np.sin(theta))
    factors = np.stack([a_even, a_odd, b_even, zero.astype(np.float64)], axis=1)
    return forward.astype(np.float32), inverse.astype(np.float32), factors.astype(np.float32)


def split3(value):
    high = value.astype(BF16)
    rest = value - high.astype(F32)
    mid = rest.astype(BF16)
    return high, mid, (rest - mid.astype(F32)).astype(BF16)


def bank_kernel(bank_ref, w1, w2, v1, v2):
    for tile in range(bank_ref.shape[0]):
        value = bank_ref[tile]
        for mat, outs in ((value, (w1, w2)), (value.T, (v1, v2))):
            for out, piece in zip(outs, split3(mat)):
                out[tile] = piece


def gather_kernel(state, force, mult, out, sbuf, fbuf, mbuf, sin, sout):
    ns, nm = sbuf.shape[0], mbuf.shape[0]
    pairs = [(state, sbuf), (force, fbuf), (mult, mbuf)]
    loads = [pltpu.make_async_copy(a, b, sin.at[i]) for i, (a, b) in enumerate(pairs)]
    for load in loads:
        load.start()
    targets = [(sbuf, 0, ns), (fbuf, ns, ns), (mbuf, 2 * ns, nm), (sbuf, 2 * ns + nm, ns)]
    end = 3 * ns + nm
    while end < out.shape[0]:
        count = min(ns, out.shape[0] - end)
        targets.append((fbuf, end, count))
        end += count
    stores = []
    for load, (_, buf) in zip(loads, pairs):
        load.wait()
        for src, start, count in targets:
            if src is buf:
                stores.append(
                    pltpu.make_async_copy(
                        buf.at[pl.ds(0, count)], out.at[pl.ds(start, count)], sout.at[len(stores)]
                    )
                )
                stores[-1].start()
    for store in stores:
        store.wait()


def extra_kernel(at_ref, initial, mass, stiff, stab, offs, ktiles, cols, gtiles, out, buf):
    nb, ncb = mass.shape[0], stab.shape[0]
    buf[...] = jnp.zeros(buf.shape, F32)
    start = 0
    for first, second in (
        (initial[...], mass[...]),
        (stiff[: nb // 2], stiff[nb // 2 :]),
        (stab[: ncb // 2], stab[ncb // 2 :]),
        (offs[...].astype(F32), ktiles[...].astype(F32)),
        (cols[...].astype(F32), gtiles[...].astype(F32)),
    ):
        count, width = first.shape
        buf[pl.ds(start, count, stride=2), :width] = first
        buf[pl.ds(start + 1, count, stride=2), :width] = second
        start += 2 * count
    out[...] = buf[pl.ds(at_ref[0], 2), :]


def finish_kernel(cols_ref, tiles_ref, state, mult, stab, update, w1, w2, new_state, new_mult):
    ncb, gnb = cols_ref.shape
    new_state[...] = state[...] + update[...]
    owner = lax.broadcasted_iota(jnp.int32, mult.shape, 0) // 2
    total = jnp.zeros(mult.shape, F32)
    for j in range(gnb):
        value = jnp.concatenate(
            [new_state[pl.ds(cols_ref[c, j] * 2, 2), :] for c in range(ncb)], axis=0
        )
        high, mid, _ = split3(value)
        stack = jnp.concatenate([high, mid], axis=0)
        stack = jnp.concatenate([stack, stack], axis=1)
        for c in range(ncb):
            both = jnp.concatenate([w1[tiles_ref[c, j]], w2[tiles_ref[c, j]]])
            res = jnp.dot(stack, both, preferred_element_type=F32)
            total += jnp.where(owner == c, res[: 2 * ncb] + res[2 * ncb :], 0.0)
    weight = jnp.zeros(mult.shape, F32)
    for c in range(ncb):
        weight = jnp.where(owner == c, stab[c : c + 1], weight)
    new_mult[...] = mult[...] + (total - weight * mult[...]) / weight


def swapped(value):
    rows = value.shape[0]
    even = lax.broadcasted_iota(jnp.int32, value.shape, 0) % 2 == 0
    return jnp.where(even, pltpu.roll(value, rows - 1, 0), pltpu.roll(value, 1, 0))


def doubled(value, odd):
    rows = value.shape[0]
    even = lax.broadcasted_iota(jnp.int32, value.shape, 0) % 2 == 0
    if odd:
        return jnp.where(even, pltpu.roll(value, rows - 1, 0), value)
    return jnp.where(even, value, pltpu.roll(value, 1, 0))


def make_solve(nb, ncb, co, tiles, knb, gnb, lay):
    nrow = 2 * nb * co
    crow = 2 * ncb * co
    prow = tiles * nrow
    nidx = 2 * co * (knb + ncb)

    def kernel(
        fac_ref, own_ref, r_ref, w1_hbm, w2_hbm, v1_hbm, v2_hbm, out_ref,
        p_ref, q_ref, acc, gts, xs, rhs, e_ref, c_ref, xt, xl, gy, sc, istab, wide, idxv, idxs, sem,
        w1, w2, v1, v2, sems,
    ):
        a_even, a_odd, b_even, is_zero = fac_ref[0], fac_ref[1], fac_ref[2], fac_ref[3]

        def part(name, rows, start=0):
            start += lay[name] * 2 * co
            return r_ref[start : start + rows]

        loads = [
            pltpu.make_async_copy(src, dst, sems.at[i])
            for i, (src, dst) in enumerate(
                ((w1_hbm, w1), (w2_hbm, w2), (v1_hbm, v1), (v2_hbm, v2))
            )
        ]
        for load in loads:
            load.start()
        raw = part("idx", nidx).astype(jnp.int32)
        lane = lax.broadcasted_iota(jnp.int32, raw.shape, 1)
        line = lax.broadcasted_iota(jnp.int32, raw.shape, 0)
        coord = (line >> 1) & (co - 1)
        column, tile = raw, pltpu.roll(raw, nidx - 1, 0)
        block = coord * nb + lane + column - REACH
        inside = (block >= 0) & (block < nb * co)
        k_row = ((block & (nb - 1)) * co + (block >> (nb.bit_length() - 1))) * 2
        k_row = jnp.where(inside, tile * nrow + k_row, prow)
        g_row = (column * co + coord) * 2
        q_row = tile * crow + line - 2 * knb * co
        q_row = pltpu.roll(q_row, gnb, 1)
        g_rows = jnp.where(lane < gnb, tile * nrow + g_row, pltpu.roll(g_row, 2 * gnb, 1))
        g_rows = jnp.where((lane >= gnb) & (lane < 2 * gnb), q_row, g_rows)
        wide[...] = jnp.where(line < 2 * knb * co, k_row, g_rows)
        idxv[...] = jnp.zeros(idxv.shape, jnp.int32)
        idxv[: nidx // 2] = wide[pl.ds(0, nidx // 2, stride=2), :]
        copy = pltpu.make_async_copy(idxv, idxs, sem)
        copy.start()
        p_ref[prow : prow + 8] = jnp.zeros((8, BLK), F32)
        gts[...] = jnp.zeros(gts.shape, F32)

        def products(x1, x2, x3, mats, dst, beside):
            rows = x1.shape[0]
            pairs = [(x1, x1), (x2, x2)]
            if x3 is not None:
                pairs.append((x3, jnp.zeros_like(x3)))
            stack = jnp.concatenate([jnp.concatenate(p, axis=1) for p in pairs], axis=0)
            m1, m2 = mats
            for pair in range(tiles // 2):
                b1 = jnp.concatenate([m1[2 * pair], m1[2 * pair + 1]], axis=1)
                b2 = jnp.concatenate([m2[2 * pair], m2[2 * pair + 1]], axis=1)
                res = jnp.dot(stack, jnp.concatenate([b1, b2]), preferred_element_type=F32)
                low = res[rows : 2 * rows]
                if x3 is not None:
                    low = low + res[2 * rows :]
                res = res[:rows] + low
                for side in range(2):
                    start = (2 * pair + side) * rows
                    dst[start : start + rows] = res[:, side * BLK : side * BLK + BLK]
                beside(pair)

        def couple(i):
            count = nb // (tiles // 2)
            for b in range(i * count, (i + 1) * count):
                for o in range(co):
                    row = (b * co + o) * 2
                    total = p_ref[pl.ds(idxs[o, b], 2), :]
                    for k in range(1, knb):
                        total = total + p_ref[pl.ds(idxs[k * co + o, b], 2), :]
                    acc[row : row + 2] = total

        def constrain():
            for c in range(ncb):
                for o in range(co):
                    row = (c * co + o) * 2
                    at = (knb + c) * co + o
                    total = p_ref[pl.ds(idxs[at, 0], 2), :]
                    for j in range(1, gnb):
                        total = total + p_ref[pl.ds(idxs[at, j], 2), :]
                    gy[row : row + 2] = total

        def scatter():
            for c in range(ncb):
                for o in range(co):
                    at = (knb + c) * co + o
                    for j in range(gnb):
                        src, dst = idxs[at, gnb + j], idxs[at, 2 * gnb + j]
                        gts[c, pl.ds(dst, 2), :] = q_ref[pl.ds(src, 2), :]

        def coupled(rows):
            total = acc[rows]
            for c in range(ncb):
                total = total + gts[c, rows]
            return total

        chunk = nrow // (tiles // 2)
        even = lax.broadcasted_iota(jnp.int32, (chunk, BLK), 0) % 2 == 0

        def prepare(i):
            start = i * chunk
            rows = slice(start, start + chunk)
            state = part("state", chunk, start)
            cm = part("wrap", chunk, start)
            mass = doubled(cm, True)
            stiff = doubled(part("stiff", chunk, start % (nrow // 2)), start >= nrow // 2)
            wrap = jnp.where(even, cm, is_zero * pltpu.roll(cm, 1, 0))
            d_self = jnp.where(even, a_even, a_odd) * mass + stiff
            d_other = jnp.where(even, a_odd, a_even) * mass + stiff
            cross = jnp.where(even, b_even, -b_even) * mass
            inv = 1.0 / (d_self * d_other + cross * cross)
            e_ref[rows] = d_other * inv
            c_ref[rows] = cross * inv
            rhs[rows] = part("force", chunk, start) + wrap - (d_self * state + cross * swapped(state))

        def advance(first, full):
            for i in range(nrow // chunk):
                rows = slice(i * chunk, i * chunk + chunk)
                res = rhs[rows] - coupled(rows)
                if first:
                    rhs[rows] = res
                value = e_ref[rows] * res - c_ref[rows] * swapped(res)
                xt[rows, :BLK], xt[rows, BLK:], low = split3(value)
                if full:
                    xs[rows] = value
                    xl[rows] = low

        mult = part("mult", crow)
        shalf = part("stab", crow // 2)
        stab = jnp.concatenate([doubled(shalf, False), doubled(shalf, True)], axis=0)
        istab[...] = 1.0 / stab
        for i in range(nrow // chunk):
            prepare(i)
        for load in loads[:2]:
            load.wait()
        products(*split3(part("state", nrow)), (w1, w2), p_ref, lambda i: None)
        copy.wait()
        for load in loads[2:]:
            load.wait()
        products(*split3(mult), (v1, v2), q_ref, couple)
        constrain()
        scatter()
        sc[...] = stab * mult - gy[...]
        advance(True, False)

        def sweep(low, full):
            x3 = xl[...] if low else None
            products(xt[:, :BLK], xt[:, BLK:], x3, (w1, w2), p_ref, lambda i: None)
            constrain()
            products(*split3((gy[...] - sc[...]) * istab[...]), (v1, v2), q_ref, couple)
            scatter()
            advance(False, full)

        def loop(count, low, full):
            for _ in range(count):
                sweep(low, full)

        loop(SWEEPS - 2 - FULL, False, False)
        sweep(False, True)
        loop(FULL, True, True)
        own = own_ref[0]
        parts = out_ref.shape[0] // (2 * nb)
        for b in range(nb):
            value = xs[pl.ds((b * co + own) * 2, 2), :]
            for z in range(parts):
                row = (b * parts + z) * 2
                out_ref[row : row + 2] = value

    return kernel, [
        pltpu.VMEM((prow + 8, BLK), F32),
        pltpu.VMEM((tiles * crow, BLK), F32),
        pltpu.VMEM((nrow, BLK), F32),
        pltpu.VMEM((ncb, nrow, BLK), F32),
        pltpu.VMEM((nrow, BLK), F32),
        pltpu.VMEM((nrow, BLK), F32),
        pltpu.VMEM((nrow, BLK), F32),
        pltpu.VMEM((nrow, BLK), F32),
        pltpu.VMEM((nrow, 2 * BLK), BF16),
        pltpu.VMEM((nrow, BLK), BF16),
        pltpu.VMEM((crow, BLK), F32),
        pltpu.VMEM((crow, BLK), F32),
        pltpu.VMEM((crow, BLK), F32),
        pltpu.VMEM((nidx, BLK), jnp.int32),
        pltpu.VMEM((-(-nidx // 16) * 8, BLK), jnp.int32),
        pltpu.SMEM((-(-nidx // 16) * 8, BLK), jnp.int32),
        pltpu.SemaphoreType.DMA(()),
        pltpu.VMEM((tiles, BLK, BLK), BF16),
        pltpu.VMEM((tiles, BLK, BLK), BF16),
        pltpu.VMEM((tiles, BLK, BLK), BF16),
        pltpu.VMEM((tiles, BLK, BLK), BF16),
        pltpu.SemaphoreType.DMA((4,)),
    ]


VM = pl.BlockSpec(memory_space=pltpu.VMEM)
SM = pl.BlockSpec(memory_space=pltpu.SMEM)


def layout(nb, ncb):
    state, force, mult = 0, nb, 2 * nb
    wrap = mult + ncb
    stiff = wrap + nb
    stab = stiff + nb // 2
    idx = stab + ncb // 2
    return {"state": state, "force": force, "mult": mult, "wrap": wrap, "stiff": stiff, "stab": stab, "idx": idx}


def solve_call(fac, own, recv, mats, nb, ncb, co, tiles, knb, gnb, lay, parts):
    kernel, scratch = make_solve(nb, ncb, co, tiles, knb, gnb, lay)
    return pl.pallas_call(
        kernel,
        out_shape=jax.ShapeDtypeStruct((2 * nb * parts, BLK), F32),
        in_specs=[SM, SM, VM] + [pl.BlockSpec(memory_space=pl.ANY)] * 4,
        out_specs=VM,
        scratch_shapes=scratch,
        name="solve",
    )(fac, own, recv, *mats)


def bank_call(bank):
    shape = jax.ShapeDtypeStruct(bank.shape, BF16)
    return pl.pallas_call(
        bank_kernel, out_shape=[shape] * 4, in_specs=[VM], out_specs=[VM] * 4, name="bank"
    )(bank)


def gather_call(state, force, mult, count):
    hbm = pl.BlockSpec(memory_space=pl.ANY)
    return pl.pallas_call(
        gather_kernel,
        out_shape=jax.ShapeDtypeStruct((count, 2, BLK), F32),
        in_specs=[hbm] * 3,
        out_specs=hbm,
        scratch_shapes=[pltpu.VMEM(v.shape, F32) for v in (state, force, mult)]
        + [pltpu.SemaphoreType.DMA((3,)), pltpu.SemaphoreType.DMA((8,))],
        name="gather",
    )(state, force, mult)


def extra_call(at, initial, mass, stiff, stab, offs, ktiles, cols, gtiles, rows):
    return pl.pallas_call(
        extra_kernel,
        out_shape=jax.ShapeDtypeStruct((2, BLK), F32),
        in_specs=[SM] + [VM] * 8,
        out_specs=VM,
        scratch_shapes=[pltpu.VMEM((rows, BLK), F32)],
        name="extra",
    )(at, initial, mass, stiff, stab, offs, ktiles, cols, gtiles)


def finish_call(cols, tiles, state, mult, stab, update, w1, w2):
    return pl.pallas_call(
        finish_kernel,
        out_shape=[
            jax.ShapeDtypeStruct(state.shape, F32),
            jax.ShapeDtypeStruct(mult.shape, F32),
        ],
        in_specs=[SM, SM] + [VM] * 6,
        out_specs=[VM, VM],
        name="finish",
    )(cols, tiles, state, mult, stab, update, w1, w2)


def make_local(forward, inverse, factors, low):
    steps = forward.shape[0]
    group = ("high", "low")

    def blocks(value):
        return value.reshape(value.shape[0], -1, BLK).transpose(1, 0, 2)

    def local(
        state, multiplier, force, initial, mass, stiff_diag, stab,
        bank, k_offsets, k_tiles, g_cols, g_tiles,
    ):
        nb = state.shape[1] // BLK
        ncb = multiplier.shape[1] // BLK
        tiles = bank.shape[0]
        tm = lax.axis_size(group)
        co = lax.axis_size("coord")
        high = tm // low
        t = lax.axis_index(group)
        o = lax.axis_index("coord")
        lay = layout(nb, ncb)
        sent = gather_call(blocks(state), blocks(force), blocks(multiplier), tm)
        columns = lax.all_to_all(sent, group, split_axis=0, concat_axis=0, tiled=True)
        columns = columns.reshape(steps, BLK)
        at = t - lay["wrap"]
        count = 2 * (tm - lay["wrap"])
        extra = extra_call(
            jnp.clip(2 * at, 0, count - 2).reshape(1),
            initial.reshape(nb, BLK),
            mass.reshape(nb, BLK),
            stiff_diag.reshape(nb, BLK),
            stab.reshape(ncb, BLK),
            k_offsets.T,
            k_tiles.T,
            g_cols,
            g_tiles,
            -(-count // 8) * 8,
        )
        is_wrap = (at >= 0) & (at < nb)
        wrap = jnp.where(is_wrap, extra[1] * (extra[0] - ALPHA * columns[-1]), extra[0])
        extra = jnp.stack([wrap, extra[1]])
        spectrum = jnp.dot(forward, columns, precision=HIGHEST).reshape(tm, 2, BLK)
        spectrum = jnp.where(at < 0, spectrum, extra[None])
        spread = jnp.broadcast_to(spectrum[:, None], (tm, co, 2, BLK)).reshape(tm * co, 2, BLK)
        recv = lax.all_to_all(
            spread, group + ("coord",), split_axis=0, concat_axis=0, tiled=True
        ).reshape(tm * co * 2, BLK)

        mats = bank_call(bank)
        recv = pltpu.with_memory_space_constraint(recv, pltpu.VMEM)
        fac = lax.dynamic_index_in_dim(jnp.asarray(factors), t, 0, keepdims=False)
        solved = solve_call(
            fac, o.reshape(1).astype(jnp.int32), recv, mats,
            nb, ncb, co, tiles, k_tiles.shape[1], g_tiles.shape[1], lay, low,
        )
        slots = lax.all_to_all(
            solved.reshape(tm, 2, BLK), group, split_axis=0, concat_axis=0, tiled=True
        ).reshape(steps, BLK)
        table = lax.dynamic_slice_in_dim(
            jnp.asarray(inverse), lax.axis_index("low") * (2 * high), 2 * high, axis=0
        )
        table = lax.optimization_barrier(table)
        kept = (
            blocks(state).reshape(2 * nb, BLK),
            blocks(multiplier).reshape(2 * ncb, BLK),
            stab.reshape(ncb, BLK),
        )
        kept = [pltpu.with_memory_space_constraint(v, pltpu.VMEM) for v in kept]
        rows, *kept = lax.optimization_barrier(
            (jnp.dot(table, slots, precision=HIGHEST), *kept)
        )
        rows = lax.all_to_all(
            rows.reshape(high, 2, BLK), "high", split_axis=0, concat_axis=0, tiled=True
        ).reshape(2 * nb, BLK)
        new_state, new_mult = finish_call(
            g_cols,
            g_tiles,
            *kept,
            pltpu.with_memory_space_constraint(rows, pltpu.VMEM),
            *[pltpu.with_memory_space_constraint(m, pltpu.VMEM) for m in mats[:2]],
        )

        def lines(value):
            return value.reshape(-1, 2, BLK).transpose(1, 0, 2).reshape(2, -1)

        return lines(new_state), lines(new_mult)

    return local


def solution(mesh):
    tm, co = mesh.shape["tm"], mesh.shape["coord"]
    low = 4
    split = Mesh(mesh.devices.reshape(tm // low, low, co), ("high", "low", "coord"))
    forward, inverse, factors = tables(2 * tm, low)
    time = ("high", "low")
    return jax.shard_map(
        make_local(forward, inverse, factors, low),
        mesh=split,
        in_specs=(
            P(time, "coord"),
            P(time, "coord"),
            P(time, "coord"),
            P("coord"),
            P("coord"),
            P("coord"),
            P("coord"),
            P(),
            P("coord", None),
            P("coord", None),
            P("coord", None),
            P("coord", None),
        ),
        out_specs=(P(time, "coord"), P(time, "coord")),
        check_vma=False,
    )
```
